32 devices in a mesh: dp: 8 (over z, core), expert: 4 (over y, x).
Axes of the slice: x: 2, y: 2, z: 4, core: 2. Of those that a mesh axis runs over, the one named last changes fastest.
Arguments:
- tokens: bfloat16 [24576, 2048], P(('dp', 'expert')), may hold values from -6 to 6
- target: bfloat16 [24576, 2048], P(('dp', 'expert')), may hold values from -4 to 4
- route_index: int32 [8, 4, 4, 16], P('dp', None, 'expert'), may hold values from 0 to 767, as said below
- route_count: int32 [8, 4, 4], P('dp', None, 'expert'), may hold values from 1 to 16, as said below
- route_gate: float32 [8, 4, 4, 16], P('dp', None, 'expert'), may hold values from 0.1 to 1
- gate_weight: bfloat16 [2048, 4, 768], P('dp', 'expert'), may hold values from -0.125 to 0.125
- up_weight: bfloat16 [2048, 4, 768], P('dp', 'expert'), may hold values from -0.125 to 0.125
- down_weight: bfloat16 [2048, 4, 768], P('dp', 'expert'), may hold values from -0.21875 to 0.21875
Outputs:
- token_grad: bfloat16 [24576, 2048], P(('dp', 'expert'))
- gate_gradient: float32 [2048, 4, 768], P('dp', 'expert')
- up_gradient: float32 [2048, 4, 768], P('dp', 'expert')
- down_gradient: float32 [2048, 4, 768], P('dp', 'expert')
The draws below stay inside these ranges and needn't reach their ends.
Inputs may be any that keep to these rules, and one draw needn't show every extreme that they name: `route_index`: within each list of 16 slots the indices are distinct; each names a token of the source device. `route_count`: in every group one expert has all 16 slots live from every source device; slots at or beyond the count are unused.
All inputs are finite; a program needn't handle non-finite values.
Results may differ from the reference program's by a relative error of at most 0.0059.
Values may be sent and summed in bfloat16 or wider, within the bound.
A program may use at most 128 MiB of HBM per device.

```python
import jax
import jax.numpy as jnp

D = 2048
FF = 768
TOK_DEV = 768
SLOTS = 16
GROUPS = 8
SOURCES = 4
EXPERTS = 4
TOKENS = 24576


def draw_route_count(key, part):
    keys_all = jax.random.split(jax.random.fold_in(key, 11), 3)
    shift_by = jax.random.randint(keys_all[0], (GROUPS, EXPERTS, 1), 0, 4).astype(jnp.int32)
    level_top = jnp.maximum(jnp.right_shift(jnp.full((GROUPS, EXPERTS, 1), SLOTS, jnp.int32), shift_by), 1)
    level_low = jnp.maximum(level_top // 2, 1)
    counts_drawn = jax.random.randint(keys_all[1], (GROUPS, EXPERTS, SOURCES), level_low, level_top + 1)
    full_expert = jax.random.randint(keys_all[2], (GROUPS, 1, 1), 0, EXPERTS)
    filled = jnp.where(jnp.arange(EXPERTS, dtype=jnp.int32)[None, :, None] == full_expert, SLOTS, counts_drawn)
    return filled.astype(jnp.int32)


def draw_route_index(key, part):
    keys_all = jax.random.split(jax.random.fold_in(key, 23), GROUPS * EXPERTS * SOURCES)
    chosen = jax.vmap(lambda subkey: jax.random.permutation(subkey, TOK_DEV)[:SLOTS])(keys_all)
    return chosen.reshape(GROUPS, EXPERTS, SOURCES, SLOTS).astype(jnp.int32)


def block_scale(own_key, dims, pieces, smallest, top_value):
    level = 1.0
    for position, parts in pieces:
        heights = jax.random.uniform(jax.random.fold_in(jax.random.fold_in(own_key, 6), position), (parts,), jnp.float32, smallest / len(pieces), top_value / len(pieces))
        level = level * jnp.repeat(jnp.exp(heights), dims[position] // parts).reshape((-1,) + (1,) * (len(dims) - 1 - position))
    return level


def scatter_about(own_key, shape, deviation, most, shards=(), held_as=jnp.bfloat16):
    gain = block_scale(own_key, shape, shards, -0.22, 0.18) if shards else 1.0
    array = jax.random.normal(own_key, shape, jnp.float32) * deviation * gain
    return jnp.minimum(jnp.maximum(array, -most), most).astype(held_as)


def setup_inputs(seed: int = 0) -> dict:
    splits = jax.random.split(jax.random.key(seed), 9)
    tokens = scatter_about(splits[0], (TOKENS, D), 1.0, 6.0, ((0, 32),))
    target = scatter_about(splits[1], (TOKENS, D), 0.5, 4.0, ((0, 32),))
    route_index = draw_route_index(jax.random.fold_in(splits[8], 71), 0)
    route_count = draw_route_count(jax.random.fold_in(splits[8], 71), 0)
    route_gate = jnp.clip(0.1 + 0.9 * jax.random.uniform(splits[4], (GROUPS, EXPERTS, SOURCES, SLOTS), jnp.float32) ** block_scale(splits[4], (GROUPS, EXPERTS, SOURCES, SLOTS), ((0, 8), (2, 4)), -0.2, 0.2), 0.1, 1.0)
    gate_weight = scatter_about(splits[5], (D, EXPERTS, FF), D ** -0.5, 0.125, ((0, 8), (1, 4)))
    up_weight = scatter_about(splits[6], (D, EXPERTS, FF), D ** -0.5, 0.125, ((0, 8), (1, 4)))
    down_weight = scatter_about(splits[7], (D, EXPERTS, FF), FF ** -0.5, 0.21875, ((0, 8), (1, 4)))
    return {"tokens": tokens, "target": target, "route_index": route_index, "route_count": route_count, "route_gate": route_gate, "gate_weight": gate_weight, "up_weight": up_weight, "down_weight": down_weight}


def reference(tokens, target, route_index, route_count, route_gate, gate_weight, up_weight, down_weight):
    groups, experts, sources, per_source = route_index.shape
    model_width = tokens.shape[1]
    device_tokens = tokens.shape[0] // (groups * sources)
    usable = jnp.arange(per_source, dtype=jnp.int32)[None, None, None, :] < route_count[:, :, :, None]
    offsets = (jnp.arange(groups, dtype=jnp.int32)[:, None, None, None] * sources + jnp.arange(sources, dtype=jnp.int32)[None, None, :, None]) * device_tokens
    slot_token = (offsets + route_index).astype(jnp.int32).reshape(groups, experts, sources * per_source)
    slot_weight = jnp.where(usable, route_gate, 0.0).astype(jnp.float32).reshape(groups, experts, sources * per_source)
    usable_rows = usable.reshape(groups, experts, sources * per_source)
    expert_rows = tokens[slot_token] * usable_rows[..., None].astype(tokens.dtype)
    rows_wide = expert_rows.astype(jnp.float32)
    gate_wide = gate_weight.astype(jnp.float32)
    up_wide = up_weight.astype(jnp.float32)
    down_wide = down_weight.astype(jnp.float32)
    gate_pre = jnp.einsum("gerd,def->gerf", rows_wide, gate_wide)
    up_pre = jnp.einsum("gerd,def->gerf", rows_wide, up_wide)
    sigma = jax.nn.sigmoid(gate_pre)
    active = gate_pre * sigma
    hidden = (active * up_pre).astype(jnp.bfloat16)
    expert_out = jnp.einsum("gerf,def->gerd", hidden.astype(jnp.float32), down_wide).astype(jnp.bfloat16)
    flat_token = slot_token.reshape(-1)
    combined = jnp.zeros((tokens.shape[0], model_width), jnp.float32).at[flat_token].add(
        (slot_weight[..., None] * expert_out.astype(jnp.float32)).reshape(-1, model_width))
    out_grad = combined - target.astype(jnp.float32)
    slot_grad = (slot_weight[..., None] * out_grad[slot_token]).astype(jnp.bfloat16)
    hidden_grad = jnp.einsum("gerd,def->gerf", slot_grad.astype(jnp.float32), down_wide)
    gate_grad = (hidden_grad * up_pre * sigma * (1.0 + gate_pre * (1.0 - sigma))).astype(jnp.bfloat16)
    up_grad = (hidden_grad * active).astype(jnp.bfloat16)
    row_grad = (jnp.einsum("gerf,def->gerd", gate_grad.astype(jnp.float32), gate_wide)
                + jnp.einsum("gerf,def->gerd", up_grad.astype(jnp.float32), up_wide)).astype(jnp.bfloat16)
    token_grad = jnp.zeros((tokens.shape[0], model_width), jnp.float32).at[flat_token].add(
        row_grad.astype(jnp.float32).reshape(-1, model_width)).astype(jnp.bfloat16)
    factor = (groups * sources * per_source) ** -0.5
    gate_gradient = jnp.einsum("gerd,gerf->def", rows_wide, gate_grad.astype(jnp.float32)) * factor
    up_gradient = jnp.einsum("gerd,gerf->def", rows_wide, up_grad.astype(jnp.float32)) * factor
    down_gradient = jnp.einsum("gerd,gerf->def", slot_grad.astype(jnp.float32), hidden.astype(jnp.float32)) * factor
    return token_grad, gate_gradient, up_gradient, down_gradient
```

```python
import contextlib
import functools
import math

import jax
import jax.numpy as jnp
from jax import lax
from jax.experimental import pallas as pl
from jax.experimental.pallas import tpu as pltpu
from jax.sharding import PartitionSpec as P

F32 = jnp.float32
BF16 = jnp.bfloat16
VMEM_LIMIT = 67000000
CORES = 2
PIECES = 3
LAG = 2
LAG_PLANE = 2
LAG_BACK = 2


def dot(a, b, dims, precision=None):
    return lax.dot_general(
        a, b, (dims, ((), ())), preferred_element_type=F32, precision=precision
    )


def scope(name):
    return contextlib.nullcontext()


NN = ((1,), (0,))
NT = ((1,), (1,))
TN = ((0,), (0,))


def direct_kernel(
    planes, experts, slots, factor,
    index, count, gate, tokens, target, gw, uw, dw,
    cb_out, hot_out, gg_out, ug_out, dg_out,
    TOK, TGT, ROWS, TROWS, W, R, EO, RET, SG, G, RG, CB, PS, PR, H, GU, RX, GX, HX, GUX,
    t_loc, g_loc, w_loc, w_send, w_recv, a_loc, a_send, a_recv, p_send, p_recv,
    h_send, h_recv, x_send, x_recv, GRADS, o_loc,
):
    dp = lax.axis_index("dp")
    me_e = lax.axis_index("expert")
    me_z = dp // CORES
    core = dp % CORES
    peers = planes * experts
    per_group = experts * slots
    half = gw.shape[0]
    chunk = CORES * half
    ff = gw.shape[1]
    me = me_z * experts + me_e
    sibling = {"dp": me_z * CORES + (1 - core), "expert": me_e}
    order = sorted(range(1, planes), key=lambda k: -min(k, planes - k))

    def at(z, e):
        return {"dp": z * CORES + core, "expert": e}

    def plane(k):
        return (me_z + k) % planes

    def slot_rows(n):
        return pl.ds(pl.multiple_of(n * slots, slots), slots)

    def cols(z):
        return pl.ds(pl.multiple_of(z * chunk, chunk), chunk)

    def group_rows(z):
        return pl.ds(pl.multiple_of(z * per_group, per_group), per_group)

    barrier = pltpu.get_barrier_semaphore()

    def greet(k, carry):
        p = (me + k) % peers
        pl.semaphore_signal(
            barrier, inc=1, device_id=at(p // experts, p % experts),
            device_id_type=pl.DeviceIdType.MESH,
        )
        return carry

    lax.fori_loop(1, peers, greet, 0)
    pl.semaphore_signal(
        barrier, inc=1, device_id=sibling, device_id_type=pl.DeviceIdType.MESH
    )
    tok_copies = {}
    for k in order + [0]:
        z = plane(k)
        tok_copies[k] = pltpu.make_async_copy(
            tokens.at[:, cols(z)], TOK.at[:, cols(z)], t_loc.at[k]
        )
        tok_copies[k].start()
    locals_w = []
    for i, w in enumerate((gw, uw, dw)):
        c = pltpu.make_async_copy(w, W.at[i, core], w_loc.at[i])
        c.start()
        locals_w.append(c)
    tgt_copy = pltpu.make_async_copy(target, TGT, g_loc)
    tgt_copy.start()

    lane = lax.broadcasted_iota(jnp.int32, (slots, slots), 1)
    own_lane = lane == lax.broadcasted_iota(jnp.int32, (slots, slots), 0)
    slot_id = lax.broadcasted_iota(jnp.int32, (slots, 1), 0)
    names, weights = [], []
    for e in range(experts):
        live = slot_id < jnp.broadcast_to(count[0:1, e : e + 1], (slots, 1))
        ids = jnp.broadcast_to(index[0, e], (slots, slots))
        ids = jnp.sum(jnp.where(own_lane, ids, 0), axis=1, keepdims=True)
        names.append(jnp.where(live, ids, -1))
        g = jnp.broadcast_to(gate[0, e], (slots, slots))
        g = jnp.sum(jnp.where(own_lane, g, 0.0), axis=1, keepdims=True)
        weights.append(jnp.where(live, g, 0.0))
    names = jnp.concatenate(names, axis=0)
    wcol = jnp.concatenate(weights, axis=0)
    hot = (
        names == lax.broadcasted_iota(jnp.int32, (per_group, TOK.shape[0]), 1)
    ).astype(F32).astype(BF16)
    hot_out[...] = hot

    def remote(src, dst, s, r, dev):
        c = pltpu.make_async_remote_copy(
            src_ref=src, dst_ref=dst, send_sem=s, recv_sem=r,
            device_id=dev, device_id_type=pl.DeviceIdType.MESH,
        )
        c.start()
        return c

    def to_plane(i, z, source, land):
        here = z == me_z

        @pl.when(here)
        def _():
            pltpu.make_async_copy(source(me_z, me_e), land, a_loc.at[i]).start()

        first = jnp.where(here, 1, 0)

        def send(j, carry):
            e = (me_e + j) % experts
            remote(source(z, e), land, a_send.at[i], a_recv.at[i, me_z], at(z, e))
            return carry

        lax.fori_loop(first, experts, send, 0)

    def owners(src, dst, i, z):
        to_plane(i, z, lambda z, e: src.at[slot_rows(e), cols(z)], dst.at[slot_rows(me)])

    def sources(src, dst, i, z):
        to_plane(
            i, z, lambda z, e: src.at[slot_rows(z * experts + e)],
            dst.at[slot_rows(me_e), cols(me_z)],
        )

    def take(sem, ref):
        pltpu.make_async_copy(ref, ref, sem).wait()

    def arrived(i, k):
        if k == 0:
            take(a_recv.at[i, me_z], R.at[pl.ds(0, (experts - 1) * slots)])
            take(a_loc.at[i], R.at[pl.ds(0, slots)])
        else:
            take(a_recv.at[i, plane(k)], R.at[pl.ds(0, per_group)])

    outs = []

    def put(i, src, dst):
        c = pltpu.make_async_copy(src, dst, o_loc.at[i])
        c.start()
        outs.append(c)

    def weight(i):
        return W[i].reshape(chunk, ff)

    pl.semaphore_wait(barrier, peers)
    for k in order + [0]:
        z = plane(k)
        tok_copies[k].wait()
        ROWS[:, cols(z)] = dot(hot, TOK[:, cols(z)], NN).astype(BF16)
        owners(ROWS, R, 0, z)
    sent_w = [
        remote(w, W.at[i, core], w_send.at[i], w_recv.at[i], sibling)
        for i, w in enumerate((gw, uw, dw))
    ]

    def send_sum(i, k):
        remote(
            PS.at[i, group_rows(plane(k))], PR.at[i, k - 1],
            p_send.at[i], p_recv.at[i, k - 1], at(plane(k), me_e),
        )

    def pass_on(buf, i, s, way):
        to = me_z + way

        @pl.when(jnp.logical_and(to >= 0, to < planes))
        def _():
            rows_s = buf.at[group_rows(s)]
            remote(
                rows_s, rows_s, h_send.at[i, (way + 1) // 2, s], h_recv.at[i, s],
                at(to, me_e),
            )

    def spread(buf, i):
        for way in (1, -1):
            pass_on(buf, i, me_z, way)

    def along(bufs, first, fn):
        fn(me_z)
        for far in range(1, planes):
            for way in (1, -1):
                s = me_z - way * far

                @pl.when(jnp.logical_and(s >= 0, s < planes))
                def _():
                    for j, buf in enumerate(bufs):
                        take(h_recv.at[first + j, s], buf.at[group_rows(s)])
                        pass_on(buf, first + j, s, way)
                    fn(s)

    def spread_sent(buf, i):
        for s in range(planes):
            rows_s = buf.at[pl.ds(s * per_group, per_group)]

            @pl.when(jnp.logical_and(me_z > 0, me_z <= s))
            def _():
                take(h_send.at[i, 0, s], rows_s)

            @pl.when(jnp.logical_and(me_z < planes - 1, me_z >= s))
            def _():
                take(h_send.at[i, 1, s], rows_s)

    def total(i, own):
        for k in order:
            take(p_recv.at[i, k - 1], PR.at[i, k - 1])
            own = own + PR[i, k - 1].astype(F32)
        return own

    keep = pl.ds(pl.multiple_of(core * half, half), half)
    give = pl.ds(pl.multiple_of((1 - core) * half, half), half)
    mine = group_rows(me_z)

    for i in range(2):
        locals_w[i].wait()
        sent_w[i].wait_recv()
    for k in order:
        z = plane(k)
        arrived(0, k)
        for i in range(2):
            PS[i, group_rows(z), :] = dot(R[group_rows(z), :], weight(i), NN).astype(BF16)
            send_sum(i, k)
    arrived(0, 0)
    gate_own = dot(R[mine, :], weight(0), NN)
    up_own = dot(R[mine, :], weight(1), NN)
    x_rows = remote(R.at[:, give], RX, x_send.at[0], x_recv.at[0], sibling)
    tgt_copy.wait()
    for z in range(planes):
        piece = slice(z * chunk, (z + 1) * chunk)
        TROWS[:, piece] = dot(hot, TGT[:, piece], NN)
    same = dot(hot, hot, NT).astype(BF16)
    gate_pre = total(0, gate_own)
    up_pre = total(1, up_own)
    sigma = jax.nn.sigmoid(gate_pre)
    active = gate_pre * sigma
    H[mine, :] = (active * up_pre).astype(BF16)
    spread(H, 0)
    locals_w[2].wait()
    sent_w[2].wait_recv()

    def expert_out(z):
        EO[group_rows(z), :] = dot(H[group_rows(z), :], weight(2), NT).astype(BF16)
        sources(EO, RET, 1, z)

    along([H], 0, expert_out)
    x_hidden = remote(H, HX, x_send.at[1], x_recv.at[1], sibling)
    for k in order + [0]:
        z = plane(k)
        arrived(1, k)
        part = wcol * RET[:, cols(z)].astype(F32)
        combined = -TROWS[:, cols(z)]
        for _ in range(3):
            top = part.astype(BF16)
            combined = combined + dot(same, top, NN)
            part = part - top.astype(F32)
        SG[:, cols(z)] = (wcol * combined).astype(BF16)
        owners(SG, G, 2, z)

    for k in order:
        z = plane(k)
        arrived(2, k)
        PS[2, group_rows(z), :] = dot(G[group_rows(z), :], weight(2), NN).astype(BF16)
        send_sum(2, k)
    arrived(2, 0)
    own = dot(G[mine, :], weight(2), NN)
    x_grad = remote(G.at[:, give], GX, x_send.at[2], x_recv.at[2], sibling)
    x_hidden.wait_recv()
    x_grad.wait_recv()
    GRADS[2] = (dot(G[:, keep], H[...], TN) + dot(GX[...], HX[...], TN)) * factor
    put(2, GRADS.at[2], dg_out)
    hidden_grad = total(2, own)
    GU[0, mine, :] = (
        hidden_grad * up_pre * sigma * (1.0 + gate_pre * (1.0 - sigma))
    ).astype(BF16)
    spread(GU.at[0], 1)
    GU[1, mine, :] = (hidden_grad * active).astype(BF16)
    spread(GU.at[1], 2)

    def row_grad(z):
        RG[group_rows(z), :] = (
            dot(GU[0, group_rows(z), :], weight(0), NT)
            + dot(GU[1, group_rows(z), :], weight(1), NT)
        ).astype(BF16)
        sources(RG, CB, 3, z)

    along([GU.at[0], GU.at[1]], 1, row_grad)
    x_gate = remote(GU.at[0], GUX.at[0], x_send.at[3], x_recv.at[3], sibling)
    x_up = remote(GU.at[1], GUX.at[1], x_send.at[4], x_recv.at[4], sibling)
    x_rows.wait_recv()
    x_gate.wait_recv()
    GRADS[0] = (dot(R[:, keep], GU[0], TN) + dot(RX[...], GUX[0], TN)) * factor
    put(0, GRADS.at[0], gg_out)
    x_up.wait_recv()
    GRADS[1] = (dot(R[:, keep], GU[1], TN) + dot(RX[...], GUX[1], TN)) * factor
    put(1, GRADS.at[1], ug_out)
    for k in order + [0]:
        arrived(3, k)
    put(3, CB, cb_out)

    for c in sent_w + [x_rows, x_hidden, x_grad, x_gate, x_up]:
        c.wait_send()
    for i in range(4):
        take(a_send.at[i], R.at[pl.ds(0, (peers - 1) * slots)])
    for i in range(3):
        take(p_send.at[i], PR.at[i])
    for i, buf in enumerate((H, GU.at[0], GU.at[1])):
        spread_sent(buf, i)
    for c in outs:
        c.wait()


def chain_kernel(
    planes, experts, slots, factor, pieces,
    index, count, gate, tokens, target, gw, uw, dw,
    cb_out, hot_out, gg_out, ug_out, dg_out,
    TOK, TGT, ROWS, TROWS, META, MT, W, R, TR, G, EOG,
    OWN, IN, OUT, HOWN, HIN, HOUT, H, GU, RG, CB, RX, GX, HX, GUX, GRADS,
    t_loc, g_loc, w_loc, w_send, w_recv, a_send, a_recv, e_send, e_recv,
    c_send, c_recv, h_send, h_recv, x_send, x_recv, o_loc,
):
    dp = lax.axis_index("dp")
    me_e = lax.axis_index("expert")
    me_z = dp // CORES
    core = dp % CORES
    peers = planes * experts
    per_group = experts * slots
    half = gw.shape[0]
    chunk = CORES * half
    ff = gw.shape[1]
    fw = ff // pieces
    me = me_z * experts + me_e
    sibling = {"dp": me_z * CORES + (1 - core), "expert": me_e}
    far_first = sorted(range(1, planes), key=lambda k: -min(k, planes - k)) + [0]
    ways = (1, -1)
    dist = (me_z, planes - 1 - me_z)
    depth = jnp.maximum(dist[0], dist[1])

    def at(z, e):
        return {"dp": z * CORES + core, "expert": e}

    def plane(k):
        return (me_z + k) % planes

    def slot_rows(n):
        return pl.ds(pl.multiple_of(n * slots, slots), slots)

    def cols(z):
        return pl.ds(pl.multiple_of(z * chunk, chunk), chunk)

    def group_rows(z):
        return pl.ds(pl.multiple_of(z * per_group, per_group), per_group)

    def turn(g):
        if planes % 2:
            return g
        return planes // 2 - 1 - g // 2 + (g % 2) * (2 * (g // 2) + 1)

    barrier = pltpu.get_barrier_semaphore()

    def greet(k, carry):
        p = (me + k) % peers
        pl.semaphore_signal(
            barrier, inc=1, device_id=at(p // experts, p % experts),
            device_id_type=pl.DeviceIdType.MESH,
        )
        return carry

    lax.fori_loop(1, peers, greet, 0)
    pl.semaphore_signal(
        barrier, inc=1, device_id=sibling, device_id_type=pl.DeviceIdType.MESH
    )
    tok_copies = {}
    for k in far_first:
        tok_copies[k] = pltpu.make_async_copy(
            tokens.at[:, cols(plane(k))], TOK.at[:, cols(plane(k))], t_loc.at[k]
        )
        tok_copies[k].start()
    locals_w = []
    keep = pl.ds(pl.multiple_of(core * half, half), half)
    give = pl.ds(pl.multiple_of((1 - core) * half, half), half)
    for i, w in enumerate((gw, uw, dw)):
        c = pltpu.make_async_copy(w, W.at[i, keep], w_loc.at[i])
        c.start()
        locals_w.append(c)
    tgt_copy = pltpu.make_async_copy(target, TGT, g_loc)
    tgt_copy.start()

    lane = lax.broadcasted_iota(jnp.int32, (slots, slots), 1)
    own_lane = lane == lax.broadcasted_iota(jnp.int32, (slots, slots), 0)
    slot_id = lax.broadcasted_iota(jnp.int32, (slots, 1), 0)
    names, weights = [], []
    for e in range(experts):
        live = slot_id < jnp.broadcast_to(count[0:1, e : e + 1], (slots, 1))
        ids = jnp.broadcast_to(index[0, e], (slots, slots))
        ids = jnp.sum(jnp.where(own_lane, ids, 0), axis=1, keepdims=True)
        names.append(jnp.where(live, ids, -1))
        g = jnp.broadcast_to(gate[0, e], (slots, slots))
        g = jnp.sum(jnp.where(own_lane, g, 0.0), axis=1, keepdims=True)
        weights.append(jnp.where(live, g, 0.0))
    names = jnp.concatenate(names, axis=0)
    wcol = jnp.concatenate(weights, axis=0)
    hot = (
        names == lax.broadcasted_iota(jnp.int32, (per_group, TOK.shape[0]), 1)
    ).astype(F32).astype(BF16)
    hot_out[...] = hot

    def remote(src, dst, s, r, dev):
        c = pltpu.make_async_remote_copy(
            src_ref=src, dst_ref=dst, send_sem=s, recv_sem=r,
            device_id=dev, device_id_type=pl.DeviceIdType.MESH,
        )
        c.start()
        return c

    def take(sem, ref):
        pltpu.make_async_copy(ref, ref, sem).wait()

    def to_plane(i, z, source, land):
        here = z == me_z

        @pl.when(here)
        def _():
            pltpu.make_async_copy(source(me_z, me_e), land, a_recv.at[i, me_z]).start()

        def send(j, carry):
            e = (me_e + j) % experts
            remote(source(z, e), land, a_send.at[i], a_recv.at[i, me_z], at(z, e))
            return carry

        lax.fori_loop(jnp.where(here, 1, 0), experts, send, 0)

    for k in far_first:
        z = plane(k)
        tok_copies[k].wait()
        ROWS[:, cols(z)] = dot(hot, TOK[:, cols(z)], NN).astype(BF16)
    for way, d in zip(ways, range(2)):
        @pl.when(dist[d] == 0)
        def _():
            IN[d] = jnp.zeros(IN.shape[1:], BF16)
            HIN[d] = jnp.zeros(HIN.shape[1:], BF16)

    with scope("barrier"):
        pl.semaphore_wait(barrier, peers)
    sent_w = [
        remote(w, W.at[i, keep], w_send.at[i], w_recv.at[i], sibling)
        for i, w in enumerate((gw, uw, dw))
    ]
    for k in far_first:
        to_plane(
            0, plane(k), lambda z, e: ROWS.at[slot_rows(e), cols(z)], R.at[slot_rows(me)]
        )
    with scope("trows"):
        tgt_copy.wait()
        for k in far_first:
            z = plane(k)
            TROWS[:, cols(z)] = dot(hot, TGT[:, cols(z)], NN).astype(BF16)
            to_plane(
                1, z, lambda z, e: TROWS.at[slot_rows(e), cols(z)], TR.at[slot_rows(me)]
            )
    with scope("meta"):
        square = (per_group, per_group)
        eye = lax.broadcasted_iota(jnp.int32, square, 0) == lax.broadcasted_iota(
            jnp.int32, square, 1
        )
        wrow = jnp.sum(jnp.where(eye, wcol, 0.0), axis=0, keepdims=True)
        mix = wcol * dot(hot, hot, NT) * wrow
        pad = (META.shape[1] - 256) // 2
        META[...] = jnp.zeros(META.shape, BF16)
        for part, start, stop in (
            (mix, 0, per_group), (jnp.broadcast_to(wcol, (per_group, 128)), 2 * pad, 2 * pad + 128)
        ):
            top = part.astype(BF16)
            step = pad if start == 0 else 128
            META[:, start:stop] = top
            META[:, start + step : stop + step] = (part - top.astype(F32)).astype(BF16)
        for k in far_first:
            to_plane(2, plane(k), lambda z, e: META.at[slot_rows(e)], MT.at[slot_rows(me)])

    with scope("w_wait"):
        for i in range(3):
            locals_w[i].wait()
            sent_w[i].wait_recv()

    def piece(f):
        return pl.ds(pl.multiple_of(f * fw, fw), fw)

    def group_of(c):
        return turn(c // pieces)

    def rows_in(z):
        take(a_recv.at[0, z], R.at[pl.ds(0, per_group)])

    def partial_sums(c):
        z, f = group_of(c), c % pieces

        @pl.when(f == 0)
        def _():
            with scope("x_wait"):
                rows_in(z)

        with scope("own"):
            rows = R[group_rows(z), :]
            for i in range(2):
                OWN[c, :, i * fw : (i + 1) * fw] = dot(rows, W[i, :, piece(f)], NN)

    def move(own, inn, out, send, recv, d, c):
        @pl.when(dist[d] > 0)
        def _():
            with scope("mv%d" % (own is HOWN)):
                take(recv.at[d, c], inn.at[d, c])

        @pl.when(dist[d] < planes - 1)
        def _():
            out[d, c] = (own[c] + inn[d, c].astype(F32)).astype(BF16)
            remote(
                out.at[d, c], inn.at[d, c], send.at[d], recv.at[d, c],
                at(me_z + ways[d], me_e),
            )

    def total(own, inn, c):
        return own[c] + inn[0, c].astype(F32) + inn[1, c].astype(F32)

    def to_sibling(i, src, dst):
        remote(src, dst, x_send.at[i], x_recv.at[i], sibling)

    def forward(c):
        z, f = group_of(c), c % pieces
        with scope("fwd"):
            both = total(OWN, IN, c)
            OWN[c] = both
            pre, up = both[:, :fw], both[:, fw:]
            H[group_rows(z), piece(f)] = (pre * jax.nn.sigmoid(pre) * up).astype(BF16)

        @pl.when(f == pieces - 1)
        def _():
            with scope("eo"):
                EOG[z, me_e] = dot(H[group_rows(z), :], W[2], NT).astype(BF16)

                def send(j, carry):
                    remote(
                        EOG.at[z, me_e], EOG.at[z, me_e], e_send, e_recv.at[z],
                        at(me_z, (me_e + j) % experts),
                    )
                    return carry

                lax.fori_loop(1, experts, send, 0)
                to_sibling(1, H.at[group_rows(z)], HX.at[group_rows(z)])

    def slot_grads(g):
        z = turn(g)
        with scope("eo_wait"):
            take(e_recv.at[z], EOG.at[z, pl.ds(0, experts - 1)])
            take(a_recv.at[1, z], TR.at[pl.ds(0, per_group)])
            take(a_recv.at[2, z], MT.at[pl.ds(0, per_group)])
        with scope("comb"):
            for s in range(experts):
                its = slice(s * slots, (s + 1) * slots)
                mine = slot_rows(z * experts + s)
                outs = jnp.concatenate([EOG[z, e, its, :] for e in range(experts)], axis=0)
                wide = dot(MT[mine, 0:per_group], outs, NN) + dot(
                    MT[mine, pad : pad + per_group], outs, NN
                )
                w = MT[mine, 2 * pad : 2 * pad + 1].astype(F32) + MT[
                    mine, 2 * pad + 128 : 2 * pad + 129
                ].astype(F32)
                G[mine, :] = (wide - w * TR[mine, :].astype(F32)).astype(BF16)
            HOWN[g] = dot(G[group_rows(z), :], W[2], NN)
            to_sibling(2, G.at[group_rows(z), give], GX.at[group_rows(z)])

    def backward(g):
        z = turn(g)
        rows = group_rows(z)
        with scope("bwd"):
            hidden_grad = total(HOWN, HIN, g)
            for f in range(pieces):
                both = OWN[g * pieces + f]
                pre, up = both[:, :fw], both[:, fw:]
                grad = hidden_grad[:, f * fw : (f + 1) * fw]
                sigma = jax.nn.sigmoid(pre)
                GU[0, rows, f * fw : (f + 1) * fw] = (
                    grad * up * sigma * (1.0 + pre * (1.0 - sigma))
                ).astype(BF16)
                GU[1, rows, f * fw : (f + 1) * fw] = (grad * (pre * sigma)).astype(BF16)
            RG[rows, :] = (
                dot(GU[0, rows, :], W[0], NT) + dot(GU[1, rows, :], W[1], NT)
            ).astype(BF16)
            to_plane(
                3, z, lambda z, e: RG.at[slot_rows(z * experts + e)],
                CB.at[slot_rows(me_e), cols(me_z)],
            )
            for i in range(2):
                to_sibling(3 + i, GU.at[i, rows], GUX.at[i, rows])

    steps = planes * pieces
    ready = LAG * depth
    combined = pieces - 1 + ready + LAG_PLANE
    started = pieces - 1 + LAG * (planes - 1) + LAG_PLANE
    moved = started + LAG_BACK * depth

    def each(t, fn, last):
        @pl.when(jnp.logical_and(t >= 0, t < last))
        def _():
            fn(t)

    def each_group(t, fn):
        @pl.when(jnp.logical_and(jnp.logical_and(t >= 0, t < steps), t % pieces == 0))
        def _():
            fn(t // pieces)

    def grad(i, left, left_x, right, right_x, out):
        GRADS[i] = (dot(left, right, TN) + dot(left_x, right_x, TN)) * factor
        c = pltpu.make_async_copy(GRADS.at[i], out, o_loc.at[i])
        c.start()

    def tick(t, carry):
        each(t, partial_sums, steps)
        for d in range(2):
            each(
                t - LAG * dist[d],
                functools.partial(move, OWN, IN, OUT, c_send, c_recv, d), steps,
            )
        each(t - ready, forward, steps)
        each_group(t - combined, slot_grads)
        for d in range(2):
            each_group(
                t - started - LAG_BACK * dist[d],
                functools.partial(move, HOWN, HIN, HOUT, h_send, h_recv, d),
            )
        each_group(t - moved, backward)
        return carry

    end = steps - pieces + pieces - 1 + (LAG + LAG_BACK) * (planes - 1) + LAG_PLANE + 1
    middle = steps - pieces + pieces - 1 + LAG * (planes - 1) + LAG_PLANE + 1
    lax.fori_loop(0, middle, tick, 0)
    to_sibling(0, R.at[:, give], RX)
    with scope("dgrad"):
        take(x_recv.at[1], HX)
        take(x_recv.at[2], GX)
        grad(2, G[:, keep], GX[...], H[...], HX[...], dg_out)
    lax.fori_loop(middle, end, tick, 0)
    with scope("xg"):
        take(x_recv.at[0], RX)
        take(x_recv.at[3], GUX.at[0])
        take(x_recv.at[4], GUX.at[1])
    with scope("gugrad"):
        grad(0, R[:, keep], RX[...], GU[0], GUX[0], gg_out)
        grad(1, R[:, keep], RX[...], GU[1], GUX[1], ug_out)
    with scope("cb_wait"):
        for k in far_first:
            take(a_recv.at[3, plane(k)], R.at[pl.ds(0, per_group)])
    with scope("tail"):
        back = pltpu.make_async_copy(CB, cb_out, o_loc.at[3])
        back.start()
        for c in sent_w:
            c.wait_send()
        others = pl.ds(0, (peers - 1) * slots)
        for i, buf in enumerate((R, TR, MT, RG)):
            take(a_send.at[i], buf.at[others])
        take(e_send, EOG.at[:, pl.ds(0, experts - 1)])
        for d in range(2):
            @pl.when(dist[d] < planes - 1)
            def _():
                take(c_send.at[d], OUT.at[d])
                take(h_send.at[d], HOUT.at[d])
        for i, buf in enumerate((RX, HX, GX, GUX.at[0], GUX.at[1])):
            take(x_send.at[i], buf)
        for i, out in enumerate((gg_out, ug_out, dg_out)):
            pltpu.make_async_copy(GRADS.at[i], out, o_loc.at[i]).wait()
        back.wait()


def finish(hot, cb, gg, ug, dg, tg_out, gg_out, ug_out, dg_out):
    tg_out[...] = dot(hot[...], cb[...], TN).astype(BF16)
    gg_out[:, 0, :] = gg[...]
    ug_out[:, 0, :] = ug[...]
    dg_out[:, 0, :] = dg[...]


def direct_scratch(planes, picked, count, width, half, ff):
    chunk = CORES * half
    all_rows = planes * picked
    dma = pltpu.SemaphoreType.DMA
    return [
        pltpu.VMEM((count, width), BF16),
        pltpu.VMEM((count, width), BF16),
        pltpu.VMEM((picked, width), BF16),
        pltpu.VMEM((picked, width), F32),
        pltpu.VMEM((3, CORES, half, ff), BF16),
        pltpu.VMEM((all_rows, chunk), BF16),
        pltpu.VMEM((all_rows, chunk), BF16),
        pltpu.VMEM((picked, width), BF16),
        pltpu.VMEM((picked, width), BF16),
        pltpu.VMEM((all_rows, chunk), BF16),
        pltpu.VMEM((all_rows, chunk), BF16),
        pltpu.VMEM((picked, width), BF16),
        pltpu.VMEM((3, all_rows, ff), BF16),
        pltpu.VMEM((3, planes - 1, picked, ff), BF16),
        pltpu.VMEM((all_rows, ff), BF16),
        pltpu.VMEM((2, all_rows, ff), BF16),
        pltpu.VMEM((all_rows, half), BF16),
        pltpu.VMEM((all_rows, half), BF16),
        pltpu.VMEM((all_rows, ff), BF16),
        pltpu.VMEM((2, all_rows, ff), BF16),
        dma((planes,)), dma,
        dma((3,)), dma((3,)), dma((3,)),
        dma((4,)), dma((4,)), dma((4, planes)),
        dma((3,)), dma((3, planes)),
        dma((3, 2, planes)), dma((3, planes)),
        dma((5,)), dma((5,)),
        pltpu.VMEM((3, half, ff), F32), dma((4,)),
    ]


def chain_scratch(planes, experts, picked, count, width, half, ff, pieces):
    chunk = CORES * half
    all_rows = planes * picked
    steps = planes * pieces
    fw = ff // pieces
    table = 2 * (-(-picked // 128) * 128) + 256
    dma = pltpu.SemaphoreType.DMA
    return [
        pltpu.VMEM((count, width), BF16),
        pltpu.VMEM((count, width), BF16),
        pltpu.VMEM((picked, width), BF16),
        pltpu.VMEM((picked, width), BF16),
        pltpu.VMEM((picked, table), BF16),
        pltpu.VMEM((all_rows, table), BF16),
        pltpu.VMEM((3, chunk, ff), BF16),
        pltpu.VMEM((all_rows, chunk), BF16),
        pltpu.VMEM((all_rows, chunk), BF16),
        pltpu.VMEM((all_rows, chunk), BF16),
        pltpu.VMEM((planes, experts, picked, chunk), BF16),
        pltpu.VMEM((steps, picked, 2 * fw), F32),
        pltpu.VMEM((2, steps, picked, 2 * fw), BF16),
        pltpu.VMEM((2, steps, picked, 2 * fw), BF16),
        pltpu.VMEM((planes, picked, ff), F32),
        pltpu.VMEM((2, planes, picked, ff), BF16),
        pltpu.VMEM((2, planes, picked, ff), BF16),
        pltpu.VMEM((all_rows, ff), BF16),
        pltpu.VMEM((2, all_rows, ff), BF16),
        pltpu.VMEM((all_rows, chunk), BF16),
        pltpu.VMEM((picked, width), BF16),
        pltpu.VMEM((all_rows, half), BF16),
        pltpu.VMEM((all_rows, half), BF16),
        pltpu.VMEM((all_rows, ff), BF16),
        pltpu.VMEM((2, all_rows, ff), BF16),
        pltpu.VMEM((3, half, ff), F32),
        dma((planes,)), dma, dma((3,)), dma((3,)), dma((3,)),
        dma((4,)), dma((4, planes)), dma, dma((planes,)),
        dma((2,)), dma((2, steps)), dma((2,)), dma((2, planes)),
        dma((5,)), dma((5,)), dma((4,)),
    ]


def held_bytes(scratch):
    return sum(
        math.prod(s.shape) * jnp.dtype(s.dtype).itemsize
        for s in scratch
        if getattr(s, "memory_space", None) == pltpu.VMEM
    )


def on_device(
    tokens, target, route_index, route_count, route_gate, gate_weight, up_weight, down_weight
):
    groups = lax.axis_size("dp")
    experts = lax.axis_size("expert")
    planes = groups // CORES
    slots = route_index.shape[3]
    count, width = tokens.shape
    half, _, ff = gate_weight.shape
    picked = experts * slots
    factor = (groups * experts * slots) ** (-0.5)
    pieces = max(n for n in range(1, PIECES + 1) if ff % (128 * n) == 0)
    vmem = pl.BlockSpec(memory_space=pltpu.VMEM)
    anyw = pl.BlockSpec(memory_space=pl.ANY)
    grad = jax.ShapeDtypeStruct((half, ff), F32)
    scratch = chain_scratch(planes, experts, picked, count, width, half, ff, pieces)
    body = functools.partial(chain_kernel, planes, experts, slots, factor, pieces)
    if held_bytes(scratch) > VMEM_LIMIT * 3 // 4:
        scratch = direct_scratch(planes, picked, count, width, half, ff)
        body = functools.partial(direct_kernel, planes, experts, slots, factor)
    came_back, hot, gate_gradient, up_gradient, down_gradient = pl.pallas_call(
        body,
        out_shape=(
            jax.ShapeDtypeStruct((picked, width), BF16),
            jax.ShapeDtypeStruct((picked, count), BF16),
            grad, grad, grad,
        ),
        in_specs=[vmem] * 3 + [anyw] * 5,
        out_specs=(anyw, vmem) + (anyw,) * 3,
        scratch_shapes=scratch,
        compiler_params=pltpu.CompilerParams(
            collective_id=0, has_side_effects=True, vmem_limit_bytes=VMEM_LIMIT
        ),
        name="routed_layer",
    )(
        route_index, route_count.reshape(1, experts), route_gate, tokens, target,
        gate_weight.reshape(half, ff), up_weight.reshape(half, ff),
        down_weight.reshape(half, ff),
    )
    steps = 2
    part = pl.BlockSpec((half // steps, ff), lambda i: (i, 0))
    part_out = pl.BlockSpec((half // steps, 1, ff), lambda i: (i, 0, 0))
    grad = jax.ShapeDtypeStruct((half, 1, ff), F32)
    return tuple(pl.pallas_call(
        finish,
        grid=(steps,),
        out_shape=(jax.ShapeDtypeStruct((count, width), BF16), grad, grad, grad),
        in_specs=[
            pl.BlockSpec((picked, count // steps), lambda i: (0, i)),
            pl.BlockSpec((picked, width), lambda i: (0, 0)),
            part, part, part,
        ],
        out_specs=(
            pl.BlockSpec((count // steps, width), lambda i: (i, 0)),
            part_out, part_out, part_out,
        ),
        compiler_params=pltpu.CompilerParams(vmem_limit_bytes=VMEM_LIMIT),
        name="finish",
    )(hot, came_back, gate_gradient, up_gradient, down_gradient))


def solution(mesh):
    return jax.shard_map(
        on_device,
        mesh=mesh,
        in_specs=(
            P(("dp", "expert"), None),
            P(("dp", "expert"), None),
            P("dp", None, "expert", None),
            P("dp", None, "expert"),
            P("dp", None, "expert", None),
            P("dp", "expert", None),
            P("dp", "expert", None),
            P("dp", "expert", None),
        ),
        out_specs=(
            P(("dp", "expert"), None),
            P("dp", "expert", None),
            P("dp", "expert", None),
            P("dp", "expert", None),
        ),
        check_vma=False,
    )
```

```python
import contextlib
import functools
import math

import jax
import jax.numpy as jnp
from jax import lax
from jax.experimental import pallas as pl
from jax.experimental.pallas import tpu as pltpu
from jax.sharding import PartitionSpec as P

F32 = jnp.float32
BF16 = jnp.bfloat16
VMEM_LIMIT = 67000000
CORES = 2
PIECES = 3
LAG = 3
LAG_PLANE = 4
LAG_BACK = 4
LAG_ROWS = 0
BACK_PIECES = 3
TARGET_AT = -1
TARGET_STEP = 0
NEAR_TOKENS = False
NEAR_TARGETS = False
CHAIN_LIMIT = 44000000
FINISH_LIMIT = 40000000


def dot(a, b, dims, precision=None):
    return lax.dot_general(
        a, b, (dims, ((), ())), preferred_element_type=F32, precision=precision
    )


def scope(name):
    return contextlib.nullcontext()


NN = ((1,), (0,))
NT = ((1,), (1,))
TN = ((0,), (0,))


def direct_kernel(
    planes, experts, slots, factor,
    index, count, gate, tokens, target, gw, uw, dw,
    cb_out, hot_out, gg_out, ug_out, dg_out,
    TOK, TGT, ROWS, TROWS, W, R, EO, RET, SG, G, RG, CB, PS, PR, H, GU, RX, GX, HX, GUX,
    t_loc, g_loc, w_loc, w_send, w_recv, a_loc, a_send, a_recv, p_send, p_recv,
    h_send, h_recv, x_send, x_recv, GRADS, o_loc,
):
    dp = lax.axis_index("dp")
    me_e = lax.axis_index("expert")
    me_z = dp // CORES
    core = dp % CORES
    peers = planes * experts
    per_group = experts * slots
    half = gw.shape[0]
    chunk = CORES * half
    ff = gw.shape[1]
    me = me_z * experts + me_e
    sibling = {"dp": me_z * CORES + (1 - core), "expert": me_e}
    order = sorted(range(1, planes), key=lambda k: -min(k, planes - k))

    def at(z, e):
        return {"dp": z * CORES + core, "expert": e}

    def plane(k):
        return (me_z + k) % planes

    def slot_rows(n):
        return pl.ds(pl.multiple_of(n * slots, slots), slots)

    def cols(z):
        return pl.ds(pl.multiple_of(z * chunk, chunk), chunk)

    def group_rows(z):
        return pl.ds(pl.multiple_of(z * per_group, per_group), per_group)

    barrier = pltpu.get_barrier_semaphore()

    def greet(k, carry):
        p = (me + k) % peers
        pl.semaphore_signal(
            barrier, inc=1, device_id=at(p // experts, p % experts),
            device_id_type=pl.DeviceIdType.MESH,
        )
        return carry

    lax.fori_loop(1, peers, greet, 0)
    pl.semaphore_signal(
        barrier, inc=1, device_id=sibling, device_id_type=pl.DeviceIdType.MESH
    )
    tok_copies = {}
    for k in order + [0]:
        z = plane(k)
        tok_copies[k] = pltpu.make_async_copy(
            tokens.at[:, cols(z)], TOK.at[:, cols(z)], t_loc.at[k]
        )
        tok_copies[k].start()
    locals_w = []
    for i, w in enumerate((gw, uw, dw)):
        c = pltpu.make_async_copy(w, W.at[i, core], w_loc.at[i])
        c.start()
        locals_w.append(c)
    tgt_copy = pltpu.make_async_copy(target, TGT, g_loc)
    tgt_copy.start()

    lane = lax.broadcasted_iota(jnp.int32, (slots, slots), 1)
    own_lane = lane == lax.broadcasted_iota(jnp.int32, (slots, slots), 0)
    slot_id = lax.broadcasted_iota(jnp.int32, (slots, 1), 0)
    names, weights = [], []
    for e in range(experts):
        live = slot_id < jnp.broadcast_to(count[0:1, e : e + 1], (slots, 1))
        ids = jnp.broadcast_to(index[0, e], (slots, slots))
        ids = jnp.sum(jnp.where(own_lane, ids, 0), axis=1, keepdims=True)
        names.append(jnp.where(live, ids, -1))
        g = jnp.broadcast_to(gate[0, e], (slots, slots))
        g = jnp.sum(jnp.where(own_lane, g, 0.0), axis=1, keepdims=True)
        weights.append(jnp.where(live, g, 0.0))
    names = jnp.concatenate(names, axis=0)
    wcol = jnp.concatenate(weights, axis=0)
    hot = (
        names == lax.broadcasted_iota(jnp.int32, (per_group, TOK.shape[0]), 1)
    ).astype(F32).astype(BF16)
    hot_out[...] = hot

    def remote(src, dst, s, r, dev):
        c = pltpu.make_async_remote_copy(
            src_ref=src, dst_ref=dst, send_sem=s, recv_sem=r,
            device_id=dev, device_id_type=pl.DeviceIdType.MESH,
        )
        c.start()
        return c

    def to_plane(i, z, source, land):
        here = z == me_z

        @pl.when(here)
        def _():
            pltpu.make_async_copy(source(me_z, me_e), land, a_loc.at[i]).start()

        first = jnp.where(here, 1, 0)

        def send(j, carry):
            e = (me_e + j) % experts
            remote(source(z, e), land, a_send.at[i], a_recv.at[i, me_z], at(z, e))
            return carry

        lax.fori_loop(first, experts, send, 0)

    def owners(src, dst, i, z):
        to_plane(i, z, lambda z, e: src.at[slot_rows(e), cols(z)], dst.at[slot_rows(me)])

    def sources(src, dst, i, z):
        to_plane(
            i, z, lambda z, e: src.at[slot_rows(z * experts + e)],
            dst.at[slot_rows(me_e), cols(me_z)],
        )

    def take(sem, ref):
        pltpu.make_async_copy(ref, ref, sem).wait()

    def arrived(i, k):
        if k == 0:
            take(a_recv.at[i, me_z], R.at[pl.ds(0, (experts - 1) * slots)])
            take(a_loc.at[i], R.at[pl.ds(0, slots)])
        else:
            take(a_recv.at[i, plane(k)], R.at[pl.ds(0, per_group)])

    outs = []

    def put(i, src, dst):
        c = pltpu.make_async_copy(src, dst, o_loc.at[i])
        c.start()
        outs.append(c)

    def weight(i):
        return W[i].reshape(chunk, ff)

    pl.semaphore_wait(barrier, peers)
    for k in order + [0]:
        z = plane(k)
        tok_copies[k].wait()
        ROWS[:, cols(z)] = dot(hot, TOK[:, cols(z)], NN).astype(BF16)
        owners(ROWS, R, 0, z)
    sent_w = [
        remote(w, W.at[i, core], w_send.at[i], w_recv.at[i], sibling)
        for i, w in enumerate((gw, uw, dw))
    ]

    def send_sum(i, k):
        remote(
            PS.at[i, group_rows(plane(k))], PR.at[i, k - 1],
            p_send.at[i], p_recv.at[i, k - 1], at(plane(k), me_e),
        )

    def pass_on(buf, i, s, way):
        to = me_z + way

        @pl.when(jnp.logical_and(to >= 0, to < planes))
        def _():
            rows_s = buf.at[group_rows(s)]
            remote(
                rows_s, rows_s, h_send.at[i, (way + 1) // 2, s], h_recv.at[i, s],
                at(to, me_e),
            )

    def spread(buf, i):
        for way in (1, -1):
            pass_on(buf, i, me_z, way)

    def along(bufs, first, fn):
        fn(me_z)
        for far in range(1, planes):
            for way in (1, -1):
                s = me_z - way * far

                @pl.when(jnp.logical_and(s >= 0, s < planes))
                def _():
                    for j, buf in enumerate(bufs):
                        take(h_recv.at[first + j, s], buf.at[group_rows(s)])
                        pass_on(buf, first + j, s, way)
                    fn(s)

    def spread_sent(buf, i):
        for s in range(planes):
            rows_s = buf.at[pl.ds(s * per_group, per_group)]

            @pl.when(jnp.logical_and(me_z > 0, me_z <= s))
            def _():
                take(h_send.at[i, 0, s], rows_s)

            @pl.when(jnp.logical_and(me_z < planes - 1, me_z >= s))
            def _():
                take(h_send.at[i, 1, s], rows_s)

    def total(i, own):
        for k in order:
            take(p_recv.at[i, k - 1], PR.at[i, k - 1])
            own = own + PR[i, k - 1].astype(F32)
        return own

    keep = pl.ds(pl.multiple_of(core * half, half), half)
    give = pl.ds(pl.multiple_of((1 - core) * half, half), half)
    mine = group_rows(me_z)

    for i in range(2):
        locals_w[i].wait()
        sent_w[i].wait_recv()
    for k in order:
        z = plane(k)
        arrived(0, k)
        for i in range(2):
            PS[i, group_rows(z), :] = dot(R[group_rows(z), :], weight(i), NN).astype(BF16)
            send_sum(i, k)
    arrived(0, 0)
    gate_own = dot(R[mine, :], weight(0), NN)
    up_own = dot(R[mine, :], weight(1), NN)
    x_rows = remote(R.at[:, give], RX, x_send.at[0], x_recv.at[0], sibling)
    tgt_copy.wait()
    for z in range(planes):
        piece = slice(z * chunk, (z + 1) * chunk)
        TROWS[:, piece] = dot(hot, TGT[:, piece], NN)
    same = dot(hot, hot, NT).astype(BF16)
    gate_pre = total(0, gate_own)
    up_pre = total(1, up_own)
    sigma = jax.nn.sigmoid(gate_pre)
    active = gate_pre * sigma
    H[mine, :] = (active * up_pre).astype(BF16)
    spread(H, 0)
    locals_w[2].wait()
    sent_w[2].wait_recv()

    def expert_out(z):
        EO[group_rows(z), :] = dot(H[group_rows(z), :], weight(2), NT).astype(BF16)
        sources(EO, RET, 1, z)

    along([H], 0, expert_out)
    x_hidden = remote(H, HX, x_send.at[1], x_recv.at[1], sibling)
    for k in order + [0]:
        z = plane(k)
        arrived(1, k)
        part = wcol * RET[:, cols(z)].astype(F32)
        combined = -TROWS[:, cols(z)]
        for _ in range(3):
            top = part.astype(BF16)
            combined = combined + dot(same, top, NN)
            part = part - top.astype(F32)
        SG[:, cols(z)] = (wcol * combined).astype(BF16)
        owners(SG, G, 2, z)

    for k in order:
        z = plane(k)
        arrived(2, k)
        PS[2, group_rows(z), :] = dot(G[group_rows(z), :], weight(2), NN).astype(BF16)
        send_sum(2, k)
    arrived(2, 0)
    own = dot(G[mine, :], weight(2), NN)
    x_grad = remote(G.at[:, give], GX, x_send.at[2], x_recv.at[2], sibling)
    x_hidden.wait_recv()
    x_grad.wait_recv()
    GRADS[2] = (dot(G[:, keep], H[...], TN) + dot(GX[...], HX[...], TN)) * factor
    put(2, GRADS.at[2], dg_out)
    hidden_grad = total(2, own)
    GU[0, mine, :] = (
        hidden_grad * up_pre * sigma * (1.0 + gate_pre * (1.0 - sigma))
    ).astype(BF16)
    spread(GU.at[0], 1)
    GU[1, mine, :] = (hidden_grad * active).astype(BF16)
    spread(GU.at[1], 2)

    def row_grad(z):
        RG[group_rows(z), :] = (
            dot(GU[0, group_rows(z), :], weight(0), NT)
            + dot(GU[1, group_rows(z), :], weight(1), NT)
        ).astype(BF16)
        sources(RG, CB, 3, z)

    along([GU.at[0], GU.at[1]], 1, row_grad)
    x_gate = remote(GU.at[0], GUX.at[0], x_send.at[3], x_recv.at[3], sibling)
    x_up = remote(GU.at[1], GUX.at[1], x_send.at[4], x_recv.at[4], sibling)
    x_rows.wait_recv()
    x_gate.wait_recv()
    GRADS[0] = (dot(R[:, keep], GU[0], TN) + dot(RX[...], GUX[0], TN)) * factor
    put(0, GRADS.at[0], gg_out)
    x_up.wait_recv()
    GRADS[1] = (dot(R[:, keep], GU[1], TN) + dot(RX[...], GUX[1], TN)) * factor
    put(1, GRADS.at[1], ug_out)
    for k in order + [0]:
        arrived(3, k)
    put(3, CB, cb_out)

    for c in sent_w + [x_rows, x_hidden, x_grad, x_gate, x_up]:
        c.wait_send()
    for i in range(4):
        take(a_send.at[i], R.at[pl.ds(0, (peers - 1) * slots)])
    for i in range(3):
        take(p_send.at[i], PR.at[i])
    for i, buf in enumerate((H, GU.at[0], GU.at[1])):
        spread_sent(buf, i)
    for c in outs:
        c.wait()


def chain_kernel(
    planes, experts, slots, factor, pieces,
    index_in, count_in, gate_in, tokens, target, gw, uw, dw,
    cb_out, hot_out, gg_out, ug_out, dg_out,
    index, count, gate, r_loc, TOK, TGT, ROWS, TROWS, META, MT, W, R, TR, G, EOG,
    OWN, IN, OUT, HOWN, HIN, HOUT, H, GU, RG, CB, RX, GX, HX, GUX,
    t_loc, g_loc, w_loc, w_send, w_recv, a_send, a_recv, e_send, e_recv,
    c_send, c_recv, h_send, h_recv, x_send, x_recv,
):
    dp = lax.axis_index("dp")
    me_e = lax.axis_index("expert")
    me_z = dp // CORES
    core = dp % CORES
    peers = planes * experts
    per_group = experts * slots
    half = gw.shape[0]
    chunk = CORES * half
    ff = gw.shape[1]
    fw = ff // pieces
    split = HIN.shape[1] // planes
    hw = ff // split
    me = me_z * experts + me_e
    sibling = {"dp": me_z * CORES + (1 - core), "expert": me_e}
    ways = (1, -1)
    side = jnp.where(2 * me_z < planes, 1, -1)
    near_first = list(range(1, planes)) + [0]
    far_first = sorted(range(1, planes), key=lambda k: abs(k - planes / 2)) + [0]
    dist = (me_z, planes - 1 - me_z)
    depth = jnp.maximum(dist[0], dist[1])

    def at(z, e):
        return {"dp": z * CORES + core, "expert": e}

    def plane(k):
        return (me_z + side * k + planes) % planes

    def slot_rows(n):
        return pl.ds(pl.multiple_of(n * slots, slots), slots)

    def cols(z):
        return pl.ds(pl.multiple_of(z * chunk, chunk), chunk)

    def group_rows(z):
        return pl.ds(pl.multiple_of(z * per_group, per_group), per_group)

    def turn(g):
        if planes % 2:
            return g
        return planes // 2 - 1 - g // 2 + (g % 2) * (2 * (g // 2) + 1)

    barrier = pltpu.get_barrier_semaphore()

    def greet(k, carry):
        p = (me + k) % peers
        pl.semaphore_signal(
            barrier, inc=1, device_id=at(p // experts, p % experts),
            device_id_type=pl.DeviceIdType.MESH,
        )
        return carry

    lax.fori_loop(1, peers, greet, 0)
    pl.semaphore_signal(
        barrier, inc=1, device_id=sibling, device_id_type=pl.DeviceIdType.MESH
    )
    routes = [
        pltpu.make_async_copy(src, dst, r_loc.at[i])
        for i, (src, dst) in enumerate(
            ((index_in, index), (count_in, count), (gate_in, gate))
        )
    ]
    for c in routes:
        c.start()
    tok_copies = {}
    for k in far_first:
        tok_copies[k] = pltpu.make_async_copy(
            tokens.at[:, cols(plane(k))], TOK.at[:, cols(plane(k))], t_loc.at[k]
        )
        tok_copies[k].start()
    locals_w = []
    keep = pl.ds(pl.multiple_of(core * half, half), half)
    give = pl.ds(pl.multiple_of((1 - core) * half, half), half)
    for i, w in enumerate((gw, uw, dw)):
        c = pltpu.make_async_copy(w, W.at[i, keep], w_loc.at[i])
        c.start()
        locals_w.append(c)
    tgt_copy = pltpu.make_async_copy(target, TGT, g_loc)
    tgt_copy.start()

    for c in routes:
        c.wait()
    lane = lax.broadcasted_iota(jnp.int32, (slots, slots), 1)
    own_lane = lane == lax.broadcasted_iota(jnp.int32, (slots, slots), 0)
    slot_id = lax.broadcasted_iota(jnp.int32, (slots, 1), 0)
    names, weights = [], []
    for e in range(experts):
        live = slot_id < jnp.broadcast_to(count[0:1, e : e + 1], (slots, 1))
        ids = jnp.broadcast_to(index[0, e], (slots, slots))
        ids = jnp.sum(jnp.where(own_lane, ids, 0), axis=1, keepdims=True)
        names.append(jnp.where(live, ids, -1))
        g = jnp.broadcast_to(gate[0, e], (slots, slots))
        g = jnp.sum(jnp.where(own_lane, g, 0.0), axis=1, keepdims=True)
        weights.append(jnp.where(live, g, 0.0))
    names = jnp.concatenate(names, axis=0)
    wcol = jnp.concatenate(weights, axis=0)
    hot = (
        names == lax.broadcasted_iota(jnp.int32, (per_group, TOK.shape[0]), 1)
    ).astype(F32).astype(BF16)
    hot_out[...] = hot

    def remote(src, dst, s, r, dev):
        c = pltpu.make_async_remote_copy(
            src_ref=src, dst_ref=dst, send_sem=s, recv_sem=r,
            device_id=dev, device_id_type=pl.DeviceIdType.MESH,
        )
        c.start()
        return c

    def take(sem, ref):
        pltpu.make_async_copy(ref, ref, sem).wait()

    def to_plane(i, z, source, land):
        here = z == me_z

        @pl.when(here)
        def _():
            pltpu.make_async_copy(source(me_z, me_e), land, a_recv.at[i, me_z]).start()

        def send(j, carry):
            e = (me_e + j) % experts
            remote(source(z, e), land, a_send.at[i], a_recv.at[i, me_z], at(z, e))
            return carry

        lax.fori_loop(jnp.where(here, 1, 0), experts, send, 0)

    for k in far_first:
        z = plane(k)
        tok_copies[k].wait()
        ROWS[:, cols(z)] = dot(hot, TOK[:, cols(z)], NN).astype(BF16)
    for way, d in zip(ways, range(2)):
        @pl.when(dist[d] == 0)
        def _():
            IN[d] = jnp.zeros(IN.shape[1:], BF16)
            HIN[d] = jnp.zeros(HIN.shape[1:], BF16)

    with scope("barrier"):
        pl.semaphore_wait(barrier, peers)
    sent_w = [
        remote(w, W.at[i, keep], w_send.at[i], w_recv.at[i], sibling)
        for i, w in enumerate((gw, uw, dw))
    ]
    outer = depth == planes - 1

    def ordered(fn):
        for ours, ks in ((outer, near_first), (jnp.logical_not(outer), far_first)):
            @pl.when(ours)
            def _():
                for k in ks:
                    fn(plane(k))

    def send_tokens(z):
        to_plane(0, z, lambda z, e: ROWS.at[slot_rows(e), cols(z)], R.at[slot_rows(me)])

    if NEAR_TOKENS:
        ordered(send_tokens)
    else:
        for k in far_first:
            send_tokens(plane(k))
    with scope("trows"):
        tgt_copy.wait()
        for k in far_first:
            z = plane(k)
            TROWS[:, cols(z)] = dot(hot, TGT[:, cols(z)], NN).astype(BF16)
    with scope("meta"):
        square = (per_group, per_group)
        eye = lax.broadcasted_iota(jnp.int32, square, 0) == lax.broadcasted_iota(
            jnp.int32, square, 1
        )
        wrow = jnp.sum(jnp.where(eye, wcol, 0.0), axis=0, keepdims=True)
        mix = wcol * dot(hot, hot, NT) * wrow
        pad = (META.shape[1] - 256) // 2
        META[...] = jnp.zeros(META.shape, BF16)
        for part, start, stop in (
            (mix, 0, per_group), (jnp.broadcast_to(wcol, (per_group, 128)), 2 * pad, 2 * pad + 128)
        ):
            top = part.astype(BF16)
            step = pad if start == 0 else 128
            META[:, start:stop] = top
            META[:, start + step : stop + step] = (part - top.astype(F32)).astype(BF16)

    with scope("w_wait"):
        for i in range(3):
            locals_w[i].wait()
            sent_w[i].wait_recv()

    def piece(f):
        return pl.ds(pl.multiple_of(f * fw, fw), fw)

    def group_of(c):
        return turn(c // pieces)

    def rows_in(z):
        take(a_recv.at[0, z], R.at[pl.ds(0, per_group)])

    def partial_sums(c):
        z, f = group_of(c), c % pieces

        @pl.when(f == 0)
        def _():
            with scope("x_wait"):
                rows_in(z)

        with scope("own"):
            rows = R[group_rows(z), :]
            for i in range(2):
                OWN[c, :, i * fw : (i + 1) * fw] = dot(rows, W[i, :, piece(f)], NN)

    def move(own, inn, out, send, recv, d, c):
        @pl.when(dist[d] > 0)
        def _():
            with scope("mv%d" % (own is HOWN)):
                take(recv.at[d, c], inn.at[d, c])

        @pl.when(dist[d] < planes - 1)
        def _():
            out[d, c] = (own[c] + inn[d, c].astype(F32)).astype(BF16)
            remote(
                out.at[d, c], inn.at[d, c], send.at[d], recv.at[d, c],
                at(me_z + ways[d], me_e),
            )

    def total(own, inn, c):
        return own[c] + inn[0, c].astype(F32) + inn[1, c].astype(F32)

    def to_sibling(i, src, dst):
        remote(src, dst, x_send.at[i], x_recv.at[i], sibling)

    def forward(c):
        z, f = group_of(c), c % pieces
        with scope("fwd"):
            both = total(OWN, IN, c)
            OWN[c] = both
            pre, up = both[:, :fw], both[:, fw:]
            H[group_rows(z), piece(f)] = (pre * jax.nn.sigmoid(pre) * up).astype(BF16)

        @pl.when(f == pieces - 1)
        def _():
            with scope("eo"):
                EOG[z, me_e] = dot(H[group_rows(z), :], W[2], NT).astype(BF16)

                def send(j, carry):
                    remote(
                        EOG.at[z, me_e], EOG.at[z, me_e], e_send, e_recv.at[z],
                        at(me_z, (me_e + j) % experts),
                    )
                    return carry

                lax.fori_loop(1, experts, send, 0)
                to_sibling(1, H.at[group_rows(z)], HX.at[group_rows(z)])

    def slot_grads(g):
        z = turn(g)
        with scope("eo_wait"):
            take(e_recv.at[z], EOG.at[z, pl.ds(0, experts - 1)])
            take(a_recv.at[1, z], TR.at[pl.ds(0, per_group)])
            take(a_recv.at[2, z], MT.at[pl.ds(0, per_group)])
        with scope("comb"):
            for s in range(experts):
                its = slice(s * slots, (s + 1) * slots)
                mine = slot_rows(z * experts + s)
                outs = jnp.concatenate([EOG[z, e, its, :] for e in range(experts)], axis=0)
                wide = dot(MT[mine, 0:per_group], outs, NN) + dot(
                    MT[mine, pad : pad + per_group], outs, NN
                )
                w = MT[mine, 2 * pad : 2 * pad + 1].astype(F32) + MT[
                    mine, 2 * pad + 128 : 2 * pad + 129
                ].astype(F32)
                G[mine, :] = (wide - w * TR[mine, :].astype(F32)).astype(BF16)
            for i in range(split):
                HOWN[g * split + i] = dot(
                    G[group_rows(z), :], W[2, :, i * hw : (i + 1) * hw], NN
                )
            to_sibling(2, G.at[group_rows(z), give], GX.at[group_rows(z)])

    def backward(g):
        z = turn(g)
        rows = group_rows(z)
        with scope("bwd"):
            hidden_grad = jnp.concatenate(
                [total(HOWN, HIN, g * split + i) for i in range(split)], axis=1
            )
            for f in range(pieces):
                both = OWN[g * pieces + f]
                pre, up = both[:, :fw], both[:, fw:]
                grad = hidden_grad[:, f * fw : (f + 1) * fw]
                sigma = jax.nn.sigmoid(pre)
                GU[0, rows, f * fw : (f + 1) * fw] = (
                    grad * up * sigma * (1.0 + pre * (1.0 - sigma))
                ).astype(BF16)
                GU[1, rows, f * fw : (f + 1) * fw] = (grad * (pre * sigma)).astype(BF16)
            RG[rows, :] = (
                dot(GU[0, rows, :], W[0], NT) + dot(GU[1, rows, :], W[1], NT)
            ).astype(BF16)
            for i in range(2):
                to_sibling(3 + i, GU.at[i, rows], GUX.at[i, rows])

    def send_rows(g):
        to_plane(
            3, turn(g), lambda z, e: RG.at[slot_rows(z * experts + e)],
            CB.at[slot_rows(me_e), cols(me_z)],
        )

    steps = planes * pieces
    back_steps = planes * split
    begin = pieces - 1 + LAG * (planes - 1) + LAG_PLANE

    def each(t, fn, last):
        @pl.when(jnp.logical_and(t >= 0, t < last))
        def _():
            fn(t)

    def each_group(t, fn):
        fits = jnp.logical_and(t >= 0, t < back_steps)

        @pl.when(jnp.logical_and(fits, t % split == 0))
        def _():
            fn(t // split)

    def grad(i, left, left_x, right, right_x, out):
        out[...] = (dot(left, right, TN) + dot(left_x, right_x, TN)) * factor

    def send_targets(z):
        to_plane(2, z, lambda z, e: META.at[slot_rows(e)], MT.at[slot_rows(me)])
        to_plane(
            1, z, lambda z, e: TROWS.at[slot_rows(e), cols(z)], TR.at[slot_rows(me)]
        )

    rank = jnp.maximum(planes // 2 - 1 - me_z, me_z - planes // 2)
    target_at = TARGET_AT + TARGET_STEP * rank

    def targets():
        if NEAR_TARGETS:
            ordered(send_targets)
        else:
            for k in far_first:
                send_targets(plane(k))

    @pl.when(target_at < 0)
    def _():
        targets()

    def tick(t, carry):
        @pl.when(t == target_at)
        def _():
            targets()

        each(t, partial_sums, steps)
        for d in range(2):
            each(
                t - LAG * dist[d],
                functools.partial(move, OWN, IN, OUT, c_send, c_recv, d), steps,
            )
        each(t - LAG * depth, forward, steps)
        t = t - begin
        each_group(t, slot_grads)
        for d in range(2):
            each(
                t - LAG_BACK * dist[d],
                functools.partial(move, HOWN, HIN, HOUT, h_send, h_recv, d), back_steps,
            )
        back = t - LAG_BACK * depth - (split - 1)
        each_group(back, backward)
        each_group(back - LAG_ROWS, send_rows)
        return carry

    middle = begin + back_steps + 1
    lax.fori_loop(0, middle, tick, 0)
    to_sibling(0, R.at[:, give], RX)
    with scope("dgrad"):
        take(x_recv.at[1], HX)
        take(x_recv.at[2], GX)
        grad(2, G[:, keep], GX[...], H[...], HX[...], dg_out)
    lax.fori_loop(
        middle, begin + back_steps + LAG_BACK * (planes - 1) + LAG_ROWS + split, tick, 0
    )
    with scope("xg"):
        take(x_recv.at[0], RX)
        take(x_recv.at[3], GUX.at[0])
        take(x_recv.at[4], GUX.at[1])
    with scope("gugrad"):
        grad(0, R[:, keep], RX[...], GU[0], GUX[0], gg_out)
        grad(1, R[:, keep], RX[...], GU[1], GUX[1], ug_out)
    with scope("cb_wait"):
        for k in far_first:
            take(a_recv.at[3, plane(k)], R.at[pl.ds(0, per_group)])
    with scope("tail"):
        cb_out[...] = CB[...]
        for c in sent_w:
            c.wait_send()
        others = pl.ds(0, (peers - 1) * slots)
        for i, buf in enumerate((R, TR, MT, RG)):
            take(a_send.at[i], buf.at[others])
        take(e_send, EOG.at[:, pl.ds(0, experts - 1)])
        for d in range(2):
            @pl.when(dist[d] < planes - 1)
            def _():
                take(c_send.at[d], OUT.at[d])
                take(h_send.at[d], HOUT.at[d])
        for i, buf in enumerate((RX, HX, GX, GUX.at[0], GUX.at[1])):
            take(x_send.at[i], buf)


def finish(hot, cb, gg, ug, dg, tg_out, gg_out, ug_out, dg_out, TG, t_sem, g_sem):
    copies = []
    for i, (grad, out) in enumerate(((gg, gg_out), (ug, ug_out), (dg, dg_out))):
        copies.append(pltpu.make_async_copy(grad, out.at[:, 0, :], g_sem.at[i]))
        copies[-1].start()
    parts = t_sem.shape[0]
    step = TG.shape[0] // parts
    for j in range(parts):
        rows = slice(j * step, (j + 1) * step)
        TG[rows, :] = dot(hot[:, rows], cb[...], TN).astype(BF16)
        copies.append(pltpu.make_async_copy(TG.at[rows], tg_out.at[rows], t_sem.at[j]))
        copies[-1].start()
    for c in copies:
        c.wait()


def direct_scratch(planes, picked, count, width, half, ff):
    chunk = CORES * half
    all_rows = planes * picked
    dma = pltpu.SemaphoreType.DMA
    return [
        pltpu.VMEM((count, width), BF16),
        pltpu.VMEM((count, width), BF16),
        pltpu.VMEM((picked, width), BF16),
        pltpu.VMEM((picked, width), F32),
        pltpu.VMEM((3, CORES, half, ff), BF16),
        pltpu.VMEM((all_rows, chunk), BF16),
        pltpu.VMEM((all_rows, chunk), BF16),
        pltpu.VMEM((picked, width), BF16),
        pltpu.VMEM((picked, width), BF16),
        pltpu.VMEM((all_rows, chunk), BF16),
        pltpu.VMEM((all_rows, chunk), BF16),
        pltpu.VMEM((picked, width), BF16),
        pltpu.VMEM((3, all_rows, ff), BF16),
        pltpu.VMEM((3, planes - 1, picked, ff), BF16),
        pltpu.VMEM((all_rows, ff), BF16),
        pltpu.VMEM((2, all_rows, ff), BF16),
        pltpu.VMEM((all_rows, half), BF16),
        pltpu.VMEM((all_rows, half), BF16),
        pltpu.VMEM((all_rows, ff), BF16),
        pltpu.VMEM((2, all_rows, ff), BF16),
        dma((planes,)), dma,
        dma((3,)), dma((3,)), dma((3,)),
        dma((4,)), dma((4,)), dma((4, planes)),
        dma((3,)), dma((3, planes)),
        dma((3, 2, planes)), dma((3, planes)),
        dma((5,)), dma((5,)),
        pltpu.VMEM((3, half, ff), F32), dma((4,)),
    ]


def chain_scratch(planes, experts, picked, count, width, half, ff, pieces, split):
    slots = picked // experts
    chunk = CORES * half
    all_rows = planes * picked
    steps = planes * pieces
    fw = ff // pieces
    table = 2 * (-(-picked // 128) * 128) + 256
    dma = pltpu.SemaphoreType.DMA
    return [
        pltpu.VMEM((1, experts, 1, slots), jnp.int32),
        pltpu.VMEM((1, experts), jnp.int32),
        pltpu.VMEM((1, experts, 1, slots), F32),
        dma((3,)),
        pltpu.VMEM((count, width), BF16),
        pltpu.VMEM((count, width), BF16),
        pltpu.VMEM((picked, width), BF16),
        pltpu.VMEM((picked, width), BF16),
        pltpu.VMEM((picked, table), BF16),
        pltpu.VMEM((all_rows, table), BF16),
        pltpu.VMEM((3, chunk, ff), BF16),
        pltpu.VMEM((all_rows, chunk), BF16),
        pltpu.VMEM((all_rows, chunk), BF16),
        pltpu.VMEM((all_rows, chunk), BF16),
        pltpu.VMEM((planes, experts, picked, chunk), BF16),
        pltpu.VMEM((steps, picked, 2 * fw), F32),
        pltpu.VMEM((2, steps, picked, 2 * fw), BF16),
        pltpu.VMEM((2, steps, picked, 2 * fw), BF16),
        pltpu.VMEM((planes * split, picked, ff // split), F32),
        pltpu.VMEM((2, planes * split, picked, ff // split), BF16),
        pltpu.VMEM((2, planes * split, picked, ff // split), BF16),
        pltpu.VMEM((all_rows, ff), BF16),
        pltpu.VMEM((2, all_rows, ff), BF16),
        pltpu.VMEM((all_rows, chunk), BF16),
        pltpu.VMEM((picked, width), BF16),
        pltpu.VMEM((all_rows, half), BF16),
        pltpu.VMEM((all_rows, half), BF16),
        pltpu.VMEM((all_rows, ff), BF16),
        pltpu.VMEM((2, all_rows, ff), BF16),
        dma((planes,)), dma, dma((3,)), dma((3,)), dma((3,)),
        dma((4,)), dma((4, planes)), dma, dma((planes,)),
        dma((2,)), dma((2, steps)), dma((2,)), dma((2, planes * split)),
        dma((5,)), dma((5,)),
    ]


def held_bytes(scratch):
    return sum(
        math.prod(s.shape) * jnp.dtype(s.dtype).itemsize
        for s in scratch
        if getattr(s, "memory_space", None) == pltpu.VMEM
    )


def on_device(
    tokens, target, route_index, route_count, route_gate, gate_weight, up_weight, down_weight
):
    groups = lax.axis_size("dp")
    experts = lax.axis_size("expert")
    planes = groups // CORES
    slots = route_index.shape[3]
    count, width = tokens.shape
    half, _, ff = gate_weight.shape
    picked = experts * slots
    factor = (groups * experts * slots) ** (-0.5)
    pieces, split = (
        max(n for n in range(1, most + 1) if ff % (128 * n) == 0)
        for most in (PIECES, BACK_PIECES)
    )
    vmem = pl.BlockSpec(memory_space=pltpu.VMEM)
    anyw = pl.BlockSpec(memory_space=pl.ANY)
    grad = jax.ShapeDtypeStruct((half, ff), F32)
    scratch = chain_scratch(planes, experts, picked, count, width, half, ff, pieces, split)
    body = functools.partial(chain_kernel, planes, experts, slots, factor, pieces)
    out, limit, small = vmem, CHAIN_LIMIT, anyw
    if held_bytes(scratch) > CHAIN_LIMIT * 3 // 4:
        scratch = direct_scratch(planes, picked, count, width, half, ff)
        body = functools.partial(direct_kernel, planes, experts, slots, factor)
        out, limit, small = anyw, VMEM_LIMIT, vmem
    came_back, hot, gate_gradient, up_gradient, down_gradient = pl.pallas_call(
        body,
        out_shape=(
            jax.ShapeDtypeStruct((picked, width), BF16),
            jax.ShapeDtypeStruct((picked, count), BF16),
            grad, grad, grad,
        ),
        in_specs=[small] * 3 + [anyw] * 5,
        out_specs=(out, vmem, out, out, out),
        scratch_shapes=scratch,
        compiler_params=pltpu.CompilerParams(
            collective_id=0, has_side_effects=True, vmem_limit_bytes=limit
        ),
        name="routed_layer",
    )(
        *(
            pltpu.with_memory_space_constraint(x, pltpu.MemorySpace.HBM)
            for x in (
                route_index, route_count.reshape(1, experts), route_gate, tokens, target, gate_weight.reshape(half, ff), up_weight.reshape(half, ff),
                down_weight.reshape(half, ff),
            )
        ),
    )
    parts = max(n for n in range(1, 9) if count % (128 * n) == 0)
    grad = jax.ShapeDtypeStruct((half, 1, ff), F32)
    return tuple(pl.pallas_call(
        finish,
        out_shape=(jax.ShapeDtypeStruct((count, width), BF16), grad, grad, grad),
        in_specs=[vmem] * 5,
        out_specs=[anyw] * 4,
        scratch_shapes=[
            pltpu.VMEM((count, width), BF16),
            pltpu.SemaphoreType.DMA((parts,)), pltpu.SemaphoreType.DMA((3,)),
        ],
        compiler_params=pltpu.CompilerParams(vmem_limit_bytes=FINISH_LIMIT),
        name="finish",
    )(hot, came_back, gate_gradient, up_gradient, down_gradient))


def solution(mesh):
    return jax.shard_map(
        on_device,
        mesh=mesh,
        in_specs=(
            P(("dp", "expert"), None),
            P(("dp", "expert"), None),
            P("dp", None, "expert", None),
            P("dp", None, "expert"),
            P("dp", None, "expert", None),
            P("dp", "expert", None),
            P("dp", "expert", None),
            P("dp", "expert", None),
        ),
        out_specs=(
            P(("dp", "expert"), None),
            P("dp", "expert", None),
            P("dp", "expert", None),
            P("dp", "expert", None),
        ),
        check_vma=False,
    )
```

```python
import contextlib
import functools
import math

import jax
import jax.numpy as jnp
from jax import lax
from jax.experimental import pallas as pl
from jax.experimental.pallas import tpu as pltpu
from jax.sharding import PartitionSpec as P

F32 = jnp.float32
BF16 = jnp.bfloat16
VMEM_LIMIT = 67000000
CORES = 2
PIECES = 3
BACK_PIECES = 3
PARTS = 2
LAG = 5
LAG_PLANE = 6
LAG_BACK = 6
LAG_GRADS = 0
LATE = True
TURNS = (1, 0)
OUTER_FIRST = True
CHAIN_LIMIT = 44000000
FINISH_LIMIT = 40000000


def dot(a, b, dims, precision=None):
    return lax.dot_general(
        a, b, (dims, ((), ())), preferred_element_type=F32, precision=precision
    )


def scope(name):
    return contextlib.nullcontext()


NN = ((1,), (0,))
NT = ((1,), (1,))
TN = ((0,), (0,))


def direct_kernel(
    planes, experts, slots, factor,
    index, count, gate, tokens, target, gw, uw, dw,
    cb_out, hot_out, gg_out, ug_out, dg_out,
    TOK, TGT, ROWS, TROWS, W, R, EO, RET, SG, G, RG, CB, PS, PR, H, GU, RX, GX, HX, GUX,
    t_loc, g_loc, w_loc, w_send, w_recv, a_loc, a_send, a_recv, p_send, p_recv,
    h_send, h_recv, x_send, x_recv, GRADS, o_loc,
):
    dp = lax.axis_index("dp")
    me_e = lax.axis_index("expert")
    me_z = dp // CORES
    core = dp % CORES
    peers = planes * experts
    per_group = experts * slots
    half = gw.shape[0]
    chunk = CORES * half
    ff = gw.shape[1]
    me = me_z * experts + me_e
    sibling = {"dp": me_z * CORES + (1 - core), "expert": me_e}
    order = sorted(range(1, planes), key=lambda k: -min(k, planes - k))

    def at(z, e):
        return {"dp": z * CORES + core, "expert": e}

    def plane(k):
        return (me_z + k) % planes

    def slot_rows(n):
        return pl.ds(pl.multiple_of(n * slots, slots), slots)

    def cols(z):
        return pl.ds(pl.multiple_of(z * chunk, chunk), chunk)

    def group_rows(z):
        return pl.ds(pl.multiple_of(z * per_group, per_group), per_group)

    barrier = pltpu.get_barrier_semaphore()

    def greet(k, carry):
        p = (me + k) % peers
        pl.semaphore_signal(
            barrier, inc=1, device_id=at(p // experts, p % experts),
            device_id_type=pl.DeviceIdType.MESH,
        )
        return carry

    lax.fori_loop(1, peers, greet, 0)
    pl.semaphore_signal(
        barrier, inc=1, device_id=sibling, device_id_type=pl.DeviceIdType.MESH
    )
    tok_copies = {}
    for k in order + [0]:
        z = plane(k)
        tok_copies[k] = pltpu.make_async_copy(
            tokens.at[:, cols(z)], TOK.at[:, cols(z)], t_loc.at[k]
        )
        tok_copies[k].start()
    locals_w = []
    for i, w in enumerate((gw, uw, dw)):
        c = pltpu.make_async_copy(w, W.at[i, core], w_loc.at[i])
        c.start()
        locals_w.append(c)
    tgt_copy = pltpu.make_async_copy(target, TGT, g_loc)
    tgt_copy.start()

    lane = lax.broadcasted_iota(jnp.int32, (slots, slots), 1)
    own_lane = lane == lax.broadcasted_iota(jnp.int32, (slots, slots), 0)
    slot_id = lax.broadcasted_iota(jnp.int32, (slots, 1), 0)
    names, weights = [], []
    for e in range(experts):
        live = slot_id < jnp.broadcast_to(count[0:1, e : e + 1], (slots, 1))
        ids = jnp.broadcast_to(index[0, e], (slots, slots))
        ids = jnp.sum(jnp.where(own_lane, ids, 0), axis=1, keepdims=True)
        names.append(jnp.where(live, ids, -1))
        g = jnp.broadcast_to(gate[0, e], (slots, slots))
        g = jnp.sum(jnp.where(own_lane, g, 0.0), axis=1, keepdims=True)
        weights.append(jnp.where(live, g, 0.0))
    names = jnp.concatenate(names, axis=0)
    wcol = jnp.concatenate(weights, axis=0)
    hot = (
        names == lax.broadcasted_iota(jnp.int32, (per_group, TOK.shape[0]), 1)
    ).astype(F32).astype(BF16)
    hot_out[...] = hot

    def remote(src, dst, s, r, dev):
        c = pltpu.make_async_remote_copy(
            src_ref=src, dst_ref=dst, send_sem=s, recv_sem=r,
            device_id=dev, device_id_type=pl.DeviceIdType.MESH,
        )
        c.start()
        return c

    def to_plane(i, z, source, land):
        here = z == me_z

        @pl.when(here)
        def _():
            pltpu.make_async_copy(source(me_z, me_e), land, a_loc.at[i]).start()

        first = jnp.where(here, 1, 0)

        def send(j, carry):
            e = (me_e + j) % experts
            remote(source(z, e), land, a_send.at[i], a_recv.at[i, me_z], at(z, e))
            return carry

        lax.fori_loop(first, experts, send, 0)

    def owners(src, dst, i, z):
        to_plane(i, z, lambda z, e: src.at[slot_rows(e), cols(z)], dst.at[slot_rows(me)])

    def sources(src, dst, i, z):
        to_plane(
            i, z, lambda z, e: src.at[slot_rows(z * experts + e)],
            dst.at[slot_rows(me_e), cols(me_z)],
        )

    def take(sem, ref):
        pltpu.make_async_copy(ref, ref, sem).wait()

    def arrived(i, k):
        if k == 0:
            take(a_recv.at[i, me_z], R.at[pl.ds(0, (experts - 1) * slots)])
            take(a_loc.at[i], R.at[pl.ds(0, slots)])
        else:
            take(a_recv.at[i, plane(k)], R.at[pl.ds(0, per_group)])

    outs = []

    def put(i, src, dst):
        c = pltpu.make_async_copy(src, dst, o_loc.at[i])
        c.start()
        outs.append(c)

    def weight(i):
        return W[i].reshape(chunk, ff)

    pl.semaphore_wait(barrier, peers)
    for k in order + [0]:
        z = plane(k)
        tok_copies[k].wait()
        ROWS[:, cols(z)] = dot(hot, TOK[:, cols(z)], NN).astype(BF16)
        owners(ROWS, R, 0, z)
    sent_w = [
        remote(w, W.at[i, core], w_send.at[i], w_recv.at[i], sibling)
        for i, w in enumerate((gw, uw, dw))
    ]

    def send_sum(i, k):
        remote(
            PS.at[i, group_rows(plane(k))], PR.at[i, k - 1],
            p_send.at[i], p_recv.at[i, k - 1], at(plane(k), me_e),
        )

    def pass_on(buf, i, s, way):
        to = me_z + way

        @pl.when(jnp.logical_and(to >= 0, to < planes))
        def _():
            rows_s = buf.at[group_rows(s)]
            remote(
                rows_s, rows_s, h_send.at[i, (way + 1) // 2, s], h_recv.at[i, s],
                at(to, me_e),
            )

    def spread(buf, i):
        for way in (1, -1):
            pass_on(buf, i, me_z, way)

    def along(bufs, first, fn):
        fn(me_z)
        for far in range(1, planes):
            for way in (1, -1):
                s = me_z - way * far

                @pl.when(jnp.logical_and(s >= 0, s < planes))
                def _():
                    for j, buf in enumerate(bufs):
                        take(h_recv.at[first + j, s], buf.at[group_rows(s)])
                        pass_on(buf, first + j, s, way)
                    fn(s)

    def spread_sent(buf, i):
        for s in range(planes):
            rows_s = buf.at[pl.ds(s * per_group, per_group)]

            @pl.when(jnp.logical_and(me_z > 0, me_z <= s))
            def _():
                take(h_send.at[i, 0, s], rows_s)

            @pl.when(jnp.logical_and(me_z < planes - 1, me_z >= s))
            def _():
                take(h_send.at[i, 1, s], rows_s)

    def total(i, own):
        for k in order:
            take(p_recv.at[i, k - 1], PR.at[i, k - 1])
            own = own + PR[i, k - 1].astype(F32)
        return own

    keep = pl.ds(pl.multiple_of(core * half, half), half)
    give = pl.ds(pl.multiple_of((1 - core) * half, half), half)
    mine = group_rows(me_z)

    for i in range(2):
        locals_w[i].wait()
        sent_w[i].wait_recv()
    for k in order:
        z = plane(k)
        arrived(0, k)
        for i in range(2):
            PS[i, group_rows(z), :] = dot(R[group_rows(z), :], weight(i), NN).astype(BF16)
            send_sum(i, k)
    arrived(0, 0)
    gate_own = dot(R[mine, :], weight(0), NN)
    up_own = dot(R[mine, :], weight(1), NN)
    x_rows = remote(R.at[:, give], RX, x_send.at[0], x_recv.at[0], sibling)
    tgt_copy.wait()
    for z in range(planes):
        piece = slice(z * chunk, (z + 1) * chunk)
        TROWS[:, piece] = dot(hot, TGT[:, piece], NN)
    same = dot(hot, hot, NT).astype(BF16)
    gate_pre = total(0, gate_own)
    up_pre = total(1, up_own)
    sigma = jax.nn.sigmoid(gate_pre)
    active = gate_pre * sigma
    H[mine, :] = (active * up_pre).astype(BF16)
    spread(H, 0)
    locals_w[2].wait()
    sent_w[2].wait_recv()

    def expert_out(z):
        EO[group_rows(z), :] = dot(H[group_rows(z), :], weight(2), NT).astype(BF16)
        sources(EO, RET, 1, z)

    along([H], 0, expert_out)
    x_hidden = remote(H, HX, x_send.at[1], x_recv.at[1], sibling)
    for k in order + [0]:
        z = plane(k)
        arrived(1, k)
        part = wcol * RET[:, cols(z)].astype(F32)
        combined = -TROWS[:, cols(z)]
        for _ in range(3):
            top = part.astype(BF16)
            combined = combined + dot(same, top, NN)
            part = part - top.astype(F32)
        SG[:, cols(z)] = (wcol * combined).astype(BF16)
        owners(SG, G, 2, z)

    for k in order:
        z = plane(k)
        arrived(2, k)
        PS[2, group_rows(z), :] = dot(G[group_rows(z), :], weight(2), NN).astype(BF16)
        send_sum(2, k)
    arrived(2, 0)
    own = dot(G[mine, :], weight(2), NN)
    x_grad = remote(G.at[:, give], GX, x_send.at[2], x_recv.at[2], sibling)
    x_hidden.wait_recv()
    x_grad.wait_recv()
    GRADS[2] = (dot(G[:, keep], H[...], TN) + dot(GX[...], HX[...], TN)) * factor
    put(2, GRADS.at[2], dg_out)
    hidden_grad = total(2, own)
    GU[0, mine, :] = (
        hidden_grad * up_pre * sigma * (1.0 + gate_pre * (1.0 - sigma))
    ).astype(BF16)
    spread(GU.at[0], 1)
    GU[1, mine, :] = (hidden_grad * active).astype(BF16)
    spread(GU.at[1], 2)

    def row_grad(z):
        RG[group_rows(z), :] = (
            dot(GU[0, group_rows(z), :], weight(0), NT)
            + dot(GU[1, group_rows(z), :], weight(1), NT)
        ).astype(BF16)
        sources(RG, CB, 3, z)

    along([GU.at[0], GU.at[1]], 1, row_grad)
    x_gate = remote(GU.at[0], GUX.at[0], x_send.at[3], x_recv.at[3], sibling)
    x_up = remote(GU.at[1], GUX.at[1], x_send.at[4], x_recv.at[4], sibling)
    x_rows.wait_recv()
    x_gate.wait_recv()
    GRADS[0] = (dot(R[:, keep], GU[0], TN) + dot(RX[...], GUX[0], TN)) * factor
    put(0, GRADS.at[0], gg_out)
    x_up.wait_recv()
    GRADS[1] = (dot(R[:, keep], GU[1], TN) + dot(RX[...], GUX[1], TN)) * factor
    put(1, GRADS.at[1], ug_out)
    for k in order + [0]:
        arrived(3, k)
    put(3, CB, cb_out)

    for c in sent_w + [x_rows, x_hidden, x_grad, x_gate, x_up]:
        c.wait_send()
    for i in range(4):
        take(a_send.at[i], R.at[pl.ds(0, (peers - 1) * slots)])
    for i in range(3):
        take(p_send.at[i], PR.at[i])
    for i, buf in enumerate((H, GU.at[0], GU.at[1])):
        spread_sent(buf, i)
    for c in outs:
        c.wait()


def chain_kernel(
    planes, experts, slots, factor, pieces, parts,
    index_in, count_in, gate_in, tokens, target, gw, uw, dw,
    cb_out, hot_out, gg_out, ug_out, dg_out,
    index, count, gate, r_loc, TOK, TGT, ROWS, TROWS, META, MT, W, R, TR, G, EOG,
    OWN, IN, OUT, HOWN, HIN, HOUT, H, GU, RG, CB, RX, GX, HX, GUX,
    t_loc, g_loc, w_loc, w_send, w_recv, a_send, a_recv, e_send, e_recv,
    c_send, c_recv, h_send, h_recv, x_send, x_recv,
):
    dp = lax.axis_index("dp")
    me_e = lax.axis_index("expert")
    me_z = dp // CORES
    core = dp % CORES
    peers = planes * experts
    per_group = experts * slots
    half = gw.shape[0]
    chunk = CORES * half
    ff = gw.shape[1]
    fw = ff // pieces
    split = HIN.shape[1] // (planes * parts)
    unit = per_group // parts
    hw = ff // split
    me = me_z * experts + me_e
    sibling = {"dp": me_z * CORES + (1 - core), "expert": me_e}
    ways = (1, -1)
    side = jnp.where(2 * me_z < planes, 1, -1)
    far_first = sorted(range(1, planes), key=lambda k: abs(k - planes / 2)) + [0]
    dist = (me_z, planes - 1 - me_z)
    depth = jnp.maximum(dist[0], dist[1])

    def at(z, e):
        return {"dp": z * CORES + core, "expert": e}

    def plane(k):
        return (me_z + side * k + planes) % planes

    def slot_rows(n):
        return pl.ds(pl.multiple_of(n * slots, slots), slots)

    def cols(z):
        return pl.ds(pl.multiple_of(z * chunk, chunk), chunk)

    def group_rows(z):
        return pl.ds(pl.multiple_of(z * per_group, per_group), per_group)

    def unit_rows(n):
        rows = turn(n // parts) * per_group + n % parts * unit
        return pl.ds(pl.multiple_of(rows, unit), unit)

    def turn(g):
        if planes % 2:
            return g
        g = planes - 1 - g if OUTER_FIRST else g
        return planes // 2 - 1 - g // 2 + (g % 2) * (2 * (g // 2) + 1)

    barrier = pltpu.get_barrier_semaphore()

    def greet(k, carry):
        p = (me + k) % peers
        pl.semaphore_signal(
            barrier, inc=1, device_id=at(p // experts, p % experts),
            device_id_type=pl.DeviceIdType.MESH,
        )
        return carry

    lax.fori_loop(1, peers, greet, 0)
    pl.semaphore_signal(
        barrier, inc=1, device_id=sibling, device_id_type=pl.DeviceIdType.MESH
    )
    routes = [
        pltpu.make_async_copy(src, dst, r_loc.at[i])
        for i, (src, dst) in enumerate(
            ((index_in, index), (count_in, count), (gate_in, gate))
        )
    ]
    for c in routes:
        c.start()
    tok_copies = {}
    for k in far_first:
        tok_copies[k] = pltpu.make_async_copy(
            tokens.at[:, cols(plane(k))], TOK.at[:, cols(plane(k))], t_loc.at[k]
        )
        tok_copies[k].start()
    locals_w = []
    keep = pl.ds(pl.multiple_of(core * half, half), half)
    give = pl.ds(pl.multiple_of((1 - core) * half, half), half)
    for i, w in enumerate((gw, uw, dw)):
        c = pltpu.make_async_copy(w, W.at[i, keep], w_loc.at[i])
        c.start()
        locals_w.append(c)
    tgt_copy = pltpu.make_async_copy(target, TGT, g_loc)
    tgt_copy.start()

    for c in routes:
        c.wait()
    lane = lax.broadcasted_iota(jnp.int32, (slots, slots), 1)
    own_lane = lane == lax.broadcasted_iota(jnp.int32, (slots, slots), 0)
    slot_id = lax.broadcasted_iota(jnp.int32, (slots, 1), 0)
    names, weights = [], []
    for e in range(experts):
        live = slot_id < jnp.broadcast_to(count[0:1, e : e + 1], (slots, 1))
        ids = jnp.broadcast_to(index[0, e], (slots, slots))
        ids = jnp.sum(jnp.where(own_lane, ids, 0), axis=1, keepdims=True)
        names.append(jnp.where(live, ids, -1))
        g = jnp.broadcast_to(gate[0, e], (slots, slots))
        g = jnp.sum(jnp.where(own_lane, g, 0.0), axis=1, keepdims=True)
        weights.append(jnp.where(live, g, 0.0))
    names = jnp.concatenate(names, axis=0)
    wcol = jnp.concatenate(weights, axis=0)
    hot = (
        names == lax.broadcasted_iota(jnp.int32, (per_group, TOK.shape[0]), 1)
    ).astype(F32).astype(BF16)
    hot_out[...] = hot

    def remote(src, dst, s, r, dev):
        c = pltpu.make_async_remote_copy(
            src_ref=src, dst_ref=dst, send_sem=s, recv_sem=r,
            device_id=dev, device_id_type=pl.DeviceIdType.MESH,
        )
        c.start()
        return c

    def take(sem, ref):
        pltpu.make_async_copy(ref, ref, sem).wait()

    def to_plane(i, z, source, land):
        here = z == me_z

        @pl.when(here)
        def _():
            pltpu.make_async_copy(source(me_z, me_e), land, a_recv.at[i, me_z]).start()

        def send(j, carry):
            e = (me_e + j) % experts
            remote(source(z, e), land, a_send.at[i], a_recv.at[i, me_z], at(z, e))
            return carry

        lax.fori_loop(jnp.where(here, 1, 0), experts, send, 0)

    for k in far_first:
        z = plane(k)
        tok_copies[k].wait()
        ROWS[:, cols(z)] = dot(hot, TOK[:, cols(z)], NN).astype(BF16)
    for way, d in zip(ways, range(2)):
        @pl.when(dist[d] == 0)
        def _():
            IN[d] = jnp.zeros(IN.shape[1:], BF16)
            HIN[d] = jnp.zeros(HIN.shape[1:], BF16)

    with scope("barrier"):
        pl.semaphore_wait(barrier, peers)
    sent_w = [
        remote(w, W.at[i, keep], w_send.at[i], w_recv.at[i], sibling)
        for i, w in enumerate((gw, uw, dw))
    ]
    for k in far_first:
        to_plane(
            0, plane(k), lambda z, e: ROWS.at[slot_rows(e), cols(z)], R.at[slot_rows(me)]
        )
    with scope("trows"):
        tgt_copy.wait()
        for k in far_first:
            z = plane(k)
            TROWS[:, cols(z)] = dot(hot, TGT[:, cols(z)], NN).astype(BF16)
    with scope("meta"):
        square = (per_group, per_group)
        eye = lax.broadcasted_iota(jnp.int32, square, 0) == lax.broadcasted_iota(
            jnp.int32, square, 1
        )
        wrow = jnp.sum(jnp.where(eye, wcol, 0.0), axis=0, keepdims=True)
        mix = wcol * dot(hot, hot, NT) * wrow
        pad = (META.shape[1] - 256) // 2
        META[...] = jnp.zeros(META.shape, BF16)
        for part, start, stop in (
            (mix, 0, per_group), (jnp.broadcast_to(wcol, (per_group, 128)), 2 * pad, 2 * pad + 128)
        ):
            top = part.astype(BF16)
            step = pad if start == 0 else 128
            META[:, start:stop] = top
            META[:, start + step : stop + step] = (part - top.astype(F32)).astype(BF16)

    with scope("w_wait"):
        for i in range(3):
            locals_w[i].wait()
            sent_w[i].wait_recv()

    def piece(f):
        return pl.ds(pl.multiple_of(f * fw, fw), fw)

    def partial_sums(c):
        n, f = c // pieces, c % pieces

        @pl.when(c % (pieces * parts) == 0)
        def _():
            with scope("x_wait"):
                take(a_recv.at[0, turn(n // parts)], R.at[pl.ds(0, per_group)])

        with scope("own"):
            rows = R[unit_rows(n), :]
            for i in range(2):
                OWN[c, :, i * fw : (i + 1) * fw] = dot(rows, W[i, :, piece(f)], NN)

    def move(own, inn, out, send, recv, d, c):
        @pl.when(dist[d] > 0)
        def _():
            with scope("mv%d" % (own is HOWN)):
                take(recv.at[d, c], inn.at[d, c])

        @pl.when(dist[d] < planes - 1)
        def _():
            out[d, c] = (own[c] + inn[d, c].astype(F32)).astype(BF16)
            remote(
                out.at[d, c], inn.at[d, c], send.at[d], recv.at[d, c],
                at(me_z + ways[d], me_e),
            )

    def total(own, inn, c):
        return own[c] + inn[0, c].astype(F32) + inn[1, c].astype(F32)

    def to_sibling(i, src, dst):
        remote(src, dst, x_send.at[i], x_recv.at[i], sibling)

    def forward(c):
        n, f = c // pieces, c % pieces
        rows = unit_rows(n)
        with scope("fwd"):
            both = total(OWN, IN, c)
            OWN[c] = both
            pre, up = both[:, :fw], both[:, fw:]
            H[rows, piece(f)] = (pre * jax.nn.sigmoid(pre) * up).astype(BF16)

        @pl.when(f == pieces - 1)
        def _():
            with scope("eo"):
                EOG[me_e, rows, :] = dot(H[rows, :], W[2], NT).astype(BF16)
                outs = EOG.at[me_e, rows]

                def send(j, carry):
                    remote(
                        outs, outs, e_send, e_recv.at[n], at(me_z, (me_e + j) % experts)
                    )
                    return carry

                lax.fori_loop(1, experts, send, 0)
                to_sibling(1, H.at[rows], HX.at[rows])

    def slot_grads(n):
        z = turn(n // parts)
        rows = unit_rows(n)
        with scope("eo_wait"):
            take(e_recv.at[n], EOG.at[pl.ds(0, experts - 1), pl.ds(0, unit)])

            @pl.when(n % parts == 0)
            def _():
                take(a_recv.at[1, z], TR.at[pl.ds(0, per_group)])
                take(a_recv.at[2, z], MT.at[pl.ds(0, per_group)])
        with scope("comb"):
            for s in range(experts // parts):
                mine = slot_rows(z * experts + n % parts * (experts // parts) + s)
                outs = jnp.concatenate([EOG[e, mine, :] for e in range(experts)], axis=0)
                wide = dot(MT[mine, 0:per_group], outs, NN) + dot(
                    MT[mine, pad : pad + per_group], outs, NN
                )
                w = MT[mine, 2 * pad : 2 * pad + 1].astype(F32) + MT[
                    mine, 2 * pad + 128 : 2 * pad + 129
                ].astype(F32)
                G[mine, :] = (wide - w * TR[mine, :].astype(F32)).astype(BF16)
            for i in range(split):
                HOWN[n * split + i] = dot(G[rows, :], W[2, :, i * hw : (i + 1) * hw], NN)
            to_sibling(2, G.at[rows, give], GX.at[rows])

    def backward(n):
        rows = unit_rows(n)
        with scope("bwd"):
            hidden_grad = jnp.concatenate(
                [total(HOWN, HIN, n * split + i) for i in range(split)], axis=1
            )
            for f in range(pieces):
                both = OWN[n * pieces + f]
                pre, up = both[:, :fw], both[:, fw:]
                grad = hidden_grad[:, f * fw : (f + 1) * fw]
                sigma = jax.nn.sigmoid(pre)
                GU[0, rows, f * fw : (f + 1) * fw] = (
                    grad * up * sigma * (1.0 + pre * (1.0 - sigma))
                ).astype(BF16)
                GU[1, rows, f * fw : (f + 1) * fw] = (grad * (pre * sigma)).astype(BF16)
            RG[rows, :] = (
                dot(GU[0, rows, :], W[0], NT) + dot(GU[1, rows, :], W[1], NT)
            ).astype(BF16)
            send_rows(n)
            for i in range(2):
                to_sibling(3 + i, GU.at[i, rows], GUX.at[i, rows])

    def send_rows(n):
        z, share = turn(n // parts), experts // parts
        land = CB.at[slot_rows(me_e), cols(me_z)]

        def send(j, carry):
            e = n % parts * share + j
            rows = RG.at[slot_rows(z * experts + e)]
            here = jnp.logical_and(z == me_z, e == me_e)

            @pl.when(here)
            def _():
                pltpu.make_async_copy(rows, land, a_recv.at[3, me_z]).start()

            @pl.when(jnp.logical_not(here))
            def _():
                remote(rows, land, a_send.at[3], a_recv.at[3, me_z], at(z, e))

            return carry

        lax.fori_loop(0, share, send, 0)

    steps = planes * parts * pieces
    back_steps = planes * parts * split
    begin = pieces - 1 + LAG * (planes - 1) + LAG_PLANE
    begin += max(0, pieces - split) * (planes * parts - 1)

    def each(t, fn, last):
        @pl.when(jnp.logical_and(t >= 0, t < last))
        def _():
            fn(t)

    def each_group(t, fn):
        fits = jnp.logical_and(t >= 0, t < back_steps)

        @pl.when(jnp.logical_and(fits, t % split == 0))
        def _():
            fn(t // split)

    def grad(i, left, left_x, right, right_x, out):
        out[...] = (dot(left, right, TN) + dot(left_x, right_x, TN)) * factor

    def send_targets(z):
        to_plane(2, z, lambda z, e: META.at[slot_rows(e)], MT.at[slot_rows(me)])
        to_plane(
            1, z, lambda z, e: TROWS.at[slot_rows(e), cols(z)], TR.at[slot_rows(me)]
        )

    for k in far_first:
        send_targets(plane(k))

    def tick(t, carry):
        each(t, partial_sums, steps)
        for d in TURNS:
            each(
                t - LAG * dist[d],
                functools.partial(move, OWN, IN, OUT, c_send, c_recv, d), steps,
            )
        each(t - LAG * depth, forward, steps)
        t = t - begin
        each_group(t, slot_grads)
        for d in TURNS:
            each(
                t - LAG_BACK * dist[d],
                functools.partial(move, HOWN, HIN, HOUT, h_send, h_recv, d), back_steps,
            )
        back = t - LAG_BACK * (planes - 1 if LATE else depth) - (split - 1) - LAG_GRADS
        each_group(back, backward)
        return carry

    middle = begin + back_steps + 1
    lax.fori_loop(0, middle, tick, 0)
    to_sibling(0, R.at[:, give], RX)
    with scope("dgrad"):
        take(x_recv.at[1], HX)
        take(x_recv.at[2], GX)
        grad(2, G[:, keep], GX[...], H[...], HX[...], dg_out)
    lax.fori_loop(
        middle, begin + back_steps + LAG_BACK * (planes - 1) + LAG_GRADS + split, tick, 0
    )
    with scope("xg"):
        take(x_recv.at[0], RX)
        take(x_recv.at[3], GUX.at[0])
        take(x_recv.at[4], GUX.at[1])
    with scope("gugrad"):
        grad(0, R[:, keep], RX[...], GU[0], GUX[0], gg_out)
        grad(1, R[:, keep], RX[...], GU[1], GUX[1], ug_out)
    with scope("cb_wait"):
        for k in far_first:
            take(a_recv.at[3, plane(k)], R.at[pl.ds(0, per_group)])
    with scope("tail"):
        cb_out[...] = CB[...]
        for c in sent_w:
            c.wait_send()
        others = pl.ds(0, (peers - 1) * slots)
        for i, buf in enumerate((R, TR, MT, RG)):
            take(a_send.at[i], buf.at[others])
        take(e_send, EOG.at[pl.ds(0, experts - 1)])
        for d in range(2):
            @pl.when(dist[d] < planes - 1)
            def _():
                take(c_send.at[d], OUT.at[d])
                take(h_send.at[d], HOUT.at[d])
        for i, buf in enumerate((RX, HX, GX, GUX.at[0], GUX.at[1])):
            take(x_send.at[i], buf)


def finish(hot, cb, gg, ug, dg, tg_out, gg_out, ug_out, dg_out, TG, t_sem, g_sem):
    copies = []
    for i, (grad, out) in enumerate(((gg, gg_out), (ug, ug_out), (dg, dg_out))):
        copies.append(pltpu.make_async_copy(grad, out.at[:, 0, :], g_sem.at[i]))
        copies[-1].start()
    parts = t_sem.shape[0]
    step = TG.shape[0] // parts
    for j in range(parts):
        rows = slice(j * step, (j + 1) * step)
        TG[rows, :] = dot(hot[:, rows], cb[...], TN).astype(BF16)
        copies.append(pltpu.make_async_copy(TG.at[rows], tg_out.at[rows], t_sem.at[j]))
        copies[-1].start()
    for c in copies:
        c.wait()


def direct_scratch(planes, picked, count, width, half, ff):
    chunk = CORES * half
    all_rows = planes * picked
    dma = pltpu.SemaphoreType.DMA
    return [
        pltpu.VMEM((count, width), BF16),
        pltpu.VMEM((count, width), BF16),
        pltpu.VMEM((picked, width), BF16),
        pltpu.VMEM((picked, width), F32),
        pltpu.VMEM((3, CORES, half, ff), BF16),
        pltpu.VMEM((all_rows, chunk), BF16),
        pltpu.VMEM((all_rows, chunk), BF16),
        pltpu.VMEM((picked, width), BF16),
        pltpu.VMEM((picked, width), BF16),
        pltpu.VMEM((all_rows, chunk), BF16),
        pltpu.VMEM((all_rows, chunk), BF16),
        pltpu.VMEM((picked, width), BF16),
        pltpu.VMEM((3, all_rows, ff), BF16),
        pltpu.VMEM((3, planes - 1, picked, ff), BF16),
        pltpu.VMEM((all_rows, ff), BF16),
        pltpu.VMEM((2, all_rows, ff), BF16),
        pltpu.VMEM((all_rows, half), BF16),
        pltpu.VMEM((all_rows, half), BF16),
        pltpu.VMEM((all_rows, ff), BF16),
        pltpu.VMEM((2, all_rows, ff), BF16),
        dma((planes,)), dma,
        dma((3,)), dma((3,)), dma((3,)),
        dma((4,)), dma((4,)), dma((4, planes)),
        dma((3,)), dma((3, planes)),
        dma((3, 2, planes)), dma((3, planes)),
        dma((5,)), dma((5,)),
        pltpu.VMEM((3, half, ff), F32), dma((4,)),
    ]


def chain_scratch(planes, experts, picked, count, width, half, ff, pieces, split, parts):
    slots = picked // experts
    chunk = CORES * half
    all_rows = planes * picked
    steps = planes * parts * pieces
    back_steps = planes * parts * split
    unit = picked // parts
    fw = ff // pieces
    table = 2 * (-(-picked // 128) * 128) + 256
    dma = pltpu.SemaphoreType.DMA
    return [
        pltpu.VMEM((1, experts, 1, slots), jnp.int32),
        pltpu.VMEM((1, experts), jnp.int32),
        pltpu.VMEM((1, experts, 1, slots), F32),
        dma((3,)),
        pltpu.VMEM((count, width), BF16),
        pltpu.VMEM((count, width), BF16),
        pltpu.VMEM((picked, width), BF16),
        pltpu.VMEM((picked, width), BF16),
        pltpu.VMEM((picked, table), BF16),
        pltpu.VMEM((all_rows, table), BF16),
        pltpu.VMEM((3, chunk, ff), BF16),
        pltpu.VMEM((all_rows, chunk), BF16),
        pltpu.VMEM((all_rows, chunk), BF16),
        pltpu.VMEM((all_rows, chunk), BF16),
        pltpu.VMEM((experts, all_rows, chunk), BF16),
        pltpu.VMEM((steps, unit, 2 * fw), F32),
        pltpu.VMEM((2, steps, unit, 2 * fw), BF16),
        pltpu.VMEM((2, steps, unit, 2 * fw), BF16),
        pltpu.VMEM((back_steps, unit, ff // split), F32),
        pltpu.VMEM((2, back_steps, unit, ff // split), BF16),
        pltpu.VMEM((2, back_steps, unit, ff // split), BF16),
        pltpu.VMEM((all_rows, ff), BF16),
        pltpu.VMEM((2, all_rows, ff), BF16),
        pltpu.VMEM((all_rows, chunk), BF16),
        pltpu.VMEM((picked, width), BF16),
        pltpu.VMEM((all_rows, half), BF16),
        pltpu.VMEM((all_rows, half), BF16),
        pltpu.VMEM((all_rows, ff), BF16),
        pltpu.VMEM((2, all_rows, ff), BF16),
        dma((planes,)), dma, dma((3,)), dma((3,)), dma((3,)),
        dma((4,)), dma((4, planes)), dma, dma((planes * parts,)),
        dma((2,)), dma((2, steps)), dma((2,)), dma((2, back_steps)),
        dma((5,)), dma((5,)),
    ]


def held_bytes(scratch):
    return sum(
        math.prod(s.shape) * jnp.dtype(s.dtype).itemsize
        for s in scratch
        if getattr(s, "memory_space", None) == pltpu.VMEM
    )


def on_device(
    tokens, target, route_index, route_count, route_gate, gate_weight, up_weight, down_weight
):
    groups = lax.axis_size("dp")
    experts = lax.axis_size("expert")
    planes = groups // CORES
    slots = route_index.shape[3]
    count, width = tokens.shape
    half, _, ff = gate_weight.shape
    picked = experts * slots
    factor = (groups * experts * slots) ** (-0.5)
    pieces, split = (
        max(n for n in range(1, most + 1) if ff % (128 * n) == 0)
        for most in (PIECES, BACK_PIECES)
    )
    vmem = pl.BlockSpec(memory_space=pltpu.VMEM)
    anyw = pl.BlockSpec(memory_space=pl.ANY)
    grad = jax.ShapeDtypeStruct((half, ff), F32)
    parts = PARTS if experts % PARTS == 0 else 1
    scratch = chain_scratch(
        planes, experts, picked, count, width, half, ff, pieces, split, parts
    )
    body = functools.partial(chain_kernel, planes, experts, slots, factor, pieces, parts)
    out, limit, small = vmem, CHAIN_LIMIT, anyw
    if held_bytes(scratch) > CHAIN_LIMIT * 3 // 4:
        scratch = direct_scratch(planes, picked, count, width, half, ff)
        body = functools.partial(direct_kernel, planes, experts, slots, factor)
        out, limit, small = anyw, VMEM_LIMIT, vmem
    came_back, hot, gate_gradient, up_gradient, down_gradient = pl.pallas_call(
        body,
        out_shape=(
            jax.ShapeDtypeStruct((picked, width), BF16),
            jax.ShapeDtypeStruct((picked, count), BF16),
            grad, grad, grad,
        ),
        in_specs=[small] * 3 + [anyw] * 5,
        out_specs=(out, vmem, out, out, out),
        scratch_shapes=scratch,
        compiler_params=pltpu.CompilerParams(
            collective_id=0, has_side_effects=True, vmem_limit_bytes=limit
        ),
        name="routed_layer",
    )(
        *(
            pltpu.with_memory_space_constraint(x, pltpu.MemorySpace.HBM)
            for x in (
                route_index, route_count.reshape(1, experts), route_gate, tokens, target, gate_weight.reshape(half, ff), up_weight.reshape(half, ff),
                down_weight.reshape(half, ff),
            )
        ),
    )
    blocks = max(n for n in range(1, 9) if count % (128 * n) == 0)
    grad = jax.ShapeDtypeStruct((half, 1, ff), F32)
    return tuple(pl.pallas_call(
        finish,
        out_shape=(jax.ShapeDtypeStruct((count, width), BF16), grad, grad, grad),
        in_specs=[vmem] * 5,
        out_specs=[anyw] * 4,
        scratch_shapes=[
            pltpu.VMEM((count, width), BF16),
            pltpu.SemaphoreType.DMA((blocks,)), pltpu.SemaphoreType.DMA((3,)),
        ],
        compiler_params=pltpu.CompilerParams(vmem_limit_bytes=FINISH_LIMIT),
        name="finish",
    )(hot, came_back, gate_gradient, up_gradient, down_gradient))


def solution(mesh):
    return jax.shard_map(
        on_device,
        mesh=mesh,
        in_specs=(
            P(("dp", "expert"), None),
            P(("dp", "expert"), None),
            P("dp", None, "expert", None),
            P("dp", None, "expert"),
            P("dp", None, "expert", None),
            P("dp", "expert", None),
            P("dp", "expert", None),
            P("dp", "expert", None),
        ),
        out_specs=(
            P(("dp", "expert"), None),
            P("dp", "expert", None),
            P("dp", "expert", None),
            P("dp", "expert", None),
        ),
        check_vma=False,
    )
```

```python
import contextlib
import functools
import math

import jax
import jax.numpy as jnp
from jax import lax
from jax.experimental import pallas as pl
from jax.experimental.pallas import tpu as pltpu
from jax.sharding import PartitionSpec as P

F32 = jnp.float32
BF16 = jnp.bfloat16
VMEM_LIMIT = 67000000
CORES = 2
PIECES = 3
BACK_PIECES = 3
PARTS = 2
LAG = 5
LAG_PLANE = 6
LAG_BACK = 6
LAG_GRADS = 0
LATE = True
TURNS = (1, 0)
OUTER_FIRST = True
CHAIN_LIMIT = 44000000
FINISH_LIMIT = 40000000


def dot(a, b, dims, precision=None):
    return lax.dot_general(
        a, b, (dims, ((), ())), preferred_element_type=F32, precision=precision
    )


def scope(name):
    return contextlib.nullcontext()


NN = ((1,), (0,))
NT = ((1,), (1,))
TN = ((0,), (0,))


def direct_kernel(
    planes, experts, slots, factor,
    index, count, gate, tokens, target, gw, uw, dw,
    cb_out, hot_out, gg_out, ug_out, dg_out,
    TOK, TGT, ROWS, TROWS, W, R, EO, RET, SG, G, RG, CB, PS, PR, H, GU, RX, GX, HX, GUX,
    t_loc, g_loc, w_loc, w_send, w_recv, a_loc, a_send, a_recv, p_send, p_recv,
    h_send, h_recv, x_send, x_recv, GRADS, o_loc,
):
    dp = lax.axis_index("dp")
    me_e = lax.axis_index("expert")
    me_z = dp // CORES
    core = dp % CORES
    peers = planes * experts
    per_group = experts * slots
    half = gw.shape[0]
    chunk = CORES * half
    ff = gw.shape[1]
    me = me_z * experts + me_e
    sibling = {"dp": me_z * CORES + (1 - core), "expert": me_e}
    order = sorted(range(1, planes), key=lambda k: -min(k, planes - k))

    def at(z, e):
        return {"dp": z * CORES + core, "expert": e}

    def plane(k):
        return (me_z + k) % planes

    def slot_rows(n):
        return pl.ds(pl.multiple_of(n * slots, slots), slots)

    def cols(z):
        return pl.ds(pl.multiple_of(z * chunk, chunk), chunk)

    def group_rows(z):
        return pl.ds(pl.multiple_of(z * per_group, per_group), per_group)

    barrier = pltpu.get_barrier_semaphore()

    def greet(k, carry):
        p = (me + k) % peers
        pl.semaphore_signal(
            barrier, inc=1, device_id=at(p // experts, p % experts),
            device_id_type=pl.DeviceIdType.MESH,
        )
        return carry

    lax.fori_loop(1, peers, greet, 0)
    pl.semaphore_signal(
        barrier, inc=1, device_id=sibling, device_id_type=pl.DeviceIdType.MESH
    )
    tok_copies = {}
    for k in order + [0]:
        z = plane(k)
        tok_copies[k] = pltpu.make_async_copy(
            tokens.at[:, cols(z)], TOK.at[:, cols(z)], t_loc.at[k]
        )
        tok_copies[k].start()
    locals_w = []
    for i, w in enumerate((gw, uw, dw)):
        c = pltpu.make_async_copy(w, W.at[i, core], w_loc.at[i])
        c.start()
        locals_w.append(c)
    tgt_copy = pltpu.make_async_copy(target, TGT, g_loc)
    tgt_copy.start()

    lane = lax.broadcasted_iota(jnp.int32, (slots, slots), 1)
    own_lane = lane == lax.broadcasted_iota(jnp.int32, (slots, slots), 0)
    slot_id = lax.broadcasted_iota(jnp.int32, (slots, 1), 0)
    names, weights = [], []
    for e in range(experts):
        live = slot_id < jnp.broadcast_to(count[0:1, e : e + 1], (slots, 1))
        ids = jnp.broadcast_to(index[0, e], (slots, slots))
        ids = jnp.sum(jnp.where(own_lane, ids, 0), axis=1, keepdims=True)
        names.append(jnp.where(live, ids, -1))
        g = jnp.broadcast_to(gate[0, e], (slots, slots))
        g = jnp.sum(jnp.where(own_lane, g, 0.0), axis=1, keepdims=True)
        weights.append(jnp.where(live, g, 0.0))
    names = jnp.concatenate(names, axis=0)
    wcol = jnp.concatenate(weights, axis=0)
    hot = (
        names == lax.broadcasted_iota(jnp.int32, (per_group, TOK.shape[0]), 1)
    ).astype(F32).astype(BF16)
    hot_out[...] = hot

    def remote(src, dst, s, r, dev):
        c = pltpu.make_async_remote_copy(
            src_ref=src, dst_ref=dst, send_sem=s, recv_sem=r,
            device_id=dev, device_id_type=pl.DeviceIdType.MESH,
        )
        c.start()
        return c

    def to_plane(i, z, source, land):
        here = z == me_z

        @pl.when(here)
        def _():
            pltpu.make_async_copy(source(me_z, me_e), land, a_loc.at[i]).start()

        first = jnp.where(here, 1, 0)

        def send(j, carry):
            e = (me_e + j) % experts
            remote(source(z, e), land, a_send.at[i], a_recv.at[i, me_z], at(z, e))
            return carry

        lax.fori_loop(first, experts, send, 0)

    def owners(src, dst, i, z):
        to_plane(i, z, lambda z, e: src.at[slot_rows(e), cols(z)], dst.at[slot_rows(me)])

    def sources(src, dst, i, z):
        to_plane(
            i, z, lambda z, e: src.at[slot_rows(z * experts + e)],
            dst.at[slot_rows(me_e), cols(me_z)],
        )

    def take(sem, ref):
        pltpu.make_async_copy(ref, ref, sem).wait()

    def arrived(i, k):
        if k == 0:
            take(a_recv.at[i, me_z], R.at[pl.ds(0, (experts - 1) * slots)])
            take(a_loc.at[i], R.at[pl.ds(0, slots)])
        else:
            take(a_recv.at[i, plane(k)], R.at[pl.ds(0, per_group)])

    outs = []

    def put(i, src, dst):
        c = pltpu.make_async_copy(src, dst, o_loc.at[i])
        c.start()
        outs.append(c)

    def weight(i):
        return W[i].reshape(chunk, ff)

    pl.semaphore_wait(barrier, peers)
    for k in order + [0]:
        z = plane(k)
        tok_copies[k].wait()
        ROWS[:, cols(z)] = dot(hot, TOK[:, cols(z)], NN).astype(BF16)
        owners(ROWS, R, 0, z)
    sent_w = [
        remote(w, W.at[i, core], w_send.at[i], w_recv.at[i], sibling)
        for i, w in enumerate((gw, uw, dw))
    ]

    def send_sum(i, k):
        remote(
            PS.at[i, group_rows(plane(k))], PR.at[i, k - 1],
            p_send.at[i], p_recv.at[i, k - 1], at(plane(k), me_e),
        )

    def pass_on(buf, i, s, way):
        to = me_z + way

        @pl.when(jnp.logical_and(to >= 0, to < planes))
        def _():
            rows_s = buf.at[group_rows(s)]
            remote(
                rows_s, rows_s, h_send.at[i, (way + 1) // 2, s], h_recv.at[i, s],
                at(to, me_e),
            )

    def spread(buf, i):
        for way in (1, -1):
            pass_on(buf, i, me_z, way)

    def along(bufs, first, fn):
        fn(me_z)
        for far in range(1, planes):
            for way in (1, -1):
                s = me_z - way * far

                @pl.when(jnp.logical_and(s >= 0, s < planes))
                def _():
                    for j, buf in enumerate(bufs):
                        take(h_recv.at[first + j, s], buf.at[group_rows(s)])
                        pass_on(buf, first + j, s, way)
                    fn(s)

    def spread_sent(buf, i):
        for s in range(planes):
            rows_s = buf.at[pl.ds(s * per_group, per_group)]

            @pl.when(jnp.logical_and(me_z > 0, me_z <= s))
            def _():
                take(h_send.at[i, 0, s], rows_s)

            @pl.when(jnp.logical_and(me_z < planes - 1, me_z >= s))
            def _():
                take(h_send.at[i, 1, s], rows_s)

    def total(i, own):
        for k in order:
            take(p_recv.at[i, k - 1], PR.at[i, k - 1])
            own = own + PR[i, k - 1].astype(F32)
        return own

    keep = pl.ds(pl.multiple_of(core * half, half), half)
    give = pl.ds(pl.multiple_of((1 - core) * half, half), half)
    mine = group_rows(me_z)

    for i in range(2):
        locals_w[i].wait()
        sent_w[i].wait_recv()
    for k in order:
        z = plane(k)
        arrived(0, k)
        for i in range(2):
            PS[i, group_rows(z), :] = dot(R[group_rows(z), :], weight(i), NN).astype(BF16)
            send_sum(i, k)
    arrived(0, 0)
    gate_own = dot(R[mine, :], weight(0), NN)
    up_own = dot(R[mine, :], weight(1), NN)
    x_rows = remote(R.at[:, give], RX, x_send.at[0], x_recv.at[0], sibling)
    tgt_copy.wait()
    for z in range(planes):
        piece = slice(z * chunk, (z + 1) * chunk)
        TROWS[:, piece] = dot(hot, TGT[:, piece], NN)
    same = dot(hot, hot, NT).astype(BF16)
    gate_pre = total(0, gate_own)
    up_pre = total(1, up_own)
    sigma = jax.nn.sigmoid(gate_pre)
    active = gate_pre * sigma
    H[mine, :] = (active * up_pre).astype(BF16)
    spread(H, 0)
    locals_w[2].wait()
    sent_w[2].wait_recv()

    def expert_out(z):
        EO[group_rows(z), :] = dot(H[group_rows(z), :], weight(2), NT).astype(BF16)
        sources(EO, RET, 1, z)

    along([H], 0, expert_out)
    x_hidden = remote(H, HX, x_send.at[1], x_recv.at[1], sibling)
    for k in order + [0]:
        z = plane(k)
        arrived(1, k)
        part = wcol * RET[:, cols(z)].astype(F32)
        combined = -TROWS[:, cols(z)]
        for _ in range(3):
            top = part.astype(BF16)
            combined = combined + dot(same, top, NN)
            part = part - top.astype(F32)
        SG[:, cols(z)] = (wcol * combined).astype(BF16)
        owners(SG, G, 2, z)

    for k in order:
        z = plane(k)
        arrived(2, k)
        PS[2, group_rows(z), :] = dot(G[group_rows(z), :], weight(2), NN).astype(BF16)
        send_sum(2, k)
    arrived(2, 0)
    own = dot(G[mine, :], weight(2), NN)
    x_grad = remote(G.at[:, give], GX, x_send.at[2], x_recv.at[2], sibling)
    x_hidden.wait_recv()
    x_grad.wait_recv()
    GRADS[2] = (dot(G[:, keep], H[...], TN) + dot(GX[...], HX[...], TN)) * factor
    put(2, GRADS.at[2], dg_out)
    hidden_grad = total(2, own)
    GU[0, mine, :] = (
        hidden_grad * up_pre * sigma * (1.0 + gate_pre * (1.0 - sigma))
    ).astype(BF16)
    spread(GU.at[0], 1)
    GU[1, mine, :] = (hidden_grad * active).astype(BF16)
    spread(GU.at[1], 2)

    def row_grad(z):
        RG[group_rows(z), :] = (
            dot(GU[0, group_rows(z), :], weight(0), NT)
            + dot(GU[1, group_rows(z), :], weight(1), NT)
        ).astype(BF16)
        sources(RG, CB, 3, z)

    along([GU.at[0], GU.at[1]], 1, row_grad)
    x_gate = remote(GU.at[0], GUX.at[0], x_send.at[3], x_recv.at[3], sibling)
    x_up = remote(GU.at[1], GUX.at[1], x_send.at[4], x_recv.at[4], sibling)
    x_rows.wait_recv()
    x_gate.wait_recv()
    GRADS[0] = (dot(R[:, keep], GU[0], TN) + dot(RX[...], GUX[0], TN)) * factor
    put(0, GRADS.at[0], gg_out)
    x_up.wait_recv()
    GRADS[1] = (dot(R[:, keep], GU[1], TN) + dot(RX[...], GUX[1], TN)) * factor
    put(1, GRADS.at[1], ug_out)
    for k in order + [0]:
        arrived(3, k)
    put(3, CB, cb_out)

    for c in sent_w + [x_rows, x_hidden, x_grad, x_gate, x_up]:
        c.wait_send()
    for i in range(4):
        take(a_send.at[i], R.at[pl.ds(0, (peers - 1) * slots)])
    for i in range(3):
        take(p_send.at[i], PR.at[i])
    for i, buf in enumerate((H, GU.at[0], GU.at[1])):
        spread_sent(buf, i)
    for c in outs:
        c.wait()


def chain_kernel(
    planes, experts, slots, factor, pieces, parts,
    index_in, count_in, gate_in, tokens, target, gw, uw, dw,
    cb_out, hot_out, gg_out, ug_out, dg_out,
    index, count, gate, r_loc, TOK, TGT, ROWS, TROWS, META, MT, W, R, TR, G, EOG,
    OWN, IN, OUT, HOWN, HIN, HOUT, H, GU, RG, CB, RX, GX, HX, GUX,
    t_loc, g_loc, w_loc, w_send, w_recv, a_send, a_recv, e_send, e_recv,
    c_send, c_recv, h_send, h_recv, x_send, x_recv,
):
    dp = lax.axis_index("dp")
    me_e = lax.axis_index("expert")
    me_z = dp // CORES
    core = dp % CORES
    peers = planes * experts
    per_group = experts * slots
    half = gw.shape[0]
    chunk = CORES * half
    ff = gw.shape[1]
    fw = ff // pieces
    split = HIN.shape[1] // (planes * parts)
    unit = per_group // parts
    hw = ff // split
    me = me_z * experts + me_e
    sibling = {"dp": me_z * CORES + (1 - core), "expert": me_e}
    ways = (1, -1)
    side = jnp.where(2 * me_z < planes, 1, -1)
    far_first = sorted(range(1, planes), key=lambda k: abs(k - planes / 2)) + [0]
    dist = (me_z, planes - 1 - me_z)
    depth = jnp.maximum(dist[0], dist[1])

    def at(z, e):
        return {"dp": z * CORES + core, "expert": e}

    def plane(k):
        return (me_z + side * k + planes) % planes

    def slot_rows(n):
        return pl.ds(pl.multiple_of(n * slots, slots), slots)

    def cols(z):
        return pl.ds(pl.multiple_of(z * chunk, chunk), chunk)

    def group_rows(z):
        return pl.ds(pl.multiple_of(z * per_group, per_group), per_group)

    def unit_rows(n):
        rows = turn(n // parts) * per_group + n % parts * unit
        return pl.ds(pl.multiple_of(rows, unit), unit)

    def turn(g):
        if planes % 2:
            return g
        g = planes - 1 - g if OUTER_FIRST else g
        return planes // 2 - 1 - g // 2 + (g % 2) * (2 * (g // 2) + 1)

    barrier = pltpu.get_barrier_semaphore()

    def greet(k, carry):
        p = (me + k) % peers
        pl.semaphore_signal(
            barrier, inc=1, device_id=at(p // experts, p % experts),
            device_id_type=pl.DeviceIdType.MESH,
        )
        return carry

    lax.fori_loop(1, peers, greet, 0)
    pl.semaphore_signal(
        barrier, inc=1, device_id=sibling, device_id_type=pl.DeviceIdType.MESH
    )
    routes = [
        pltpu.make_async_copy(src, dst, r_loc.at[i])
        for i, (src, dst) in enumerate(
            ((index_in, index), (count_in, count), (gate_in, gate))
        )
    ]
    for c in routes:
        c.start()
    tok_copies = {}
    for k in far_first:
        tok_copies[k] = pltpu.make_async_copy(
            tokens.at[:, cols(plane(k))], TOK.at[:, cols(plane(k))], t_loc.at[k]
        )
        tok_copies[k].start()
    locals_w = []
    keep = pl.ds(pl.multiple_of(core * half, half), half)
    give = pl.ds(pl.multiple_of((1 - core) * half, half), half)
    for i, w in enumerate((gw, uw, dw)):
        c = pltpu.make_async_copy(w, W.at[i, keep], w_loc.at[i])
        c.start()
        locals_w.append(c)
    tgt_copy = pltpu.make_async_copy(target, TGT, g_loc)
    tgt_copy.start()

    for c in routes:
        c.wait()
    lane = lax.broadcasted_iota(jnp.int32, (slots, slots), 1)
    own_lane = lane == lax.broadcasted_iota(jnp.int32, (slots, slots), 0)
    slot_id = lax.broadcasted_iota(jnp.int32, (slots, 1), 0)
    names, weights = [], []
    for e in range(experts):
        live = slot_id < jnp.broadcast_to(count[0:1, e : e + 1], (slots, 1))
        ids = jnp.broadcast_to(index[0, e], (slots, slots))
        ids = jnp.sum(jnp.where(own_lane, ids, 0), axis=1, keepdims=True)
        names.append(jnp.where(live, ids, -1))
        g = jnp.broadcast_to(gate[0, e], (slots, slots))
        g = jnp.sum(jnp.where(own_lane, g, 0.0), axis=1, keepdims=True)
        weights.append(jnp.where(live, g, 0.0))
    names = jnp.concatenate(names, axis=0)
    wcol = jnp.concatenate(weights, axis=0)
    hot = (
        names == lax.broadcasted_iota(jnp.int32, (per_group, TOK.shape[0]), 1)
    ).astype(F32).astype(BF16)
    hot_out[...] = hot

    def remote(src, dst, s, r, dev):
        c = pltpu.make_async_remote_copy(
            src_ref=src, dst_ref=dst, send_sem=s, recv_sem=r,
            device_id=dev, device_id_type=pl.DeviceIdType.MESH,
        )
        c.start()
        return c

    def take(sem, ref):
        pltpu.make_async_copy(ref, ref, sem).wait()

    def to_plane(i, z, source, land):
        here = z == me_z

        @pl.when(here)
        def _():
            pltpu.make_async_copy(source(me_z, me_e), land, a_recv.at[i, me_z]).start()

        def send(j, carry):
            e = (me_e + j) % experts
            remote(source(z, e), land, a_send.at[i], a_recv.at[i, me_z], at(z, e))
            return carry

        lax.fori_loop(jnp.where(here, 1, 0), experts, send, 0)

    for k in far_first:
        z = plane(k)
        tok_copies[k].wait()
        ROWS[:, cols(z)] = dot(hot, TOK[:, cols(z)], NN).astype(BF16)
    for way, d in zip(ways, range(2)):
        @pl.when(dist[d] == 0)
        def _():
            IN[d] = jnp.zeros(IN.shape[1:], BF16)
            HIN[d] = jnp.zeros(HIN.shape[1:], BF16)

    with scope("barrier"):
        pl.semaphore_wait(barrier, peers)
    sent_w = [
        remote(w, W.at[i, keep], w_send.at[i], w_recv.at[i], sibling)
        for i, w in enumerate((gw, uw, dw))
    ]
    for k in far_first:
        to_plane(
            0, plane(k), lambda z, e: ROWS.at[slot_rows(e), cols(z)], R.at[slot_rows(me)]
        )
    with scope("trows"):
        tgt_copy.wait()
        for k in far_first:
            z = plane(k)
            TROWS[:, cols(z)] = dot(hot, TGT[:, cols(z)], NN).astype(BF16)
    with scope("meta"):
        square = (per_group, per_group)
        eye = lax.broadcasted_iota(jnp.int32, square, 0) == lax.broadcasted_iota(
            jnp.int32, square, 1
        )
        wrow = jnp.sum(jnp.where(eye, wcol, 0.0), axis=0, keepdims=True)
        mix = dot(hot, hot, NT) * wrow
        top = mix.astype(BF16)
        if META.shape[1] > 2 * per_group:
            META[...] = jnp.zeros(META.shape, BF16)
        META[:, 0:per_group] = top
        META[:, per_group : 2 * per_group] = (mix - top.astype(F32)).astype(BF16)

    with scope("w_wait"):
        for i in range(3):
            locals_w[i].wait()
            sent_w[i].wait_recv()

    def piece(f):
        return pl.ds(pl.multiple_of(f * fw, fw), fw)

    def partial_sums(c):
        n, f = c // pieces, c % pieces

        @pl.when(c % (pieces * parts) == 0)
        def _():
            with scope("x_wait"):
                take(a_recv.at[0, turn(n // parts)], R.at[pl.ds(0, per_group)])

        with scope("own"):
            rows = R[unit_rows(n), :]
            for i in range(2):
                OWN[c, :, i * fw : (i + 1) * fw] = dot(rows, W[i, :, piece(f)], NN)

    def move(own, inn, out, send, recv, d, c):
        @pl.when(dist[d] > 0)
        def _():
            with scope("mv%d" % (own is HOWN)):
                take(recv.at[d, c], inn.at[d, c])

        @pl.when(dist[d] < planes - 1)
        def _():
            out[d, c] = (own[c] + inn[d, c].astype(F32)).astype(BF16)
            remote(
                out.at[d, c], inn.at[d, c], send.at[d], recv.at[d, c],
                at(me_z + ways[d], me_e),
            )

    def total(own, inn, c):
        return own[c] + inn[0, c].astype(F32) + inn[1, c].astype(F32)

    def to_sibling(i, src, dst):
        remote(src, dst, x_send.at[i], x_recv.at[i], sibling)

    def forward(c):
        n, f = c // pieces, c % pieces
        rows = unit_rows(n)
        with scope("fwd"):
            both = total(OWN, IN, c)
            OWN[c] = both
            pre, up = both[:, :fw], both[:, fw:]
            H[rows, piece(f)] = (pre * jax.nn.sigmoid(pre) * up).astype(BF16)

        @pl.when(f == pieces - 1)
        def _():
            with scope("eo"):
                EOG[me_e, rows, :] = dot(H[rows, :], W[2], NT).astype(BF16)
                outs = EOG.at[me_e, rows]

                def send(j, carry):
                    remote(
                        outs, outs, e_send, e_recv.at[n], at(me_z, (me_e + j) % experts)
                    )
                    return carry

                lax.fori_loop(1, experts, send, 0)
                to_sibling(1, H.at[rows], HX.at[rows])

    spread = (slots, 2 * per_group)
    own_slot = (
        lax.broadcasted_iota(jnp.int32, spread, 1) % per_group
        == lax.broadcasted_iota(jnp.int32, spread, 0) + me_e * slots
    )

    def slot_grads(n):
        z = turn(n // parts)
        rows = unit_rows(n)
        with scope("eo_wait"):
            take(e_recv.at[n], EOG.at[pl.ds(0, experts - 1), pl.ds(0, unit)])

            @pl.when(n % parts == 0)
            def _():
                take(a_recv.at[1, z], TR.at[pl.ds(0, per_group)])
                take(a_recv.at[2, z], MT.at[pl.ds(0, per_group)])
        with scope("comb"):
            for s in range(experts // parts):
                mine = slot_rows(z * experts + n % parts * (experts // parts) + s)
                outs = [EOG[e, mine, :] for e in range(experts)]
                table = MT[mine, 0 : 2 * per_group]
                wide = dot(table, jnp.concatenate(outs + outs, axis=0), NN)
                w = jnp.sum(
                    jnp.where(own_slot, table.astype(F32), 0.0), axis=1, keepdims=True
                )
                G[mine, :] = (w * (wide - TR[mine, :].astype(F32))).astype(BF16)
            for i in range(split):
                HOWN[n * split + i] = dot(G[rows, :], W[2, :, i * hw : (i + 1) * hw], NN)
            to_sibling(2, G.at[rows, give], GX.at[rows])

    def backward(n):
        rows = unit_rows(n)
        with scope("bwd"):
            hidden_grad = jnp.concatenate(
                [total(HOWN, HIN, n * split + i) for i in range(split)], axis=1
            )
            for f in range(pieces):
                both = OWN[n * pieces + f]
                pre, up = both[:, :fw], both[:, fw:]
                grad = hidden_grad[:, f * fw : (f + 1) * fw]
                sigma = jax.nn.sigmoid(pre)
                GU[0, rows, f * fw : (f + 1) * fw] = (
                    grad * up * sigma * (1.0 + pre * (1.0 - sigma))
                ).astype(BF16)
                GU[1, rows, f * fw : (f + 1) * fw] = (grad * (pre * sigma)).astype(BF16)
            RG[rows, :] = (
                dot(GU[0, rows, :], W[0], NT) + dot(GU[1, rows, :], W[1], NT)
            ).astype(BF16)
            send_rows(n)
            for i in range(2):
                to_sibling(3 + i, GU.at[i, rows], GUX.at[i, rows])

    def send_rows(n):
        z, share = turn(n // parts), experts // parts
        land = CB.at[slot_rows(me_e), cols(me_z)]

        def send(j, carry):
            e = n % parts * share + j
            rows = RG.at[slot_rows(z * experts + e)]
            here = jnp.logical_and(z == me_z, e == me_e)

            @pl.when(here)
            def _():
                pltpu.make_async_copy(rows, land, a_recv.at[3, me_z]).start()

            @pl.when(jnp.logical_not(here))
            def _():
                remote(rows, land, a_send.at[3], a_recv.at[3, me_z], at(z, e))

            return carry

        lax.fori_loop(0, share, send, 0)

    steps = planes * parts * pieces
    back_steps = planes * parts * split
    begin = pieces - 1 + LAG * (planes - 1) + LAG_PLANE
    begin += max(0, pieces - split) * (planes * parts - 1)

    def each(t, fn, last):
        @pl.when(jnp.logical_and(t >= 0, t < last))
        def _():
            fn(t)

    def each_group(t, fn):
        fits = jnp.logical_and(t >= 0, t < back_steps)

        @pl.when(jnp.logical_and(fits, t % split == 0))
        def _():
            fn(t // split)

    def grad(i, left, left_x, right, right_x, out):
        out[...] = (dot(left, right, TN) + dot(left_x, right_x, TN)) * factor

    def send_targets(z):
        to_plane(2, z, lambda z, e: META.at[slot_rows(e)], MT.at[slot_rows(me)])
        to_plane(
            1, z, lambda z, e: TROWS.at[slot_rows(e), cols(z)], TR.at[slot_rows(me)]
        )

    for k in far_first:
        send_targets(plane(k))

    def tick(t, carry):
        each(t, partial_sums, steps)
        for d in TURNS:
            each(
                t - LAG * dist[d],
                functools.partial(move, OWN, IN, OUT, c_send, c_recv, d), steps,
            )
        each(t - LAG * depth, forward, steps)
        t = t - begin
        each_group(t, slot_grads)
        for d in TURNS:
            each(
                t - LAG_BACK * dist[d],
                functools.partial(move, HOWN, HIN, HOUT, h_send, h_recv, d), back_steps,
            )
        back = t - LAG_BACK * (planes - 1 if LATE else depth) - (split - 1) - LAG_GRADS
        each_group(back, backward)
        return carry

    middle = begin + back_steps + 1
    lax.fori_loop(0, middle, tick, 0)
    to_sibling(0, R.at[:, give], RX)
    with scope("dgrad"):
        take(x_recv.at[1], HX)
        take(x_recv.at[2], GX)
        grad(2, G[:, keep], GX[...], H[...], HX[...], dg_out)
    lax.fori_loop(
        middle, begin + back_steps + LAG_BACK * (planes - 1) + LAG_GRADS + split, tick, 0
    )
    with scope("xg"):
        take(x_recv.at[0], RX)
        take(x_recv.at[3], GUX.at[0])
        take(x_recv.at[4], GUX.at[1])
    with scope("gugrad"):
        grad(0, R[:, keep], RX[...], GU[0], GUX[0], gg_out)
        grad(1, R[:, keep], RX[...], GU[1], GUX[1], ug_out)
    with scope("cb_wait"):
        for k in far_first:
            take(a_recv.at[3, plane(k)], R.at[pl.ds(0, per_group)])
    with scope("tail"):
        cb_out[...] = CB[...]
        for c in sent_w:
            c.wait_send()
        others = pl.ds(0, (peers - 1) * slots)
        for i, buf in enumerate((R, TR, MT, RG)):
            take(a_send.at[i], buf.at[others])
        take(e_send, EOG.at[pl.ds(0, experts - 1)])
        for d in range(2):
            @pl.when(dist[d] < planes - 1)
            def _():
                take(c_send.at[d], OUT.at[d])
                take(h_send.at[d], HOUT.at[d])
        for i, buf in enumerate((RX, HX, GX, GUX.at[0], GUX.at[1])):
            take(x_send.at[i], buf)


def finish(hot, cb, gg, ug, dg, tg_out, gg_out, ug_out, dg_out, TG, t_sem, g_sem):
    copies = []
    for i, (grad, out) in enumerate(((gg, gg_out), (ug, ug_out), (dg, dg_out))):
        copies.append(pltpu.make_async_copy(grad, out.at[:, 0, :], g_sem.at[i]))
        copies[-1].start()
    parts = t_sem.shape[0]
    step = TG.shape[0] // parts
    for j in range(parts):
        rows = slice(j * step, (j + 1) * step)
        TG[rows, :] = dot(hot[:, rows], cb[...], TN).astype(BF16)
        copies.append(pltpu.make_async_copy(TG.at[rows], tg_out.at[rows], t_sem.at[j]))
        copies[-1].start()
    for c in copies:
        c.wait()


def direct_scratch(planes, picked, count, width, half, ff):
    chunk = CORES * half
    all_rows = planes * picked
    dma = pltpu.SemaphoreType.DMA
    return [
        pltpu.VMEM((count, width), BF16),
        pltpu.VMEM((count, width), BF16),
        pltpu.VMEM((picked, width), BF16),
        pltpu.VMEM((picked, width), F32),
        pltpu.VMEM((3, CORES, half, ff), BF16),
        pltpu.VMEM((all_rows, chunk), BF16),
        pltpu.VMEM((all_rows, chunk), BF16),
        pltpu.VMEM((picked, width), BF16),
        pltpu.VMEM((picked, width), BF16),
        pltpu.VMEM((all_rows, chunk), BF16),
        pltpu.VMEM((all_rows, chunk), BF16),
        pltpu.VMEM((picked, width), BF16),
        pltpu.VMEM((3, all_rows, ff), BF16),
        pltpu.VMEM((3, planes - 1, picked, ff), BF16),
        pltpu.VMEM((all_rows, ff), BF16),
        pltpu.VMEM((2, all_rows, ff), BF16),
        pltpu.VMEM((all_rows, half), BF16),
        pltpu.VMEM((all_rows, half), BF16),
        pltpu.VMEM((all_rows, ff), BF16),
        pltpu.VMEM((2, all_rows, ff), BF16),
        dma((planes,)), dma,
        dma((3,)), dma((3,)), dma((3,)),
        dma((4,)), dma((4,)), dma((4, planes)),
        dma((3,)), dma((3, planes)),
        dma((3, 2, planes)), dma((3, planes)),
        dma((5,)), dma((5,)),
        pltpu.VMEM((3, half, ff), F32), dma((4,)),
    ]


def chain_scratch(planes, experts, picked, count, width, half, ff, pieces, split, parts):
    slots = picked // experts
    chunk = CORES * half
    all_rows = planes * picked
    steps = planes * parts * pieces
    back_steps = planes * parts * split
    unit = picked // parts
    fw = ff // pieces
    table = -(-2 * picked // 128) * 128
    dma = pltpu.SemaphoreType.DMA
    return [
        pltpu.VMEM((1, experts, 1, slots), jnp.int32),
        pltpu.VMEM((1, experts), jnp.int32),
        pltpu.VMEM((1, experts, 1, slots), F32),
        dma((3,)),
        pltpu.VMEM((count, width), BF16),
        pltpu.VMEM((count, width), BF16),
        pltpu.VMEM((picked, width), BF16),
        pltpu.VMEM((picked, width), BF16),
        pltpu.VMEM((picked, table), BF16),
        pltpu.VMEM((all_rows, table), BF16),
        pltpu.VMEM((3, chunk, ff), BF16),
        pltpu.VMEM((all_rows, chunk), BF16),
        pltpu.VMEM((all_rows, chunk), BF16),
        pltpu.VMEM((all_rows, chunk), BF16),
        pltpu.VMEM((experts, all_rows, chunk), BF16),
        pltpu.VMEM((steps, unit, 2 * fw), F32),
        pltpu.VMEM((2, steps, unit, 2 * fw), BF16),
        pltpu.VMEM((2, steps, unit, 2 * fw), BF16),
        pltpu.VMEM((back_steps, unit, ff // split), F32),
        pltpu.VMEM((2, back_steps, unit, ff // split), BF16),
        pltpu.VMEM((2, back_steps, unit, ff // split), BF16),
        pltpu.VMEM((all_rows, ff), BF16),
        pltpu.VMEM((2, all_rows, ff), BF16),
        pltpu.VMEM((all_rows, chunk), BF16),
        pltpu.VMEM((picked, width), BF16),
        pltpu.VMEM((all_rows, half), BF16),
        pltpu.VMEM((all_rows, half), BF16),
        pltpu.VMEM((all_rows, ff), BF16),
        pltpu.VMEM((2, all_rows, ff), BF16),
        dma((planes,)), dma, dma((3,)), dma((3,)), dma((3,)),
        dma((4,)), dma((4, planes)), dma, dma((planes * parts,)),
        dma((2,)), dma((2, steps)), dma((2,)), dma((2, back_steps)),
        dma((5,)), dma((5,)),
    ]


def held_bytes(scratch):
    return sum(
        math.prod(s.shape) * jnp.dtype(s.dtype).itemsize
        for s in scratch
        if getattr(s, "memory_space", None) == pltpu.VMEM
    )


def on_device(
    tokens, target, route_index, route_count, route_gate, gate_weight, up_weight, down_weight
):
    groups = lax.axis_size("dp")
    experts = lax.axis_size("expert")
    planes = groups // CORES
    slots = route_index.shape[3]
    count, width = tokens.shape
    half, _, ff = gate_weight.shape
    picked = experts * slots
    factor = (groups * experts * slots) ** (-0.5)
    pieces, split = (
        max(n for n in range(1, most + 1) if ff % (128 * n) == 0)
        for most in (PIECES, BACK_PIECES)
    )
    vmem = pl.BlockSpec(memory_space=pltpu.VMEM)
    anyw = pl.BlockSpec(memory_space=pl.ANY)
    grad = jax.ShapeDtypeStruct((half, ff), F32)
    parts = PARTS if experts % PARTS == 0 else 1
    scratch = chain_scratch(
        planes, experts, picked, count, width, half, ff, pieces, split, parts
    )
    body = functools.partial(chain_kernel, planes, experts, slots, factor, pieces, parts)
    out, limit, small = vmem, CHAIN_LIMIT, anyw
    if held_bytes(scratch) > CHAIN_LIMIT * 3 // 4:
        scratch = direct_scratch(planes, picked, count, width, half, ff)
        body = functools.partial(direct_kernel, planes, experts, slots, factor)
        out, limit, small = anyw, VMEM_LIMIT, vmem
    came_back, hot, gate_gradient, up_gradient, down_gradient = pl.pallas_call(
        body,
        out_shape=(
            jax.ShapeDtypeStruct((picked, width), BF16),
            jax.ShapeDtypeStruct((picked, count), BF16),
            grad, grad, grad,
        ),
        in_specs=[small] * 3 + [anyw] * 5,
        out_specs=(out, vmem, out, out, out),
        scratch_shapes=scratch,
        compiler_params=pltpu.CompilerParams(
            collective_id=0, has_side_effects=True, vmem_limit_bytes=limit
        ),
        name="routed_layer",
    )(
        *(
            pltpu.with_memory_space_constraint(x, pltpu.MemorySpace.HBM)
            for x in (
                route_index, route_count.reshape(1, experts), route_gate, tokens, target, gate_weight.reshape(half, ff), up_weight.reshape(half, ff),
                down_weight.reshape(half, ff),
            )
        ),
    )
    blocks = max(n for n in range(1, 9) if count % (128 * n) == 0)
    grad = jax.ShapeDtypeStruct((half, 1, ff), F32)
    return tuple(pl.pallas_call(
        finish,
        out_shape=(jax.ShapeDtypeStruct((count, width), BF16), grad, grad, grad),
        in_specs=[vmem] * 5,
        out_specs=[anyw] * 4,
        scratch_shapes=[
            pltpu.VMEM((count, width), BF16),
            pltpu.SemaphoreType.DMA((blocks,)), pltpu.SemaphoreType.DMA((3,)),
        ],
        compiler_params=pltpu.CompilerParams(vmem_limit_bytes=FINISH_LIMIT),
        name="finish",
    )(hot, came_back, gate_gradient, up_gradient, down_gradient))


def solution(mesh):
    return jax.shard_map(
        on_device,
        mesh=mesh,
        in_specs=(
            P(("dp", "expert"), None),
            P(("dp", "expert"), None),
            P("dp", None, "expert", None),
            P("dp", None, "expert"),
            P("dp", None, "expert", None),
            P("dp", "expert", None),
            P("dp", "expert", None),
            P("dp", "expert", None),
        ),
        out_specs=(
            P(("dp", "expert"), None),
            P("dp", "expert", None),
            P("dp", "expert", None),
            P("dp", "expert", None),
        ),
        check_vma=False,
    )
```

```python
import contextlib
import functools
import math

import jax
import jax.numpy as jnp
from jax import lax
from jax.experimental import pallas as pl
from jax.experimental.pallas import tpu as pltpu
from jax.sharding import PartitionSpec as P

F32 = jnp.float32
BF16 = jnp.bfloat16
VMEM_LIMIT = 67000000
CORES = 2
PIECES = 3
BACK_PIECES = 3
PARTS = 2
LAG = 5
LAG_PLANE = 6
LAG_BACK = 6
LAG_GRADS = 0
LATE = False
TURNS = (1, 0)
OUTER_FIRST = False
CHAIN_LIMIT = 44000000
FINISH_LIMIT = 40000000


def dot(a, b, dims, precision=None):
    return lax.dot_general(
        a, b, (dims, ((), ())), preferred_element_type=F32, precision=precision
    )


def scope(name):
    return contextlib.nullcontext()


NN = ((1,), (0,))
NT = ((1,), (1,))
TN = ((0,), (0,))


def direct_kernel(
    planes, experts, slots, factor,
    index, count, gate, tokens, target, gw, uw, dw,
    cb_out, hot_out, gg_out, ug_out, dg_out,
    TOK, TGT, ROWS, TROWS, W, R, EO, RET, SG, G, RG, CB, PS, PR, H, GU, RX, GX, HX, GUX,
    t_loc, g_loc, w_loc, w_send, w_recv, a_loc, a_send, a_recv, p_send, p_recv,
    h_send, h_recv, x_send, x_recv, GRADS, o_loc,
):
    dp = lax.axis_index("dp")
    me_e = lax.axis_index("expert")
    me_z = dp // CORES
    core = dp % CORES
    peers = planes * experts
    per_group = experts * slots
    half = gw.shape[0]
    chunk = CORES * half
    ff = gw.shape[1]
    me = me_z * experts + me_e
    sibling = {"dp": me_z * CORES + (1 - core), "expert": me_e}
    order = sorted(range(1, planes), key=lambda k: -min(k, planes - k))

    def at(z, e):
        return {"dp": z * CORES + core, "expert": e}

    def plane(k):
        return (me_z + k) % planes

    def slot_rows(n):
        return pl.ds(pl.multiple_of(n * slots, slots), slots)

    def cols(z):
        return pl.ds(pl.multiple_of(z * chunk, chunk), chunk)

    def group_rows(z):
        return pl.ds(pl.multiple_of(z * per_group, per_group), per_group)

    barrier = pltpu.get_barrier_semaphore()

    def greet(k, carry):
        p = (me + k) % peers
        pl.semaphore_signal(
            barrier, inc=1, device_id=at(p // experts, p % experts),
            device_id_type=pl.DeviceIdType.MESH,
        )
        return carry

    lax.fori_loop(1, peers, greet, 0)
    pl.semaphore_signal(
        barrier, inc=1, device_id=sibling, device_id_type=pl.DeviceIdType.MESH
    )
    tok_copies = {}
    for k in order + [0]:
        z = plane(k)
        tok_copies[k] = pltpu.make_async_copy(
            tokens.at[:, cols(z)], TOK.at[:, cols(z)], t_loc.at[k]
        )
        tok_copies[k].start()
    locals_w = []
    for i, w in enumerate((gw, uw, dw)):
        c = pltpu.make_async_copy(w, W.at[i, core], w_loc.at[i])
        c.start()
        locals_w.append(c)
    tgt_copy = pltpu.make_async_copy(target, TGT, g_loc)
    tgt_copy.start()

    lane = lax.broadcasted_iota(jnp.int32, (slots, slots), 1)
    own_lane = lane == lax.broadcasted_iota(jnp.int32, (slots, slots), 0)
    slot_id = lax.broadcasted_iota(jnp.int32, (slots, 1), 0)
    names, weights = [], []
    for e in range(experts):
        live = slot_id < jnp.broadcast_to(count[0:1, e : e + 1], (slots, 1))
        ids = jnp.broadcast_to(index[0, e], (slots, slots))
        ids = jnp.sum(jnp.where(own_lane, ids, 0), axis=1, keepdims=True)
        names.append(jnp.where(live, ids, -1))
        g = jnp.broadcast_to(gate[0, e], (slots, slots))
        g = jnp.sum(jnp.where(own_lane, g, 0.0), axis=1, keepdims=True)
        weights.append(jnp.where(live, g, 0.0))
    names = jnp.concatenate(names, axis=0)
    wcol = jnp.concatenate(weights, axis=0)
    hot = (
        names == lax.broadcasted_iota(jnp.int32, (per_group, TOK.shape[0]), 1)
    ).astype(F32).astype(BF16)
    hot_out[...] = hot

    def remote(src, dst, s, r, dev):
        c = pltpu.make_async_remote_copy(
            src_ref=src, dst_ref=dst, send_sem=s, recv_sem=r,
            device_id=dev, device_id_type=pl.DeviceIdType.MESH,
        )
        c.start()
        return c

    def to_plane(i, z, source, land):
        here = z == me_z

        @pl.when(here)
        def _():
            pltpu.make_async_copy(source(me_z, me_e), land, a_loc.at[i]).start()

        first = jnp.where(here, 1, 0)

        def send(j, carry):
            e = (me_e + j) % experts
            remote(source(z, e), land, a_send.at[i], a_recv.at[i, me_z], at(z, e))
            return carry

        lax.fori_loop(first, experts, send, 0)

    def owners(src, dst, i, z):
        to_plane(i, z, lambda z, e: src.at[slot_rows(e), cols(z)], dst.at[slot_rows(me)])

    def sources(src, dst, i, z):
        to_plane(
            i, z, lambda z, e: src.at[slot_rows(z * experts + e)],
            dst.at[slot_rows(me_e), cols(me_z)],
        )

    def take(sem, ref):
        pltpu.make_async_copy(ref, ref, sem).wait()

    def arrived(i, k):
        if k == 0:
            take(a_recv.at[i, me_z], R.at[pl.ds(0, (experts - 1) * slots)])
            take(a_loc.at[i], R.at[pl.ds(0, slots)])
        else:
            take(a_recv.at[i, plane(k)], R.at[pl.ds(0, per_group)])

    outs = []

    def put(i, src, dst):
        c = pltpu.make_async_copy(src, dst, o_loc.at[i])
        c.start()
        outs.append(c)

    def weight(i):
        return W[i].reshape(chunk, ff)

    pl.semaphore_wait(barrier, peers)
    for k in order + [0]:
        z = plane(k)
        tok_copies[k].wait()
        ROWS[:, cols(z)] = dot(hot, TOK[:, cols(z)], NN).astype(BF16)
        owners(ROWS, R, 0, z)
    sent_w = [
        remote(w, W.at[i, core], w_send.at[i], w_recv.at[i], sibling)
        for i, w in enumerate((gw, uw, dw))
    ]

    def send_sum(i, k):
        remote(
            PS.at[i, group_rows(plane(k))], PR.at[i, k - 1],
            p_send.at[i], p_recv.at[i, k - 1], at(plane(k), me_e),
        )

    def pass_on(buf, i, s, way):
        to = me_z + way

        @pl.when(jnp.logical_and(to >= 0, to < planes))
        def _():
            rows_s = buf.at[group_rows(s)]
            remote(
                rows_s, rows_s, h_send.at[i, (way + 1) // 2, s], h_recv.at[i, s],
                at(to, me_e),
            )

    def spread(buf, i):
        for way in (1, -1):
            pass_on(buf, i, me_z, way)

    def along(bufs, first, fn):
        fn(me_z)
        for far in range(1, planes):
            for way in (1, -1):
                s = me_z - way * far

                @pl.when(jnp.logical_and(s >= 0, s < planes))
                def _():
                    for j, buf in enumerate(bufs):
                        take(h_recv.at[first + j, s], buf.at[group_rows(s)])
                        pass_on(buf, first + j, s, way)
                    fn(s)

    def spread_sent(buf, i):
        for s in range(planes):
            rows_s = buf.at[pl.ds(s * per_group, per_group)]

            @pl.when(jnp.logical_and(me_z > 0, me_z <= s))
            def _():
                take(h_send.at[i, 0, s], rows_s)

            @pl.when(jnp.logical_and(me_z < planes - 1, me_z >= s))
            def _():
                take(h_send.at[i, 1, s], rows_s)

    def total(i, own):
        for k in order:
            take(p_recv.at[i, k - 1], PR.at[i, k - 1])
            own = own + PR[i, k - 1].astype(F32)
        return own

    keep = pl.ds(pl.multiple_of(core * half, half), half)
    give = pl.ds(pl.multiple_of((1 - core) * half, half), half)
    mine = group_rows(me_z)

    for i in range(2):
        locals_w[i].wait()
        sent_w[i].wait_recv()
    for k in order:
        z = plane(k)
        arrived(0, k)
        for i in range(2):
            PS[i, group_rows(z), :] = dot(R[group_rows(z), :], weight(i), NN).astype(BF16)
            send_sum(i, k)
    arrived(0, 0)
    gate_own = dot(R[mine, :], weight(0), NN)
    up_own = dot(R[mine, :], weight(1), NN)
    x_rows = remote(R.at[:, give], RX, x_send.at[0], x_recv.at[0], sibling)
    tgt_copy.wait()
    for z in range(planes):
        piece = slice(z * chunk, (z + 1) * chunk)
        TROWS[:, piece] = dot(hot, TGT[:, piece], NN)
    same = dot(hot, hot, NT).astype(BF16)
    gate_pre = total(0, gate_own)
    up_pre = total(1, up_own)
    sigma = jax.nn.sigmoid(gate_pre)
    active = gate_pre * sigma
    H[mine, :] = (active * up_pre).astype(BF16)
    spread(H, 0)
    locals_w[2].wait()
    sent_w[2].wait_recv()

    def expert_out(z):
        EO[group_rows(z), :] = dot(H[group_rows(z), :], weight(2), NT).astype(BF16)
        sources(EO, RET, 1, z)

    along([H], 0, expert_out)
    x_hidden = remote(H, HX, x_send.at[1], x_recv.at[1], sibling)
    for k in order + [0]:
        z = plane(k)
        arrived(1, k)
        part = wcol * RET[:, cols(z)].astype(F32)
        combined = -TROWS[:, cols(z)]
        for _ in range(3):
            top = part.astype(BF16)
            combined = combined + dot(same, top, NN)
            part = part - top.astype(F32)
        SG[:, cols(z)] = (wcol * combined).astype(BF16)
        owners(SG, G, 2, z)

    for k in order:
        z = plane(k)
        arrived(2, k)
        PS[2, group_rows(z), :] = dot(G[group_rows(z), :], weight(2), NN).astype(BF16)
        send_sum(2, k)
    arrived(2, 0)
    own = dot(G[mine, :], weight(2), NN)
    x_grad = remote(G.at[:, give], GX, x_send.at[2], x_recv.at[2], sibling)
    x_hidden.wait_recv()
    x_grad.wait_recv()
    GRADS[2] = (dot(G[:, keep], H[...], TN) + dot(GX[...], HX[...], TN)) * factor
    put(2, GRADS.at[2], dg_out)
    hidden_grad = total(2, own)
    GU[0, mine, :] = (
        hidden_grad * up_pre * sigma * (1.0 + gate_pre * (1.0 - sigma))
    ).astype(BF16)
    spread(GU.at[0], 1)
    GU[1, mine, :] = (hidden_grad * active).astype(BF16)
    spread(GU.at[1], 2)

    def row_grad(z):
        RG[group_rows(z), :] = (
            dot(GU[0, group_rows(z), :], weight(0), NT)
            + dot(GU[1, group_rows(z), :], weight(1), NT)
        ).astype(BF16)
        sources(RG, CB, 3, z)

    along([GU.at[0], GU.at[1]], 1, row_grad)
    x_gate = remote(GU.at[0], GUX.at[0], x_send.at[3], x_recv.at[3], sibling)
    x_up = remote(GU.at[1], GUX.at[1], x_send.at[4], x_recv.at[4], sibling)
    x_rows.wait_recv()
    x_gate.wait_recv()
    GRADS[0] = (dot(R[:, keep], GU[0], TN) + dot(RX[...], GUX[0], TN)) * factor
    put(0, GRADS.at[0], gg_out)
    x_up.wait_recv()
    GRADS[1] = (dot(R[:, keep], GU[1], TN) + dot(RX[...], GUX[1], TN)) * factor
    put(1, GRADS.at[1], ug_out)
    for k in order + [0]:
        arrived(3, k)
    put(3, CB, cb_out)

    for c in sent_w + [x_rows, x_hidden, x_grad, x_gate, x_up]:
        c.wait_send()
    for i in range(4):
        take(a_send.at[i], R.at[pl.ds(0, (peers - 1) * slots)])
    for i in range(3):
        take(p_send.at[i], PR.at[i])
    for i, buf in enumerate((H, GU.at[0], GU.at[1])):
        spread_sent(buf, i)
    for c in outs:
        c.wait()


def chain_kernel(
    planes, experts, slots, factor, pieces, parts,
    index_in, count_in, gate_in, tokens, target, gw, uw, dw,
    cb_out, hot_out, gg_out, ug_out, dg_out,
    index, count, gate, r_loc, TOK, TGT, ROWS, TROWS, META, MT, W, WT, R, TR, G, EOG,
    OWN, IN, OUT, HOWN, HIN, HOUT, H, GU, RG, CB, RX, GX, HX, GUX,
    t_loc, g_loc, w_loc, w_send, w_recv, a_send, a_recv, e_send, e_recv,
    c_send, c_recv, h_send, h_recv, x_send, x_recv,
):
    dp = lax.axis_index("dp")
    me_e = lax.axis_index("expert")
    me_z = dp // CORES
    core = dp % CORES
    peers = planes * experts
    per_group = experts * slots
    half = gw.shape[0]
    chunk = CORES * half
    ff = gw.shape[1]
    fw = ff // pieces
    split = HIN.shape[1] // (planes * parts)
    unit = per_group // parts
    hw = ff // split
    me = me_z * experts + me_e
    sibling = {"dp": me_z * CORES + (1 - core), "expert": me_e}
    ways = (1, -1)
    side = jnp.where(2 * me_z < planes, 1, -1)
    far_first = sorted(range(1, planes), key=lambda k: abs(k - planes / 2)) + [0]
    dist = (me_z, planes - 1 - me_z)
    depth = jnp.maximum(dist[0], dist[1])

    def at(z, e):
        return {"dp": z * CORES + core, "expert": e}

    def plane(k):
        return (me_z + side * k + planes) % planes

    def slot_rows(n):
        return pl.ds(pl.multiple_of(n * slots, slots), slots)

    def cols(z):
        return pl.ds(pl.multiple_of(z * chunk, chunk), chunk)

    def group_rows(z):
        return pl.ds(pl.multiple_of(z * per_group, per_group), per_group)

    def unit_rows(n):
        rows = turn(n // parts) * per_group + n % parts * unit
        return pl.ds(pl.multiple_of(rows, unit), unit)

    def turn(g):
        if planes % 2:
            return g
        g = planes - 1 - g if OUTER_FIRST else g
        return planes // 2 - 1 - g // 2 + (g % 2) * (2 * (g // 2) + 1)

    barrier = pltpu.get_barrier_semaphore()

    def greet(k, carry):
        p = (me + k) % peers
        pl.semaphore_signal(
            barrier, inc=1, device_id=at(p // experts, p % experts),
            device_id_type=pl.DeviceIdType.MESH,
        )
        return carry

    lax.fori_loop(1, peers, greet, 0)
    pl.semaphore_signal(
        barrier, inc=1, device_id=sibling, device_id_type=pl.DeviceIdType.MESH
    )
    routes = [
        pltpu.make_async_copy(src, dst, r_loc.at[i])
        for i, (src, dst) in enumerate(
            ((index_in, index), (count_in, count), (gate_in, gate))
        )
    ]
    for c in routes:
        c.start()
    tok_copies = {}
    for k in far_first:
        tok_copies[k] = pltpu.make_async_copy(
            tokens.at[:, cols(plane(k))], TOK.at[:, cols(plane(k))], t_loc.at[k]
        )
        tok_copies[k].start()
    locals_w = []
    keep = pl.ds(pl.multiple_of(core * half, half), half)
    give = pl.ds(pl.multiple_of((1 - core) * half, half), half)
    for i, w in enumerate((gw, uw, dw)):
        c = pltpu.make_async_copy(w, W.at[i, keep], w_loc.at[i])
        c.start()
        locals_w.append(c)
    tgt_copy = pltpu.make_async_copy(target, TGT, g_loc)
    tgt_copy.start()

    for c in routes:
        c.wait()
    lane = lax.broadcasted_iota(jnp.int32, (slots, slots), 1)
    own_lane = lane == lax.broadcasted_iota(jnp.int32, (slots, slots), 0)
    slot_id = lax.broadcasted_iota(jnp.int32, (slots, 1), 0)
    names, weights = [], []
    for e in range(experts):
        live = slot_id < jnp.broadcast_to(count[0:1, e : e + 1], (slots, 1))
        ids = jnp.broadcast_to(index[0, e], (slots, slots))
        ids = jnp.sum(jnp.where(own_lane, ids, 0), axis=1, keepdims=True)
        names.append(jnp.where(live, ids, -1))
        g = jnp.broadcast_to(gate[0, e], (slots, slots))
        g = jnp.sum(jnp.where(own_lane, g, 0.0), axis=1, keepdims=True)
        weights.append(jnp.where(live, g, 0.0))
    names = jnp.concatenate(names, axis=0)
    wcol = jnp.concatenate(weights, axis=0)
    hot = (
        names == lax.broadcasted_iota(jnp.int32, (per_group, TOK.shape[0]), 1)
    ).astype(F32).astype(BF16)
    hot_out[...] = hot

    def remote(src, dst, s, r, dev):
        c = pltpu.make_async_remote_copy(
            src_ref=src, dst_ref=dst, send_sem=s, recv_sem=r,
            device_id=dev, device_id_type=pl.DeviceIdType.MESH,
        )
        c.start()
        return c

    def take(sem, ref):
        pltpu.make_async_copy(ref, ref, sem).wait()

    def to_plane(i, z, source, land):
        here = z == me_z

        @pl.when(here)
        def _():
            pltpu.make_async_copy(source(me_z, me_e), land, a_recv.at[i, me_z]).start()

        def send(j, carry):
            e = (me_e + j) % experts
            remote(source(z, e), land, a_send.at[i], a_recv.at[i, me_z], at(z, e))
            return carry

        lax.fori_loop(jnp.where(here, 1, 0), experts, send, 0)

    for k in far_first:
        z = plane(k)
        tok_copies[k].wait()
        ROWS[:, cols(z)] = dot(hot, TOK[:, cols(z)], NN).astype(BF16)
    for way, d in zip(ways, range(2)):
        @pl.when(dist[d] == 0)
        def _():
            IN[d] = jnp.zeros(IN.shape[1:], BF16)
            HIN[d] = jnp.zeros(HIN.shape[1:], BF16)

    with scope("barrier"):
        pl.semaphore_wait(barrier, peers)
    sent_w = [
        remote(w, W.at[i, keep], w_send.at[i], w_recv.at[i], sibling)
        for i, w in enumerate((gw, uw, dw))
    ]
    for k in far_first:
        to_plane(
            0, plane(k), lambda z, e: ROWS.at[slot_rows(e), cols(z)], R.at[slot_rows(me)]
        )
    with scope("trows"):
        tgt_copy.wait()
        for k in far_first:
            z = plane(k)
            TROWS[:, cols(z)] = dot(hot, TGT[:, cols(z)], NN).astype(BF16)
    with scope("meta"):
        square = (per_group, per_group)
        eye = lax.broadcasted_iota(jnp.int32, square, 0) == lax.broadcasted_iota(
            jnp.int32, square, 1
        )
        wrow = jnp.sum(jnp.where(eye, wcol, 0.0), axis=0, keepdims=True)
        mix = dot(hot, hot, NT) * wrow
        top = mix.astype(BF16)
        if META.shape[1] > 2 * per_group:
            META[...] = jnp.zeros(META.shape, BF16)
        META[:, 0:per_group] = top
        META[:, per_group : 2 * per_group] = (mix - top.astype(F32)).astype(BF16)

    with scope("w_wait"):
        for i in range(3):
            locals_w[i].wait()
            sent_w[i].wait_recv()
    with scope("wt"):
        for i in range(3):
            WT[i] = W[i].T

    def piece(f):
        return pl.ds(pl.multiple_of(f * fw, fw), fw)

    def partial_sums(c):
        n, f = c // pieces, c % pieces

        @pl.when(c % (pieces * parts) == 0)
        def _():
            with scope("x_wait"):
                take(a_recv.at[0, turn(n // parts)], R.at[pl.ds(0, per_group)])

        with scope("own"):
            rows = R[unit_rows(n), :]
            for i in range(2):
                OWN[c, :, i * fw : (i + 1) * fw] = dot(rows, W[i, :, piece(f)], NN)

    def move(own, inn, out, send, recv, d, c):
        @pl.when(dist[d] > 0)
        def _():
            with scope("mv%d" % (own is HOWN)):
                take(recv.at[d, c], inn.at[d, c])

        @pl.when(dist[d] < planes - 1)
        def _():
            out[d, c] = (own[c] + inn[d, c].astype(F32)).astype(BF16)
            remote(
                out.at[d, c], inn.at[d, c], send.at[d], recv.at[d, c],
                at(me_z + ways[d], me_e),
            )

    def total(own, inn, c):
        return own[c] + inn[0, c].astype(F32) + inn[1, c].astype(F32)

    def to_sibling(i, src, dst):
        remote(src, dst, x_send.at[i], x_recv.at[i], sibling)

    def forward(c):
        n, f = c // pieces, c % pieces
        rows = unit_rows(n)
        with scope("fwd"):
            both = total(OWN, IN, c)
            OWN[c] = both
            pre, up = both[:, :fw], both[:, fw:]
            H[rows, piece(f)] = (pre * jax.nn.sigmoid(pre) * up).astype(BF16)

        @pl.when(f == pieces - 1)
        def _():
            with scope("eo"):
                EOG[me_e, rows, :] = dot(H[rows, :], WT[2], NN).astype(BF16)
                outs = EOG.at[me_e, rows]

                def send(j, carry):
                    remote(
                        outs, outs, e_send, e_recv.at[n], at(me_z, (me_e + j) % experts)
                    )
                    return carry

                lax.fori_loop(1, experts, send, 0)
                to_sibling(1, H.at[rows], HX.at[rows])

    spread = (slots, 2 * per_group)
    own_slot = (
        lax.broadcasted_iota(jnp.int32, spread, 1) % per_group
        == lax.broadcasted_iota(jnp.int32, spread, 0) + me_e * slots
    )

    def slot_grads(n):
        z = turn(n // parts)
        rows = unit_rows(n)
        with scope("eo_wait"):
            take(e_recv.at[n], EOG.at[pl.ds(0, experts - 1), pl.ds(0, unit)])

            @pl.when(n % parts == 0)
            def _():
                take(a_recv.at[1, z], TR.at[pl.ds(0, per_group)])
                take(a_recv.at[2, z], MT.at[pl.ds(0, per_group)])
        with scope("comb"):
            for s in range(experts // parts):
                mine = slot_rows(z * experts + n % parts * (experts // parts) + s)
                outs = [EOG[e, mine, :] for e in range(experts)]
                table = MT[mine, 0 : 2 * per_group]
                wide = dot(table, jnp.concatenate(outs + outs, axis=0), NN)
                w = jnp.sum(
                    jnp.where(own_slot, table.astype(F32), 0.0), axis=1, keepdims=True
                )
                G[mine, :] = (w * (wide - TR[mine, :].astype(F32))).astype(BF16)
            for i in range(split):
                HOWN[n * split + i] = dot(G[rows, :], W[2, :, i * hw : (i + 1) * hw], NN)
            to_sibling(2, G.at[rows, give], GX.at[rows])

    def backward(n):
        rows = unit_rows(n)
        with scope("bwd"):
            hidden_grad = jnp.concatenate(
                [total(HOWN, HIN, n * split + i) for i in range(split)], axis=1
            )
            for f in range(pieces):
                both = OWN[n * pieces + f]
                pre, up = both[:, :fw], both[:, fw:]
                grad = hidden_grad[:, f * fw : (f + 1) * fw]
                sigma = jax.nn.sigmoid(pre)
                GU[0, rows, f * fw : (f + 1) * fw] = (
                    grad * up * sigma * (1.0 + pre * (1.0 - sigma))
                ).astype(BF16)
                GU[1, rows, f * fw : (f + 1) * fw] = (grad * (pre * sigma)).astype(BF16)
            RG[rows, :] = (
                dot(GU[0, rows, :], WT[0], NN) + dot(GU[1, rows, :], WT[1], NN)
            ).astype(BF16)
            send_rows(n)
            for i in range(2):
                to_sibling(3 + i, GU.at[i, rows], GUX.at[i, rows])

    def send_rows(n):
        z, share = turn(n // parts), experts // parts
        land = CB.at[slot_rows(me_e), cols(me_z)]

        def send(j, carry):
            e = n % parts * share + j
            rows = RG.at[slot_rows(z * experts + e)]
            here = jnp.logical_and(z == me_z, e == me_e)

            @pl.when(here)
            def _():
                pltpu.make_async_copy(rows, land, a_recv.at[3, me_z]).start()

            @pl.when(jnp.logical_not(here))
            def _():
                remote(rows, land, a_send.at[3], a_recv.at[3, me_z], at(z, e))

            return carry

        lax.fori_loop(0, share, send, 0)

    steps = planes * parts * pieces
    back_steps = planes * parts * split
    begin = pieces - 1 + LAG * (planes - 1) + LAG_PLANE
    begin += max(0, pieces - split) * (planes * parts - 1)

    def each(t, fn, last):
        @pl.when(jnp.logical_and(t >= 0, t < last))
        def _():
            fn(t)

    def each_group(t, fn):
        fits = jnp.logical_and(t >= 0, t < back_steps)

        @pl.when(jnp.logical_and(fits, t % split == 0))
        def _():
            fn(t // split)

    def grad(i, left, left_x, right, right_x, out):
        out[...] = (dot(left, right, TN) + dot(left_x, right_x, TN)) * factor

    def send_targets(z):
        to_plane(2, z, lambda z, e: META.at[slot_rows(e)], MT.at[slot_rows(me)])
        to_plane(
            1, z, lambda z, e: TROWS.at[slot_rows(e), cols(z)], TR.at[slot_rows(me)]
        )

    for k in far_first:
        send_targets(plane(k))

    def tick(t, carry):
        each(t, partial_sums, steps)
        for d in TURNS:
            each(
                t - LAG * dist[d],
                functools.partial(move, OWN, IN, OUT, c_send, c_recv, d), steps,
            )
        each(t - LAG * depth, forward, steps)
        t = t - begin
        each_group(t, slot_grads)
        for d in TURNS:
            each(
                t - LAG_BACK * dist[d],
                functools.partial(move, HOWN, HIN, HOUT, h_send, h_recv, d), back_steps,
            )
        back = t - LAG_BACK * (planes - 1 if LATE else depth) - (split - 1) - LAG_GRADS
        each_group(back, backward)
        return carry

    middle = begin + back_steps + 1
    lax.fori_loop(0, middle, tick, 0)
    to_sibling(0, R.at[:, give], RX)
    with scope("dgrad"):
        take(x_recv.at[1], HX)
        take(x_recv.at[2], GX)
        grad(2, G[:, keep], GX[...], H[...], HX[...], dg_out)
    lax.fori_loop(
        middle, begin + back_steps + LAG_BACK * (planes - 1) + LAG_GRADS + split, tick, 0
    )
    with scope("xg"):
        take(x_recv.at[0], RX)
        take(x_recv.at[3], GUX.at[0])
        take(x_recv.at[4], GUX.at[1])
    with scope("gugrad"):
        grad(0, R[:, keep], RX[...], GU[0], GUX[0], gg_out)
        grad(1, R[:, keep], RX[...], GU[1], GUX[1], ug_out)
    with scope("cb_wait"):
        for k in far_first:
            take(a_recv.at[3, plane(k)], R.at[pl.ds(0, per_group)])
    with scope("tail"):
        cb_out[...] = CB[...]
        for c in sent_w:
            c.wait_send()
        others = pl.ds(0, (peers - 1) * slots)
        for i, buf in enumerate((R, TR, MT, RG)):
            take(a_send.at[i], buf.at[others])
        take(e_send, EOG.at[pl.ds(0, experts - 1)])
        for d in range(2):
            @pl.when(dist[d] < planes - 1)
            def _():
                take(c_send.at[d], OUT.at[d])
                take(h_send.at[d], HOUT.at[d])
        for i, buf in enumerate((RX, HX, GX, GUX.at[0], GUX.at[1])):
            take(x_send.at[i], buf)


def finish(hot, cb, gg, ug, dg, tg_out, gg_out, ug_out, dg_out, TG, t_sem, g_sem):
    copies = []
    for i, (grad, out) in enumerate(((gg, gg_out), (ug, ug_out), (dg, dg_out))):
        copies.append(pltpu.make_async_copy(grad, out.at[:, 0, :], g_sem.at[i]))
        copies[-1].start()
    parts = t_sem.shape[0]
    step = TG.shape[0] // parts
    for j in range(parts):
        rows = slice(j * step, (j + 1) * step)
        TG[rows, :] = dot(hot[:, rows], cb[...], TN).astype(BF16)
        copies.append(pltpu.make_async_copy(TG.at[rows], tg_out.at[rows], t_sem.at[j]))
        copies[-1].start()
    for c in copies:
        c.wait()


def direct_scratch(planes, picked, count, width, half, ff):
    chunk = CORES * half
    all_rows = planes * picked
    dma = pltpu.SemaphoreType.DMA
    return [
        pltpu.VMEM((count, width), BF16),
        pltpu.VMEM((count, width), BF16),
        pltpu.VMEM((picked, width), BF16),
        pltpu.VMEM((picked, width), F32),
        pltpu.VMEM((3, CORES, half, ff), BF16),
        pltpu.VMEM((all_rows, chunk), BF16),
        pltpu.VMEM((all_rows, chunk), BF16),
        pltpu.VMEM((picked, width), BF16),
        pltpu.VMEM((picked, width), BF16),
        pltpu.VMEM((all_rows, chunk), BF16),
        pltpu.VMEM((all_rows, chunk), BF16),
        pltpu.VMEM((picked, width), BF16),
        pltpu.VMEM((3, all_rows, ff), BF16),
        pltpu.VMEM((3, planes - 1, picked, ff), BF16),
        pltpu.VMEM((all_rows, ff), BF16),
        pltpu.VMEM((2, all_rows, ff), BF16),
        pltpu.VMEM((all_rows, half), BF16),
        pltpu.VMEM((all_rows, half), BF16),
        pltpu.VMEM((all_rows, ff), BF16),
        pltpu.VMEM((2, all_rows, ff), BF16),
        dma((planes,)), dma,
        dma((3,)), dma((3,)), dma((3,)),
        dma((4,)), dma((4,)), dma((4, planes)),
        dma((3,)), dma((3, planes)),
        dma((3, 2, planes)), dma((3, planes)),
        dma((5,)), dma((5,)),
        pltpu.VMEM((3, half, ff), F32), dma((4,)),
    ]


def chain_scratch(planes, experts, picked, count, width, half, ff, pieces, split, parts):
    slots = picked // experts
    chunk = CORES * half
    all_rows = planes * picked
    steps = planes * parts * pieces
    back_steps = planes * parts * split
    unit = picked // parts
    fw = ff // pieces
    table = -(-2 * picked // 128) * 128
    dma = pltpu.SemaphoreType.DMA
    return [
        pltpu.VMEM((1, experts, 1, slots), jnp.int32),
        pltpu.VMEM((1, experts), jnp.int32),
        pltpu.VMEM((1, experts, 1, slots), F32),
        dma((3,)),
        pltpu.VMEM((count, width), BF16),
        pltpu.VMEM((count, width), BF16),
        pltpu.VMEM((picked, width), BF16),
        pltpu.VMEM((picked, width), BF16),
        pltpu.VMEM((picked, table), BF16),
        pltpu.VMEM((all_rows, table), BF16),
        pltpu.VMEM((3, chunk, ff), BF16),
        pltpu.VMEM((3, ff, chunk), BF16),
        pltpu.VMEM((all_rows, chunk), BF16),
        pltpu.VMEM((all_rows, chunk), BF16),
        pltpu.VMEM((all_rows, chunk), BF16),
        pltpu.VMEM((experts, all_rows, chunk), BF16),
        pltpu.VMEM((steps, unit, 2 * fw), F32),
        pltpu.VMEM((2, steps, unit, 2 * fw), BF16),
        pltpu.VMEM((2, steps, unit, 2 * fw), BF16),
        pltpu.VMEM((back_steps, unit, ff // split), F32),
        pltpu.VMEM((2, back_steps, unit, ff // split), BF16),
        pltpu.VMEM((2, back_steps, unit, ff // split), BF16),
        pltpu.VMEM((all_rows, ff), BF16),
        pltpu.VMEM((2, all_rows, ff), BF16),
        pltpu.VMEM((all_rows, chunk), BF16),
        pltpu.VMEM((picked, width), BF16),
        pltpu.VMEM((all_rows, half), BF16),
        pltpu.VMEM((all_rows, half), BF16),
        pltpu.VMEM((all_rows, ff), BF16),
        pltpu.VMEM((2, all_rows, ff), BF16),
        dma((planes,)), dma, dma((3,)), dma((3,)), dma((3,)),
        dma((4,)), dma((4, planes)), dma, dma((planes * parts,)),
        dma((2,)), dma((2, steps)), dma((2,)), dma((2, back_steps)),
        dma((5,)), dma((5,)),
    ]


def held_bytes(scratch):
    return sum(
        math.prod(s.shape) * jnp.dtype(s.dtype).itemsize
        for s in scratch
        if getattr(s, "memory_space", None) == pltpu.VMEM
    )


def on_device(
    tokens, target, route_index, route_count, route_gate, gate_weight, up_weight, down_weight
):
    groups = lax.axis_size("dp")
    experts = lax.axis_size("expert")
    planes = groups // CORES
    slots = route_index.shape[3]
    count, width = tokens.shape
    half, _, ff = gate_weight.shape
    picked = experts * slots
    factor = (groups * experts * slots) ** (-0.5)
    pieces, split = (
        max(n for n in range(1, most + 1) if ff % (128 * n) == 0)
        for most in (PIECES, BACK_PIECES)
    )
    vmem = pl.BlockSpec(memory_space=pltpu.VMEM)
    anyw = pl.BlockSpec(memory_space=pl.ANY)
    grad = jax.ShapeDtypeStruct((half, ff), F32)
    parts = PARTS if experts % PARTS == 0 else 1
    scratch = chain_scratch(
        planes, experts, picked, count, width, half, ff, pieces, split, parts
    )
    body = functools.partial(chain_kernel, planes, experts, slots, factor, pieces, parts)
    out, limit, small = vmem, CHAIN_LIMIT, anyw
    if held_bytes(scratch) > CHAIN_LIMIT * 3 // 4:
        scratch = direct_scratch(planes, picked, count, width, half, ff)
        body = functools.partial(direct_kernel, planes, experts, slots, factor)
        out, limit, small = anyw, VMEM_LIMIT, vmem
    came_back, hot, gate_gradient, up_gradient, down_gradient = pl.pallas_call(
        body,
        out_shape=(
            jax.ShapeDtypeStruct((picked, width), BF16),
            jax.ShapeDtypeStruct((picked, count), BF16),
            grad, grad, grad,
        ),
        in_specs=[small] * 3 + [anyw] * 5,
        out_specs=(out, vmem, out, out, out),
        scratch_shapes=scratch,
        compiler_params=pltpu.CompilerParams(
            collective_id=0, has_side_effects=True, vmem_limit_bytes=limit
        ),
        name="routed_layer",
    )(
        *(
            pltpu.with_memory_space_constraint(x, pltpu.MemorySpace.HBM)
            for x in (
                route_index, route_count.reshape(1, experts), route_gate, tokens, target, gate_weight.reshape(half, ff), up_weight.reshape(half, ff),
                down_weight.reshape(half, ff),
            )
        ),
    )
    blocks = max(n for n in range(1, 9) if count % (128 * n) == 0)
    grad = jax.ShapeDtypeStruct((half, 1, ff), F32)
    return tuple(pl.pallas_call(
        finish,
        out_shape=(jax.ShapeDtypeStruct((count, width), BF16), grad, grad, grad),
        in_specs=[vmem] * 5,
        out_specs=[anyw] * 4,
        scratch_shapes=[
            pltpu.VMEM((count, width), BF16),
            pltpu.SemaphoreType.DMA((blocks,)), pltpu.SemaphoreType.DMA((3,)),
        ],
        compiler_params=pltpu.CompilerParams(vmem_limit_bytes=FINISH_LIMIT),
        name="finish",
    )(hot, came_back, gate_gradient, up_gradient, down_gradient))


def solution(mesh):
    return jax.shard_map(
        on_device,
        mesh=mesh,
        in_specs=(
            P(("dp", "expert"), None),
            P(("dp", "expert"), None),
            P("dp", None, "expert", None),
            P("dp", None, "expert"),
            P("dp", None, "expert", None),
            P("dp", "expert", None),
            P("dp", "expert", None),
            P("dp", "expert", None),
        ),
        out_specs=(
            P(("dp", "expert"), None),
            P("dp", "expert", None),
            P("dp", "expert", None),
            P("dp", "expert", None),
        ),
        check_vma=False,
    )
```

```python
import contextlib
import functools
import math

import jax
import jax.numpy as jnp
from jax import lax
from jax.experimental import pallas as pl
from jax.experimental.pallas import tpu as pltpu
from jax.sharding import PartitionSpec as P

F32 = jnp.float32
BF16 = jnp.bfloat16
VMEM_LIMIT = 67000000
CORES = 2
PIECES = 3
BACK_PIECES = 3
PARTS = 2
LAG = 5
LAG_PLANE = 6
LAG_BACK = 7
LAG_GRADS = 0
LATE = False
TURNS = (1, 0)
OUTER_FIRST = False
CHAIN_LIMIT = 44000000
FINISH_LIMIT = 40000000


def dot(a, b, dims, precision=None):
    return lax.dot_general(
        a, b, (dims, ((), ())), preferred_element_type=F32, precision=precision
    )


def scope(name):
    return contextlib.nullcontext()


NN = ((1,), (0,))
NT = ((1,), (1,))
TN = ((0,), (0,))


def direct_kernel(
    planes, experts, slots, factor,
    index, count, gate, tokens, target, gw, uw, dw,
    cb_out, hot_out, gg_out, ug_out, dg_out,
    TOK, TGT, ROWS, TROWS, W, R, EO, RET, SG, G, RG, CB, PS, PR, H, GU, RX, GX, HX, GUX,
    t_loc, g_loc, w_loc, w_send, w_recv, a_loc, a_send, a_recv, p_send, p_recv,
    h_send, h_recv, x_send, x_recv, GRADS, o_loc,
):
    dp = lax.axis_index("dp")
    me_e = lax.axis_index("expert")
    me_z = dp // CORES
    core = dp % CORES
    peers = planes * experts
    per_group = experts * slots
    half = gw.shape[0]
    chunk = CORES * half
    ff = gw.shape[1]
    me = me_z * experts + me_e
    sibling = {"dp": me_z * CORES + (1 - core), "expert": me_e}
    order = sorted(range(1, planes), key=lambda k: -min(k, planes - k))

    def at(z, e):
        return {"dp": z * CORES + core, "expert": e}

    def plane(k):
        return (me_z + k) % planes

    def slot_rows(n):
        return pl.ds(pl.multiple_of(n * slots, slots), slots)

    def cols(z):
        return pl.ds(pl.multiple_of(z * chunk, chunk), chunk)

    def group_rows(z):
        return pl.ds(pl.multiple_of(z * per_group, per_group), per_group)

    barrier = pltpu.get_barrier_semaphore()

    def greet(k, carry):
        p = (me + k) % peers
        pl.semaphore_signal(
            barrier, inc=1, device_id=at(p // experts, p % experts),
            device_id_type=pl.DeviceIdType.MESH,
        )
        return carry

    lax.fori_loop(1, peers, greet, 0)
    pl.semaphore_signal(
        barrier, inc=1, device_id=sibling, device_id_type=pl.DeviceIdType.MESH
    )
    tok_copies = {}
    for k in order + [0]:
        z = plane(k)
        tok_copies[k] = pltpu.make_async_copy(
            tokens.at[:, cols(z)], TOK.at[:, cols(z)], t_loc.at[k]
        )
        tok_copies[k].start()
    locals_w = []
    for i, w in enumerate((gw, uw, dw)):
        c = pltpu.make_async_copy(w, W.at[i, core], w_loc.at[i])
        c.start()
        locals_w.append(c)
    tgt_copy = pltpu.make_async_copy(target, TGT, g_loc)
    tgt_copy.start()

    lane = lax.broadcasted_iota(jnp.int32, (slots, slots), 1)
    own_lane = lane == lax.broadcasted_iota(jnp.int32, (slots, slots), 0)
    slot_id = lax.broadcasted_iota(jnp.int32, (slots, 1), 0)
    names, weights = [], []
    for e in range(experts):
        live = slot_id < jnp.broadcast_to(count[0:1, e : e + 1], (slots, 1))
        ids = jnp.broadcast_to(index[0, e], (slots, slots))
        ids = jnp.sum(jnp.where(own_lane, ids, 0), axis=1, keepdims=True)
        names.append(jnp.where(live, ids, -1))
        g = jnp.broadcast_to(gate[0, e], (slots, slots))
        g = jnp.sum(jnp.where(own_lane, g, 0.0), axis=1, keepdims=True)
        weights.append(jnp.where(live, g, 0.0))
    names = jnp.concatenate(names, axis=0)
    wcol = jnp.concatenate(weights, axis=0)
    hot = (
        names == lax.broadcasted_iota(jnp.int32, (per_group, TOK.shape[0]), 1)
    ).astype(F32).astype(BF16)
    hot_out[...] = hot

    def remote(src, dst, s, r, dev):
        c = pltpu.make_async_remote_copy(
            src_ref=src, dst_ref=dst, send_sem=s, recv_sem=r,
            device_id=dev, device_id_type=pl.DeviceIdType.MESH,
        )
        c.start()
        return c

    def to_plane(i, z, source, land):
        here = z == me_z

        @pl.when(here)
        def _():
            pltpu.make_async_copy(source(me_z, me_e), land, a_loc.at[i]).start()

        first = jnp.where(here, 1, 0)

        def send(j, carry):
            e = (me_e + j) % experts
            remote(source(z, e), land, a_send.at[i], a_recv.at[i, me_z], at(z, e))
            return carry

        lax.fori_loop(first, experts, send, 0)

    def owners(src, dst, i, z):
        to_plane(i, z, lambda z, e: src.at[slot_rows(e), cols(z)], dst.at[slot_rows(me)])

    def sources(src, dst, i, z):
        to_plane(
            i, z, lambda z, e: src.at[slot_rows(z * experts + e)],
            dst.at[slot_rows(me_e), cols(me_z)],
        )

    def take(sem, ref):
        pltpu.make_async_copy(ref, ref, sem).wait()

    def arrived(i, k):
        if k == 0:
            take(a_recv.at[i, me_z], R.at[pl.ds(0, (experts - 1) * slots)])
            take(a_loc.at[i], R.at[pl.ds(0, slots)])
        else:
            take(a_recv.at[i, plane(k)], R.at[pl.ds(0, per_group)])

    outs = []

    def put(i, src, dst):
        c = pltpu.make_async_copy(src, dst, o_loc.at[i])
        c.start()
        outs.append(c)

    def weight(i):
        return W[i].reshape(chunk, ff)

    pl.semaphore_wait(barrier, peers)
    for k in order + [0]:
        z = plane(k)
        tok_copies[k].wait()
        ROWS[:, cols(z)] = dot(hot, TOK[:, cols(z)], NN).astype(BF16)
        owners(ROWS, R, 0, z)
    sent_w = [
        remote(w, W.at[i, core], w_send.at[i], w_recv.at[i], sibling)
        for i, w in enumerate((gw, uw, dw))
    ]

    def send_sum(i, k):
        remote(
            PS.at[i, group_rows(plane(k))], PR.at[i, k - 1],
            p_send.at[i], p_recv.at[i, k - 1], at(plane(k), me_e),
        )

    def pass_on(buf, i, s, way):
        to = me_z + way

        @pl.when(jnp.logical_and(to >= 0, to < planes))
        def _():
            rows_s = buf.at[group_rows(s)]
            remote(
                rows_s, rows_s, h_send.at[i, (way + 1) // 2, s], h_recv.at[i, s],
                at(to, me_e),
            )

    def spread(buf, i):
        for way in (1, -1):
            pass_on(buf, i, me_z, way)

    def along(bufs, first, fn):
        fn(me_z)
        for far in range(1, planes):
            for way in (1, -1):
                s = me_z - way * far

                @pl.when(jnp.logical_and(s >= 0, s < planes))
                def _():
                    for j, buf in enumerate(bufs):
                        take(h_recv.at[first + j, s], buf.at[group_rows(s)])
                        pass_on(buf, first + j, s, way)
                    fn(s)

    def spread_sent(buf, i):
        for s in range(planes):
            rows_s = buf.at[pl.ds(s * per_group, per_group)]

            @pl.when(jnp.logical_and(me_z > 0, me_z <= s))
            def _():
                take(h_send.at[i, 0, s], rows_s)

            @pl.when(jnp.logical_and(me_z < planes - 1, me_z >= s))
            def _():
                take(h_send.at[i, 1, s], rows_s)

    def total(i, own):
        for k in order:
            take(p_recv.at[i, k - 1], PR.at[i, k - 1])
            own = own + PR[i, k - 1].astype(F32)
        return own

    keep = pl.ds(pl.multiple_of(core * half, half), half)
    give = pl.ds(pl.multiple_of((1 - core) * half, half), half)
    mine = group_rows(me_z)

    for i in range(2):
        locals_w[i].wait()
        sent_w[i].wait_recv()
    for k in order:
        z = plane(k)
        arrived(0, k)
        for i in range(2):
            PS[i, group_rows(z), :] = dot(R[group_rows(z), :], weight(i), NN).astype(BF16)
            send_sum(i, k)
    arrived(0, 0)
    gate_own = dot(R[mine, :], weight(0), NN)
    up_own = dot(R[mine, :], weight(1), NN)
    x_rows = remote(R.at[:, give], RX, x_send.at[0], x_recv.at[0], sibling)
    tgt_copy.wait()
    for z in range(planes):
        piece = slice(z * chunk, (z + 1) * chunk)
        TROWS[:, piece] = dot(hot, TGT[:, piece], NN)
    same = dot(hot, hot, NT).astype(BF16)
    gate_pre = total(0, gate_own)
    up_pre = total(1, up_own)
    sigma = jax.nn.sigmoid(gate_pre)
    active = gate_pre * sigma
    H[mine, :] = (active * up_pre).astype(BF16)
    spread(H, 0)
    locals_w[2].wait()
    sent_w[2].wait_recv()

    def expert_out(z):
        EO[group_rows(z), :] = dot(H[group_rows(z), :], weight(2), NT).astype(BF16)
        sources(EO, RET, 1, z)

    along([H], 0, expert_out)
    x_hidden = remote(H, HX, x_send.at[1], x_recv.at[1], sibling)
    for k in order + [0]:
        z = plane(k)
        arrived(1, k)
        part = wcol * RET[:, cols(z)].astype(F32)
        combined = -TROWS[:, cols(z)]
        for _ in range(3):
            top = part.astype(BF16)
            combined = combined + dot(same, top, NN)
            part = part - top.astype(F32)
        SG[:, cols(z)] = (wcol * combined).astype(BF16)
        owners(SG, G, 2, z)

    for k in order:
        z = plane(k)
        arrived(2, k)
        PS[2, group_rows(z), :] = dot(G[group_rows(z), :], weight(2), NN).astype(BF16)
        send_sum(2, k)
    arrived(2, 0)
    own = dot(G[mine, :], weight(2), NN)
    x_grad = remote(G.at[:, give], GX, x_send.at[2], x_recv.at[2], sibling)
    x_hidden.wait_recv()
    x_grad.wait_recv()
    GRADS[2] = (dot(G[:, keep], H[...], TN) + dot(GX[...], HX[...], TN)) * factor
    put(2, GRADS.at[2], dg_out)
    hidden_grad = total(2, own)
    GU[0, mine, :] = (
        hidden_grad * up_pre * sigma * (1.0 + gate_pre * (1.0 - sigma))
    ).astype(BF16)
    spread(GU.at[0], 1)
    GU[1, mine, :] = (hidden_grad * active).astype(BF16)
    spread(GU.at[1], 2)

    def row_grad(z):
        RG[group_rows(z), :] = (
            dot(GU[0, group_rows(z), :], weight(0), NT)
            + dot(GU[1, group_rows(z), :], weight(1), NT)
        ).astype(BF16)
        sources(RG, CB, 3, z)

    along([GU.at[0], GU.at[1]], 1, row_grad)
    x_gate = remote(GU.at[0], GUX.at[0], x_send.at[3], x_recv.at[3], sibling)
    x_up = remote(GU.at[1], GUX.at[1], x_send.at[4], x_recv.at[4], sibling)
    x_rows.wait_recv()
    x_gate.wait_recv()
    GRADS[0] = (dot(R[:, keep], GU[0], TN) + dot(RX[...], GUX[0], TN)) * factor
    put(0, GRADS.at[0], gg_out)
    x_up.wait_recv()
    GRADS[1] = (dot(R[:, keep], GU[1], TN) + dot(RX[...], GUX[1], TN)) * factor
    put(1, GRADS.at[1], ug_out)
    for k in order + [0]:
        arrived(3, k)
    put(3, CB, cb_out)

    for c in sent_w + [x_rows, x_hidden, x_grad, x_gate, x_up]:
        c.wait_send()
    for i in range(4):
        take(a_send.at[i], R.at[pl.ds(0, (peers - 1) * slots)])
    for i in range(3):
        take(p_send.at[i], PR.at[i])
    for i, buf in enumerate((H, GU.at[0], GU.at[1])):
        spread_sent(buf, i)
    for c in outs:
        c.wait()


def chain_kernel(
    planes, experts, slots, factor, pieces, parts,
    index_in, count_in, gate_in, tokens, target, gw, uw, dw,
    cb_out, hot_out, gg_out, ug_out, dg_out,
    index, count, gate, r_loc, TOK, TGT, ROWS, TROWS, META, MT, W, WT, R, TR, G, EOG,
    OWN, IN, OUT, HOWN, HIN, HOUT, H, GU, RG, CB, RX, GX, HX, GUX,
    t_loc, g_loc, w_loc, w_send, w_recv, a_send, a_recv, e_send, e_recv,
    c_send, c_recv, h_send, h_recv, x_send, x_recv,
):
    dp = lax.axis_index("dp")
    me_e = lax.axis_index("expert")
    me_z = dp // CORES
    core = dp % CORES
    peers = planes * experts
    per_group = experts * slots
    half = gw.shape[0]
    chunk = CORES * half
    ff = gw.shape[1]
    fw = ff // pieces
    split = HIN.shape[1] // (planes * parts)
    unit = per_group // parts
    hw = ff // split
    me = me_z * experts + me_e
    sibling = {"dp": me_z * CORES + (1 - core), "expert": me_e}
    ways = (1, -1)
    side = jnp.where(2 * me_z < planes, 1, -1)
    far_first = sorted(range(1, planes), key=lambda k: abs(k - planes / 2)) + [0]
    dist = (me_z, planes - 1 - me_z)
    depth = jnp.maximum(dist[0], dist[1])

    def at(z, e):
        return {"dp": z * CORES + core, "expert": e}

    def plane(k):
        return (me_z + side * k + planes) % planes

    def slot_rows(n):
        return pl.ds(pl.multiple_of(n * slots, slots), slots)

    def cols(z):
        return pl.ds(pl.multiple_of(z * chunk, chunk), chunk)

    def group_rows(z):
        return pl.ds(pl.multiple_of(z * per_group, per_group), per_group)

    def unit_rows(n):
        rows = turn(n // parts) * per_group + n % parts * unit
        return pl.ds(pl.multiple_of(rows, unit), unit)

    def turn(g):
        if planes % 2:
            return g
        g = planes - 1 - g if OUTER_FIRST else g
        return planes // 2 - 1 - g // 2 + (g % 2) * (2 * (g // 2) + 1)

    barrier = pltpu.get_barrier_semaphore()

    def greet(k, carry):
        p = (me + k) % peers
        pl.semaphore_signal(
            barrier, inc=1, device_id=at(p // experts, p % experts),
            device_id_type=pl.DeviceIdType.MESH,
        )
        return carry

    lax.fori_loop(1, peers, greet, 0)
    pl.semaphore_signal(
        barrier, inc=1, device_id=sibling, device_id_type=pl.DeviceIdType.MESH
    )
    routes = [
        pltpu.make_async_copy(src, dst, r_loc.at[i])
        for i, (src, dst) in enumerate(
            ((index_in, index), (count_in, count), (gate_in, gate))
        )
    ]
    for c in routes:
        c.start()
    tok_copies = {}
    for k in far_first:
        tok_copies[k] = pltpu.make_async_copy(
            tokens.at[:, cols(plane(k))], TOK.at[:, cols(plane(k))], t_loc.at[k]
        )
        tok_copies[k].start()
    locals_w = []
    keep = pl.ds(pl.multiple_of(core * half, half), half)
    give = pl.ds(pl.multiple_of((1 - core) * half, half), half)
    for i, w in enumerate((gw, uw, dw)):
        c = pltpu.make_async_copy(w, W.at[i, keep], w_loc.at[i])
        c.start()
        locals_w.append(c)
    tgt_copy = pltpu.make_async_copy(target, TGT, g_loc)
    tgt_copy.start()

    for c in routes:
        c.wait()
    lane = lax.broadcasted_iota(jnp.int32, (slots, slots), 1)
    own_lane = lane == lax.broadcasted_iota(jnp.int32, (slots, slots), 0)
    slot_id = lax.broadcasted_iota(jnp.int32, (slots, 1), 0)
    names, weights = [], []
    for e in range(experts):
        live = slot_id < jnp.broadcast_to(count[0:1, e : e + 1], (slots, 1))
        ids = jnp.broadcast_to(index[0, e], (slots, slots))
        ids = jnp.sum(jnp.where(own_lane, ids, 0), axis=1, keepdims=True)
        names.append(jnp.where(live, ids, -1))
        g = jnp.broadcast_to(gate[0, e], (slots, slots))
        g = jnp.sum(jnp.where(own_lane, g, 0.0), axis=1, keepdims=True)
        weights.append(jnp.where(live, g, 0.0))
    names = jnp.concatenate(names, axis=0)
    wcol = jnp.concatenate(weights, axis=0)
    hot = (
        names == lax.broadcasted_iota(jnp.int32, (per_group, TOK.shape[0]), 1)
    ).astype(F32).astype(BF16)
    hot_out[...] = hot

    def remote(src, dst, s, r, dev):
        c = pltpu.make_async_remote_copy(
            src_ref=src, dst_ref=dst, send_sem=s, recv_sem=r,
            device_id=dev, device_id_type=pl.DeviceIdType.MESH,
        )
        c.start()
        return c

    def take(sem, ref):
        pltpu.make_async_copy(ref, ref, sem).wait()

    def to_plane(i, z, source, land):
        here = z == me_z

        @pl.when(here)
        def _():
            pltpu.make_async_copy(source(me_z, me_e), land, a_recv.at[i, me_z]).start()

        def send(j, carry):
            e = (me_e + j) % experts
            remote(source(z, e), land, a_send.at[i], a_recv.at[i, me_z], at(z, e))
            return carry

        lax.fori_loop(jnp.where(here, 1, 0), experts, send, 0)

    for k in far_first:
        z = plane(k)
        tok_copies[k].wait()
        ROWS[:, cols(z)] = dot(hot, TOK[:, cols(z)], NN).astype(BF16)
    for way, d in zip(ways, range(2)):
        @pl.when(dist[d] == 0)
        def _():
            IN[d] = jnp.zeros(IN.shape[1:], BF16)
            HIN[d] = jnp.zeros(HIN.shape[1:], BF16)

    with scope("barrier"):
        pl.semaphore_wait(barrier, peers)
    sent_w = [
        remote(w, W.at[i, keep], w_send.at[i], w_recv.at[i], sibling)
        for i, w in enumerate((gw, uw, dw))
    ]
    for k in far_first:
        to_plane(
            0, plane(k), lambda z, e: ROWS.at[slot_rows(e), cols(z)], R.at[slot_rows(me)]
        )
    with scope("trows"):
        tgt_copy.wait()
        for k in far_first:
            z = plane(k)
            TROWS[:, cols(z)] = dot(hot, TGT[:, cols(z)], NN).astype(BF16)
    with scope("meta"):
        square = (per_group, per_group)
        eye = lax.broadcasted_iota(jnp.int32, square, 0) == lax.broadcasted_iota(
            jnp.int32, square, 1
        )
        wrow = jnp.sum(jnp.where(eye, wcol, 0.0), axis=0, keepdims=True)
        mix = dot(hot, hot, NT) * wrow
        top = mix.astype(BF16)
        if META.shape[1] > 2 * per_group:
            META[...] = jnp.zeros(META.shape, BF16)
        META[:, 0:per_group] = top
        META[:, per_group : 2 * per_group] = (mix - top.astype(F32)).astype(BF16)

    with scope("w_wait"):
        for i in range(3):
            locals_w[i].wait()
            sent_w[i].wait_recv()
    with scope("wt"):
        for i in range(3):
            WT[i] = W[i].T

    def piece(f):
        return pl.ds(pl.multiple_of(f * fw, fw), fw)

    def partial_sums(c):
        n, f = c // pieces, c % pieces

        @pl.when(c % (pieces * parts) == 0)
        def _():
            with scope("x_wait"):
                take(a_recv.at[0, turn(n // parts)], R.at[pl.ds(0, per_group)])

        with scope("own"):
            rows = R[unit_rows(n), :]
            for i in range(2):
                OWN[c, :, i * fw : (i + 1) * fw] = dot(rows, W[i, :, piece(f)], NN)

    def move(own, inn, out, send, recv, d, c):
        @pl.when(dist[d] > 0)
        def _():
            with scope("mv%d" % (own is HOWN)):
                take(recv.at[d, c], inn.at[d, c])

        @pl.when(dist[d] < planes - 1)
        def _():
            out[d, c] = (own[c] + inn[d, c].astype(F32)).astype(BF16)
            remote(
                out.at[d, c], inn.at[d, c], send.at[d], recv.at[d, c],
                at(me_z + ways[d], me_e),
            )

    def total(own, inn, c):
        return own[c] + inn[0, c].astype(F32) + inn[1, c].astype(F32)

    def to_sibling(i, src, dst):
        remote(src, dst, x_send.at[i], x_recv.at[i], sibling)

    def forward(c):
        n, f = c // pieces, c % pieces
        rows = unit_rows(n)
        with scope("fwd"):
            both = total(OWN, IN, c)
            OWN[c] = both
            pre, up = both[:, :fw], both[:, fw:]
            H[rows, piece(f)] = (pre * jax.nn.sigmoid(pre) * up).astype(BF16)

        @pl.when(f == pieces - 1)
        def _():
            with scope("eo"):
                EOG[me_e, rows, :] = dot(H[rows, :], WT[2], NN).astype(BF16)
                outs = EOG.at[me_e, rows]

                def send(j, carry):
                    remote(
                        outs, outs, e_send, e_recv.at[n], at(me_z, (me_e + j) % experts)
                    )
                    return carry

                lax.fori_loop(1, experts, send, 0)
                to_sibling(1, H.at[rows], HX.at[rows])

    spread = (slots, 2 * per_group)
    own_slot = (
        lax.broadcasted_iota(jnp.int32, spread, 1) % per_group
        == lax.broadcasted_iota(jnp.int32, spread, 0) + me_e * slots
    )

    def slot_grads(n):
        z = turn(n // parts)
        rows = unit_rows(n)
        with scope("eo_wait"):
            take(e_recv.at[n], EOG.at[pl.ds(0, experts - 1), pl.ds(0, unit)])

            @pl.when(n % parts == 0)
            def _():
                take(a_recv.at[1, z], TR.at[pl.ds(0, per_group)])
                take(a_recv.at[2, z], MT.at[pl.ds(0, per_group)])
        with scope("comb"):
            for s in range(experts // parts):
                mine = slot_rows(z * experts + n % parts * (experts // parts) + s)
                outs = [EOG[e, mine, :] for e in range(experts)]
                table = MT[mine, 0 : 2 * per_group]
                wide = dot(table, jnp.concatenate(outs + outs, axis=0), NN)
                w = jnp.sum(
                    jnp.where(own_slot, table.astype(F32), 0.0), axis=1, keepdims=True
                )
                G[mine, :] = (w * (wide - TR[mine, :].astype(F32))).astype(BF16)
            for i in range(split):
                HOWN[n * split + i] = dot(G[rows, :], W[2, :, i * hw : (i + 1) * hw], NN)
            to_sibling(2, G.at[rows, give], GX.at[rows])

    def backward(n):
        rows = unit_rows(n)
        with scope("bwd"):
            hidden_grad = jnp.concatenate(
                [total(HOWN, HIN, n * split + i) for i in range(split)], axis=1
            )
            for f in range(pieces):
                both = OWN[n * pieces + f]
                pre, up = both[:, :fw], both[:, fw:]
                grad = hidden_grad[:, f * fw : (f + 1) * fw]
                sigma = jax.nn.sigmoid(pre)
                GU[0, rows, f * fw : (f + 1) * fw] = (
                    grad * up * sigma * (1.0 + pre * (1.0 - sigma))
                ).astype(BF16)
                GU[1, rows, f * fw : (f + 1) * fw] = (grad * (pre * sigma)).astype(BF16)
            RG[rows, :] = (
                dot(GU[0, rows, :], WT[0], NN) + dot(GU[1, rows, :], WT[1], NN)
            ).astype(BF16)
            send_rows(n)
            for i in range(2):
                to_sibling(3 + i, GU.at[i, rows], GUX.at[i, rows])

    def send_rows(n):
        z, share = turn(n // parts), experts // parts
        land = CB.at[slot_rows(me_e), cols(me_z)]

        def send(j, carry):
            e = n % parts * share + j
            rows = RG.at[slot_rows(z * experts + e)]
            here = jnp.logical_and(z == me_z, e == me_e)

            @pl.when(here)
            def _():
                pltpu.make_async_copy(rows, land, a_recv.at[3, me_z]).start()

            @pl.when(jnp.logical_not(here))
            def _():
                remote(rows, land, a_send.at[3], a_recv.at[3, me_z], at(z, e))

            return carry

        lax.fori_loop(0, share, send, 0)

    steps = planes * parts * pieces
    back_steps = planes * parts * split
    begin = pieces - 1 + LAG * (planes - 1) + LAG_PLANE
    begin += max(0, pieces - split) * (planes * parts - 1)

    def each(t, fn, last):
        @pl.when(jnp.logical_and(t >= 0, t < last))
        def _():
            fn(t)

    def each_group(t, fn):
        fits = jnp.logical_and(t >= 0, t < back_steps)

        @pl.when(jnp.logical_and(fits, t % split == 0))
        def _():
            fn(t // split)

    def grad(i, left, left_x, right, right_x, out):
        out[...] = (dot(left, right, TN) + dot(left_x, right_x, TN)) * factor

    def send_targets(z):
        to_plane(2, z, lambda z, e: META.at[slot_rows(e)], MT.at[slot_rows(me)])
        to_plane(
            1, z, lambda z, e: TROWS.at[slot_rows(e), cols(z)], TR.at[slot_rows(me)]
        )

    for k in far_first:
        send_targets(plane(k))

    def tick(t, carry):
        each(t, partial_sums, steps)
        for d in TURNS:
            each(
                t - LAG * dist[d],
                functools.partial(move, OWN, IN, OUT, c_send, c_recv, d), steps,
            )
        each(t - LAG * depth, forward, steps)
        t = t - begin
        each_group(t, slot_grads)
        for d in TURNS:
            each(
                t - LAG_BACK * dist[d],
                functools.partial(move, HOWN, HIN, HOUT, h_send, h_recv, d), back_steps,
            )
        back = t - LAG_BACK * (planes - 1 if LATE else depth) - (split - 1) - LAG_GRADS
        each_group(back, backward)
        return carry

    middle = begin + back_steps + 1
    lax.fori_loop(0, middle, tick, 0)
    to_sibling(0, R.at[:, give], RX)
    with scope("dgrad"):
        take(x_recv.at[1], HX)
        take(x_recv.at[2], GX)
        grad(2, G[:, keep], GX[...], H[...], HX[...], dg_out)
    lax.fori_loop(
        middle, begin + back_steps + LAG_BACK * (planes - 1) + LAG_GRADS + split, tick, 0
    )
    with scope("xg"):
        take(x_recv.at[0], RX)
        take(x_recv.at[3], GUX.at[0])
        take(x_recv.at[4], GUX.at[1])
    with scope("gugrad"):
        grad(0, R[:, keep], RX[...], GU[0], GUX[0], gg_out)
        grad(1, R[:, keep], RX[...], GU[1], GUX[1], ug_out)
    with scope("cb_wait"):
        for k in far_first:
            take(a_recv.at[3, plane(k)], R.at[pl.ds(0, per_group)])
    with scope("tail"):
        cb_out[...] = CB[...]
        for c in sent_w:
            c.wait_send()
        others = pl.ds(0, (peers - 1) * slots)
        for i, buf in enumerate((R, TR, MT, RG)):
            take(a_send.at[i], buf.at[others])
        take(e_send, EOG.at[pl.ds(0, experts - 1)])
        for d in range(2):
            @pl.when(dist[d] < planes - 1)
            def _():
                take(c_send.at[d], OUT.at[d])
                take(h_send.at[d], HOUT.at[d])
        for i, buf in enumerate((RX, HX, GX, GUX.at[0], GUX.at[1])):
            take(x_send.at[i], buf)


def finish(hot, cb, gg, ug, dg, tg_out, gg_out, ug_out, dg_out, TG, t_sem, g_sem):
    copies = []
    for i, (grad, out) in enumerate(((gg, gg_out), (ug, ug_out), (dg, dg_out))):
        copies.append(pltpu.make_async_copy(grad, out.at[:, 0, :], g_sem.at[i]))
        copies[-1].start()
    parts = t_sem.shape[0]
    step = TG.shape[0] // parts
    for j in range(parts):
        rows = slice(j * step, (j + 1) * step)
        TG[rows, :] = dot(hot[:, rows], cb[...], TN).astype(BF16)
        copies.append(pltpu.make_async_copy(TG.at[rows], tg_out.at[rows], t_sem.at[j]))
        copies[-1].start()
    for c in copies:
        c.wait()


def direct_scratch(planes, picked, count, width, half, ff):
    chunk = CORES * half
    all_rows = planes * picked
    dma = pltpu.SemaphoreType.DMA
    return [
        pltpu.VMEM((count, width), BF16),
        pltpu.VMEM((count, width), BF16),
        pltpu.VMEM((picked, width), BF16),
        pltpu.VMEM((picked, width), F32),
        pltpu.VMEM((3, CORES, half, ff), BF16),
        pltpu.VMEM((all_rows, chunk), BF16),
        pltpu.VMEM((all_rows, chunk), BF16),
        pltpu.VMEM((picked, width), BF16),
        pltpu.VMEM((picked, width), BF16),
        pltpu.VMEM((all_rows, chunk), BF16),
        pltpu.VMEM((all_rows, chunk), BF16),
        pltpu.VMEM((picked, width), BF16),
        pltpu.VMEM((3, all_rows, ff), BF16),
        pltpu.VMEM((3, planes - 1, picked, ff), BF16),
        pltpu.VMEM((all_rows, ff), BF16),
        pltpu.VMEM((2, all_rows, ff), BF16),
        pltpu.VMEM((all_rows, half), BF16),
        pltpu.VMEM((all_rows, half), BF16),
        pltpu.VMEM((all_rows, ff), BF16),
        pltpu.VMEM((2, all_rows, ff), BF16),
        dma((planes,)), dma,
        dma((3,)), dma((3,)), dma((3,)),
        dma((4,)), dma((4,)), dma((4, planes)),
        dma((3,)), dma((3, planes)),
        dma((3, 2, planes)), dma((3, planes)),
        dma((5,)), dma((5,)),
        pltpu.VMEM((3, half, ff), F32), dma((4,)),
    ]


def chain_scratch(planes, experts, picked, count, width, half, ff, pieces, split, parts):
    slots = picked // experts
    chunk = CORES * half
    all_rows = planes * picked
    steps = planes * parts * pieces
    back_steps = planes * parts * split
    unit = picked // parts
    fw = ff // pieces
    table = -(-2 * picked // 128) * 128
    dma = pltpu.SemaphoreType.DMA
    return [
        pltpu.VMEM((1, experts, 1, slots), jnp.int32),
        pltpu.VMEM((1, experts), jnp.int32),
        pltpu.VMEM((1, experts, 1, slots), F32),
        dma((3,)),
        pltpu.VMEM((count, width), BF16),
        pltpu.VMEM((count, width), BF16),
        pltpu.VMEM((picked, width), BF16),
        pltpu.VMEM((picked, width), BF16),
        pltpu.VMEM((picked, table), BF16),
        pltpu.VMEM((all_rows, table), BF16),
        pltpu.VMEM((3, chunk, ff), BF16),
        pltpu.VMEM((3, ff, chunk), BF16),
        pltpu.VMEM((all_rows, chunk), BF16),
        pltpu.VMEM((all_rows, chunk), BF16),
        pltpu.VMEM((all_rows, chunk), BF16),
        pltpu.VMEM((experts, all_rows, chunk), BF16),
        pltpu.VMEM((steps, unit, 2 * fw), F32),
        pltpu.VMEM((2, steps, unit, 2 * fw), BF16),
        pltpu.VMEM((2, steps, unit, 2 * fw), BF16),
        pltpu.VMEM((back_steps, unit, ff // split), F32),
        pltpu.VMEM((2, back_steps, unit, ff // split), BF16),
        pltpu.VMEM((2, back_steps, unit, ff // split), BF16),
        pltpu.VMEM((all_rows, ff), BF16),
        pltpu.VMEM((2, all_rows, ff), BF16),
        pltpu.VMEM((all_rows, chunk), BF16),
        pltpu.VMEM((picked, width), BF16),
        pltpu.VMEM((all_rows, half), BF16),
        pltpu.VMEM((all_rows, half), BF16),
        pltpu.VMEM((all_rows, ff), BF16),
        pltpu.VMEM((2, all_rows, ff), BF16),
        dma((planes,)), dma, dma((3,)), dma((3,)), dma((3,)),
        dma((4,)), dma((4, planes)), dma, dma((planes * parts,)),
        dma((2,)), dma((2, steps)), dma((2,)), dma((2, back_steps)),
        dma((5,)), dma((5,)),
    ]


def held_bytes(scratch):
    return sum(
        math.prod(s.shape) * jnp.dtype(s.dtype).itemsize
        for s in scratch
        if getattr(s, "memory_space", None) == pltpu.VMEM
    )


def on_device(
    tokens, target, route_index, route_count, route_gate, gate_weight, up_weight, down_weight
):
    groups = lax.axis_size("dp")
    experts = lax.axis_size("expert")
    planes = groups // CORES
    slots = route_index.shape[3]
    count, width = tokens.shape
    half, _, ff = gate_weight.shape
    picked = experts * slots
    factor = (groups * experts * slots) ** (-0.5)
    pieces, split = (
        max(n for n in range(1, most + 1) if ff % (128 * n) == 0)
        for most in (PIECES, BACK_PIECES)
    )
    vmem = pl.BlockSpec(memory_space=pltpu.VMEM)
    anyw = pl.BlockSpec(memory_space=pl.ANY)
    grad = jax.ShapeDtypeStruct((half, ff), F32)
    parts = PARTS if experts % PARTS == 0 else 1
    scratch = chain_scratch(
        planes, experts, picked, count, width, half, ff, pieces, split, parts
    )
    body = functools.partial(chain_kernel, planes, experts, slots, factor, pieces, parts)
    out, limit, small = vmem, CHAIN_LIMIT, anyw
    if held_bytes(scratch) > CHAIN_LIMIT * 3 // 4:
        scratch = direct_scratch(planes, picked, count, width, half, ff)
        body = functools.partial(direct_kernel, planes, experts, slots, factor)
        out, limit, small = anyw, VMEM_LIMIT, vmem
    came_back, hot, gate_gradient, up_gradient, down_gradient = pl.pallas_call(
        body,
        out_shape=(
            jax.ShapeDtypeStruct((picked, width), BF16),
            jax.ShapeDtypeStruct((picked, count), BF16),
            grad, grad, grad,
        ),
        in_specs=[small] * 3 + [anyw] * 5,
        out_specs=(out, vmem, out, out, out),
        scratch_shapes=scratch,
        compiler_params=pltpu.CompilerParams(
            collective_id=0, has_side_effects=True, vmem_limit_bytes=limit
        ),
        name="routed_layer",
    )(
        *(
            pltpu.with_memory_space_constraint(x, pltpu.MemorySpace.HBM)
            for x in (
                route_index, route_count.reshape(1, experts), route_gate, tokens, target, gate_weight.reshape(half, ff), up_weight.reshape(half, ff),
                down_weight.reshape(half, ff),
            )
        ),
    )
    blocks = max(n for n in range(1, 9) if count % (128 * n) == 0)
    grad = jax.ShapeDtypeStruct((half, 1, ff), F32)
    return tuple(pl.pallas_call(
        finish,
        out_shape=(jax.ShapeDtypeStruct((count, width), BF16), grad, grad, grad),
        in_specs=[vmem] * 5,
        out_specs=[anyw] * 4,
        scratch_shapes=[
            pltpu.VMEM((count, width), BF16),
            pltpu.SemaphoreType.DMA((blocks,)), pltpu.SemaphoreType.DMA((3,)),
        ],
        compiler_params=pltpu.CompilerParams(vmem_limit_bytes=FINISH_LIMIT),
        name="finish",
    )(hot, came_back, gate_gradient, up_gradient, down_gradient))


def solution(mesh):
    return jax.shard_map(
        on_device,
        mesh=mesh,
        in_specs=(
            P(("dp", "expert"), None),
            P(("dp", "expert"), None),
            P("dp", None, "expert", None),
            P("dp", None, "expert"),
            P("dp", None, "expert", None),
            P("dp", "expert", None),
            P("dp", "expert", None),
            P("dp", "expert", None),
        ),
        out_specs=(
            P(("dp", "expert"), None),
            P("dp", "expert", None),
            P("dp", "expert", None),
            P("dp", "expert", None),
        ),
        check_vma=False,
    )
```
